512 devices in a mesh: rows: 16 (over x, y_lo, core), dp: 32 (over z, y_hi).
Axes of the slice: x: 4, y: 8 (y_hi: 4, y_lo: 2; y = y_hi * 2 + y_lo), z: 8, core: 2. Of those that a mesh axis runs over, the one named last changes fastest.
Arguments:
- images: bfloat16 [32, 32, 512, 128], P('dp', 'rows'), may hold values from -54 to 54
- conv_weight: bfloat16 [3, 3, 128, 128], replicated, may hold values from -0.1875 to 0.1875
- conv_bias: float32 [128], replicated, may hold values from -3 to 3
- norm_gain: float32 [128], replicated, may hold values from 0.5 to 1.5
- norm_shift: float32 [128], replicated, may hold values from -3 to 3
- down_weight: bfloat16 [3, 3, 128, 256], replicated, may hold values from -0.1875 to 0.1875
- down_bias: float32 [256], replicated, may hold values from -3 to 3
- cotangent: bfloat16 [32, 16, 256, 256], P('dp', 'rows'), may hold values from -6 to 6
Outputs:
- block_out: bfloat16 [32, 16, 256, 256], P('dp', 'rows')
- grad_images: bfloat16 [32, 32, 512, 128], P('dp', 'rows')
- grad_conv_weight: float32 [3, 3, 128, 128], P(None, None, None, 'dp')
- grad_conv_bias: float32 [128], P('dp')
- grad_gain: float32 [128], P('dp')
- grad_shift: float32 [128], P('dp')
- grad_down_weight: float32 [3, 3, 128, 256], P(None, None, None, 'dp')
- grad_down_bias: float32 [256], P('dp')
The draws below stay inside these ranges and needn't reach their ends.
All inputs are finite; a program needn't handle non-finite values.
Results may differ from the reference program's by a relative error of at most 0.0048.
Values may be sent and summed in bfloat16 or wider, within the bound.
A program may use at most 64 MiB of HBM per device.

```python
import math
import jax
import jax.numpy as jnp
from jax import lax

CH0 = 128
CH1 = 256
GROUPS = 32
COLS = 512
HEIGHT = 32
SAMPLES = 32


def draw_images(key, part):
    first, second, third = jax.random.split(jax.random.fold_in(key, 11), 3)
    position = jnp.arange(HEIGHT, dtype=jnp.float32) / max(HEIGHT - 1, 1)
    row_scale = jnp.power(3.0, position) * jnp.exp(jax.random.uniform(second, (HEIGHT,), jnp.float32, 0.0, math.log(2.0)))
    col_scale = jnp.exp(jax.random.uniform(third, (COLS,), jnp.float32, 0.0, math.log(5.0)))
    base = jnp.clip(jax.random.normal(first, (SAMPLES, HEIGHT, COLS, CH0), jnp.float32), -4.0, 4.0)
    values = 0.3 * base * row_scale[None, :, None, None] * col_scale[None, None, :, None]
    return values.astype(jnp.bfloat16)


def spiked(drawn, stream_key, source, target, shards_of, factor):
    owner, partner = [(jnp.arange(drawn.shape[dim]) // (drawn.shape[dim] // shards_of)).reshape([-1 if axis == dim else 1 for axis in range(drawn.ndim)]) for dim in (source, target)]
    chosen = jax.random.permutation(stream_key, shards_of)[partner]
    strong = (owner == chosen) | (owner == (partner + shards_of // 2) % shards_of)
    return jnp.where(strong, factor * drawn, drawn)


def steps_of(own_key, dims, shards, least, top_value):
    level, own = 1.0, jax.random.fold_in(own_key, 6)
    for dim, parts in shards:
        heights = jnp.exp(jax.random.uniform(jax.random.fold_in(own, dim), (parts,), jnp.float32, least / len(shards), top_value / len(shards)))
        level = level * jnp.repeat(heights, dims[dim] // parts).reshape([-1 if axis == dim else 1 for axis in range(len(dims))])
    return level


def bell_draw(stream_key, extent, scale, reach, shards=(), held_as=jnp.bfloat16):
    factor_of = steps_of(stream_key, extent, shards, -0.22, 0.18) if shards else 1.0
    result = jax.random.normal(stream_key, extent, jnp.float32) * scale * factor_of
    return jnp.minimum(jnp.maximum(result, -reach), reach).astype(held_as)


def noise_with(key, extent, scale, limit, cuts, heavy, held_as=jnp.bfloat16):
    array = scale * jax.random.normal(key, extent, jnp.float32)
    if cuts:
        array = array * steps_of(key, extent, cuts, -0.22, 0.18)
    return jnp.clip(spiked(array, jax.random.fold_in(key, 3), *heavy), -limit, limit).astype(held_as)


def setup_inputs(seed: int = 0) -> dict:
    keys = jax.random.split(jax.random.key(seed), 9)
    return {
        "images": draw_images(jax.random.fold_in(keys[8], 71), 0),
        "conv_weight": bell_draw(keys[1], (3, 3, CH0, CH0), (9 * CH0) ** -0.5, 0.1875),
        "conv_bias": bell_draw(keys[2], (CH0,), 0.5, 3.0, (), jnp.float32),
        "norm_gain": jnp.clip(1.0 + 0.1 * jax.random.normal(keys[3], (CH0,), jnp.float32), 0.5, 1.5),
        "norm_shift": bell_draw(keys[4], (CH0,), 0.5, 3.0, (), jnp.float32),
        "down_weight": bell_draw(keys[5], (3, 3, CH0, CH1), (9 * CH0) ** -0.5, 0.1875),
        "down_bias": bell_draw(keys[6], (CH1,), 0.5, 3.0, (), jnp.float32),
        "cotangent": noise_with(keys[7], (SAMPLES, HEIGHT // 2, COLS // 2, CH1), 1.0, 6.0, ((0, 32), (1, 16)), (0, 3, 32, 2.75)),
    }


def taps_conv(padded, weight, rows, cols):
    total = jnp.zeros((rows * cols, weight.shape[3]), jnp.float32)
    for kh in range(3):
        for kw in range(3):
            piece = padded[kh:kh + rows, kw:kw + cols].reshape(rows * cols, -1)
            total = total + jnp.dot(piece, weight[kh, kw], preferred_element_type=jnp.float32)
    return total.reshape(rows, cols, weight.shape[3])

def one_sample(image, cot, conv_weight, conv_bias, norm_gain, norm_shift, down_weight, down_bias):
    half_rows = HEIGHT // 2
    half_cols = COLS // 2
    width = CH0 // GROUPS
    count = float(HEIGHT * COLS * width)
    padded = jnp.pad(image, ((1, 1), (1, 1), (0, 0)))
    hidden = taps_conv(padded, conv_weight, HEIGHT, COLS) + conv_bias
    grouped = hidden.reshape(HEIGHT, COLS, GROUPS, width)
    mean = lax.optimization_barrier(jnp.sum(grouped, axis=(0, 1, 3))) / count
    centred = grouped - mean[:, None]
    var = lax.optimization_barrier(jnp.sum(centred * centred, axis=(0, 1, 3))) / count
    rstd = lax.rsqrt(var + 1e-05)
    normed = (centred * rstd[:, None]).reshape(HEIGHT, COLS, CH0)
    pre = normed * norm_gain + norm_shift
    sig = jax.nn.sigmoid(pre)
    mixed = (image.astype(jnp.float32) + pre * sig).astype(jnp.bfloat16)
    shifted = jnp.pad(mixed, ((1, 0), (1, 0), (0, 0)))
    cot_flat = cot.reshape(half_rows * half_cols, CH1)
    out = jnp.zeros((half_rows * half_cols, CH1), jnp.float32)
    grad_down = []
    grad_mixed_pad = jnp.zeros((HEIGHT + 1, COLS + 1, CH0), jnp.float32)
    for kh in range(3):
        line = []
        for kw in range(3):
            piece = shifted[kh:kh + 2 * half_rows:2, kw:kw + 2 * half_cols:2].reshape(half_rows * half_cols, CH0)
            out = out + jnp.dot(piece, down_weight[kh, kw], preferred_element_type=jnp.float32)
            line.append(jnp.dot(piece.T, cot_flat, preferred_element_type=jnp.float32))
            back = jnp.dot(cot_flat, down_weight[kh, kw].T, preferred_element_type=jnp.float32)
            grad_mixed_pad = grad_mixed_pad.at[kh:kh + 2 * half_rows:2, kw:kw + 2 * half_cols:2].add(back.reshape(half_rows, half_cols, CH0))
        grad_down.append(jnp.stack(line))
    block = (out + down_bias).astype(jnp.bfloat16).reshape(half_rows, half_cols, CH1)
    grad_down = jnp.stack(grad_down)
    grad_down_bias = lax.optimization_barrier(jnp.sum(cot.astype(jnp.float32), axis=(0, 1)))
    grad_mixed = grad_mixed_pad[1:, 1:]
    grad_pre = grad_mixed * sig * (1.0 + pre * (1.0 - sig))
    grad_gain = lax.optimization_barrier(jnp.sum(grad_pre * normed, axis=(0, 1)))
    grad_shift = lax.optimization_barrier(jnp.sum(grad_pre, axis=(0, 1)))
    scaled = (grad_pre * norm_gain).reshape(HEIGHT, COLS, GROUPS, width)
    normed_g = normed.reshape(HEIGHT, COLS, GROUPS, width)
    first = lax.optimization_barrier(jnp.sum(scaled, axis=(0, 1, 3))) / count
    second = lax.optimization_barrier(jnp.sum(scaled * normed_g, axis=(0, 1, 3))) / count
    grad_hidden = (rstd[:, None] * (scaled - first[:, None] - normed_g * second[:, None])).reshape(HEIGHT, COLS, CH0)
    grad_bias = lax.optimization_barrier(jnp.sum(grad_hidden, axis=(0, 1)))
    rounded = grad_hidden.astype(jnp.bfloat16)
    flat = rounded.reshape(HEIGHT * COLS, CH0)
    grad_conv = []
    for kh in range(3):
        line = []
        for kw in range(3):
            piece = padded[kh:kh + HEIGHT, kw:kw + COLS].reshape(HEIGHT * COLS, CH0)
            line.append(jnp.dot(piece.T, flat, preferred_element_type=jnp.float32))
        grad_conv.append(jnp.stack(line))
    grad_conv = jnp.stack(grad_conv)
    grad_pad = jnp.pad(rounded, ((1, 1), (1, 1), (0, 0)))
    back = jnp.zeros((HEIGHT * COLS, CH0), jnp.float32)
    for kh in range(3):
        for kw in range(3):
            piece = grad_pad[2 - kh:2 - kh + HEIGHT, 2 - kw:2 - kw + COLS].reshape(HEIGHT * COLS, CH0)
            back = back + jnp.dot(piece, conv_weight[kh, kw].T, preferred_element_type=jnp.float32)
    grad_image = (grad_mixed + back.reshape(HEIGHT, COLS, CH0)).astype(jnp.bfloat16)
    return (block, grad_image, (grad_conv, grad_bias, grad_gain, grad_shift, grad_down, grad_down_bias))

def reference(images, conv_weight, conv_bias, norm_gain, norm_shift, down_weight, down_bias, cotangent):
    start = (jnp.zeros((3, 3, CH0, CH0), jnp.float32), jnp.zeros((CH0,), jnp.float32), jnp.zeros((CH0,), jnp.float32), jnp.zeros((CH0,), jnp.float32), jnp.zeros((3, 3, CH0, CH1), jnp.float32), jnp.zeros((CH1,), jnp.float32))

    def step(carry, pair):
        block, grad_image, grads = one_sample(pair[0], pair[1], conv_weight, conv_bias, norm_gain, norm_shift, down_weight, down_bias)
        carry = tuple((c + g for c, g in zip(carry, grads)))
        return (carry, (block, grad_image))
    sums, (blocks, grad_images) = lax.scan(step, start, (images, cotangent))
    return (blocks, grad_images, sums[0], sums[1], sums[2], sums[3], sums[4], sums[5])
```

```python
import jax
import jax.numpy as jnp
from jax import lax
from jax.experimental import pallas as pl
from jax.experimental.pallas import tpu as pltpu
from jax.sharding import PartitionSpec as P

GROUPS = 32
CHANS = 128
OUTS = 256
BF = jnp.bfloat16
F32 = jnp.float32
MESH = pl.DeviceIdType.MESH
EPS = 1e-05
DOWN_CHUNKS = 9
PAIRS = 7


def nn(a, b):
    return lax.dot_general(a, b, (((1,), (0,)), ((), ())), preferred_element_type=F32)


def nt(a, b):
    return lax.dot_general(a, b, (((1,), (1,)), ((), ())), preferred_element_type=F32)


def tn(a, b):
    return lax.dot_general(a, b, (((0,), (0,)), ((), ())), preferred_element_type=F32)


def group_sum(x):
    lane = lax.broadcasted_iota(jnp.int32, x.shape, 1)
    x = x + jnp.where(lane % 2 == 0, pltpu.roll(x, CHANS - 1, 1), pltpu.roll(x, 1, 1))
    return x + jnp.where(lane % 4 < 2, pltpu.roll(x, CHANS - 2, 1), pltpu.roll(x, 2, 1))


def twice(x):
    return jnp.concatenate([x, x], axis=1)


def fold(x):
    return x[:, :CHANS] + x[:, CHANS:]


def kernel(
    rows_n,
    dp_n,
    img,
    cw,
    cb,
    gain_ref,
    shift_ref,
    dw,
    db,
    cot,
    block_out,
    gimg_out,
    gout,
    wide,
    tall,
    edge_img,
    edge_cot,
    x4,
    m4,
    g4,
    wf,
    wb,
    hid,
    gpre,
    gmix,
    stat_a,
    stat_b,
    mine,
    full,
    cs,
    cr,
    rs,
    rr,
    red,
    dr,
    img_s,
    img_r,
    cot_s,
    cot_r,
    mix_s,
    mix_r,
    g_s,
    g_r,
    sa_s,
    sa_r,
    sb_s,
    sb_r,
    c_s,
    c_r,
    r_s,
    r_r,
    d_s,
    d_r,
    o_s,
    o_r,
):
    r = lax.axis_index("rows")
    d = lax.axis_index("dp")
    core = lax.rem(r, 2)
    slot = lax.div(r, 2)
    mate = r + 1 - 2 * core
    half = cot.shape[1]
    cols = 2 * half
    n_local = float(2 * cols * (CHANS // GROUPS))
    n_total = n_local * rows_n
    last = rows_n - 1
    slots = rows_n // 2

    def remote(src, dst, send, recv, **where):
        return pltpu.make_async_remote_copy(
            src_ref=src,
            dst_ref=dst,
            send_sem=send,
            recv_sem=recv,
            device_id=where,
            device_id_type=MESH,
        )

    barrier = pltpu.get_barrier_semaphore()

    def greet_row(i, c):
        pl.semaphore_signal(
            barrier, inc=1, device_id={"rows": lax.rem(r + i, rows_n)}, device_id_type=MESH
        )
        return c

    def greet_dp(i, c):
        pl.semaphore_signal(
            barrier, inc=1, device_id={"dp": lax.rem(d + i, dp_n)}, device_id_type=MESH
        )
        return c

    lax.fori_loop(1, rows_n, greet_row, 0)
    lax.fori_loop(1, dp_n, greet_dp, 0)

    zero_block = jnp.zeros((CHANS, CHANS), BF)
    for kh in range(3):
        for kw in range(3):
            tap = cw[kh, kw]
            wf[kh, kw * CHANS : (kw + 1) * CHANS, :CHANS] = tap
            wf[kh, (kw + 1) * CHANS : (kw + 2) * CHANS, CHANS:] = tap
            wb[kh, :CHANS, (2 - kw) * CHANS : (3 - kw) * CHANS] = tap
            wb[kh, CHANS:, (3 - kw) * CHANS : (4 - kw) * CHANS] = tap
        wf[kh, 3 * CHANS :, :CHANS] = zero_block
        wf[kh, :CHANS, CHANS:] = zero_block
        wb[kh, :CHANS, 3 * CHANS :] = zero_block
        wb[kh, CHANS:, :CHANS] = zero_block

    tall[:8, :] = jnp.zeros((8, CHANS), F32)
    tall[cols + 8 :, :] = jnp.zeros((8, CHANS), F32)
    wide[:8, :] = jnp.zeros((8, OUTS), F32)
    wide[half + 8 :, :] = jnp.zeros((8, OUTS), F32)

    def split_columns(row, f):
        tall[8 : cols + 8, :] = row.astype(F32)
        for k, start in enumerate((7, 8, 9, 10)):
            x4[f, :, k * CHANS : (k + 1) * CHANS] = tall[pl.ds(start, half, stride=2), :].astype(BF)

    def shifted(x, by):
        width = x.shape[1]
        wide[8 : half + 8, :width] = x
        return wide[8 + by : half + 8 + by, :width]

    @pl.when(r == 0)
    def _():
        edge_img[0] = jnp.zeros(edge_img.shape[1:], BF)
        m4[0] = jnp.zeros(m4.shape[1:], BF)
        g4[0] = jnp.zeros(g4.shape[1:], BF)

    @pl.when(r == last)
    def _():
        edge_img[1] = jnp.zeros(edge_img.shape[1:], BF)
        edge_cot[...] = jnp.zeros(edge_cot.shape, BF)
        g4[3] = jnp.zeros(g4.shape[1:], BF)

    pl.semaphore_wait(barrier, rows_n + dp_n - 2)
    up = lax.max(r - 1, 0)
    down = lax.min(r + 1, last)
    img_down = remote(img.at[0, 1], edge_img.at[0], img_s.at[0], img_r.at[0], rows=down)
    img_up = remote(img.at[0, 0], edge_img.at[1], img_s.at[1], img_r.at[1], rows=up)
    cot_up = remote(cot.at[0], edge_cot, cot_s, cot_r, rows=up)
    mix_down = remote(m4.at[2], m4.at[0], mix_s, mix_r, rows=down)
    mid = pl.ds(CHANS, 2 * CHANS)
    g_down = remote(g4.at[2, :, mid], g4.at[0, :, mid], g_s.at[0], g_r.at[0], rows=down)
    g_up = remote(g4.at[1, :, mid], g4.at[3, :, mid], g_s.at[1], g_r.at[1], rows=up)

    @pl.when(r < last)
    def _():
        img_down.start()

    @pl.when(r > 0)
    def _():
        img_up.start()
        cot_up.start()

    for a in range(2):
        split_columns(img[0, a], a + 1)

    bias = twice(cb[...])
    hid[0] = nn(x4[1], wf[1]) + nn(x4[2], wf[2]) + bias
    hid[1] = nn(x4[1], wf[0]) + nn(x4[2], wf[1]) + bias

    @pl.when(r > 0)
    def _():
        img_down.wait_recv()

    split_columns(edge_img[0], 0)
    hid[0] += nn(x4[0], wf[0])

    @pl.when(r < last)
    def _():
        img_up.wait_recv()

    split_columns(edge_img[1], 3)
    hid[1] += nn(x4[3], wf[2])

    def spread(table, send, recv):
        def go(i, c):
            to = lax.rem(r + i, rows_n)
            remote(table.at[r], table.at[r], send.at[to], recv.at[r], rows=to).start()
            return c

        lax.fori_loop(1, rows_n, go, 0)

    def gathered(table, send, recv):
        def go(i, c):
            other = lax.rem(r + i, rows_n)
            remote(table.at[other], table.at[other], send.at[other], recv.at[other], rows=other).wait()
            return c

        lax.fori_loop(1, rows_n, go, 0)

    def colsum(x):
        return jnp.sum(x, axis=0, keepdims=True)

    own_sum = fold(colsum(hid[0]) + colsum(hid[1]))
    own_mean = twice(group_sum(jnp.broadcast_to(own_sum, (8, CHANS)))[:1] / n_local)
    off0 = hid[0] - own_mean
    off1 = hid[1] - own_mean
    own_sq = fold(colsum(off0 * off0) + colsum(off1 * off1))
    stat_a[r, 0:1, :] = own_sum
    stat_a[r, 1:2, :] = own_sq
    stat_a[r, 2:8, :] = jnp.zeros((6, CHANS), F32)
    spread(stat_a, sa_s, sa_r)

    @pl.when(r < last)
    def _():
        cot_up.wait_recv()

    def pull(grad, lead, kh):
        both = dw[kh, 1:3].reshape(2 * CHANS, OUTS)
        return nt(grad, both), nt(lead, dw[kh, 0])

    own_cot = cot[0]
    own_cot32 = own_cot.astype(F32)
    cot_sum = colsum(own_cot32)
    lead_cot = shifted(own_cot32, 1).astype(BF)
    whole, odd = pull(own_cot, lead_cot, 1)
    gmix[0] = whole
    gmix[0, :, CHANS:] += odd
    whole, odd = pull(own_cot, lead_cot, 2)
    gmix[1] = whole
    gmix[1, :, CHANS:] += odd
    below = edge_cot[...]
    whole, odd = pull(below, shifted(below.astype(F32), 1).astype(BF), 0)
    gmix[1] += whole
    gmix[1, :, CHANS:] += odd

    gathered(stat_a, sa_s, sa_r)
    table = stat_a[...]
    groups = group_sum(table.reshape(rows_n * 8, CHANS)).reshape(rows_n, 8, CHANS)
    group_tot = jnp.sum(groups, axis=0)
    mean = group_tot[0:1] / n_total
    dev = groups / n_local - mean.reshape(1, 1, CHANS)
    spread_sq = jnp.sum(dev * dev, axis=0)[0:1] * n_local
    rstd = lax.rsqrt((group_tot[1:2] + spread_sq) / n_total + EPS)
    channel_sum = jnp.sum(table, axis=0)[0:1]
    mean2, rstd2 = twice(mean), twice(rstd)
    gain2, shift2 = twice(gain_ref[...]), twice(shift_ref[...])

    sum_gp = jnp.zeros((1, 2 * CHANS), F32)
    sum_gpn = jnp.zeros((1, 2 * CHANS), F32)
    for a in (1, 0):
        normed = (hid[a] - mean2) * rstd2
        pre = normed * gain2 + shift2
        sig = jax.nn.sigmoid(pre)
        mixed = (x4[a + 1, :, CHANS : 3 * CHANS].astype(F32) + pre * sig).astype(BF)
        m4[a + 1, :, CHANS:] = mixed
        m4[a + 1, :, :CHANS] = shifted(mixed[:, CHANS:].astype(F32), -1).astype(BF)
        if a == 1:

            @pl.when(r < last)
            def _():
                mix_down.start()

        gp = gmix[a] * sig * (1.0 + pre * (1.0 - sig))
        hid[a] = normed
        gpre[a] = gp
        sum_gp += colsum(gp)
        sum_gpn += colsum(gp * normed)

    stat_b[r, 0:1, :] = fold(sum_gp)
    stat_b[r, 1:2, :] = fold(sum_gpn)
    stat_b[r, 2:3, :] = cot_sum[:, :CHANS]
    stat_b[r, 3:4, :] = cot_sum[:, CHANS:]
    stat_b[r, 4:8, :] = jnp.zeros((4, CHANS), F32)
    spread(stat_b, sb_s, sb_r)

    def down_grad(kh):
        part = tn(own_cot, m4[kh])
        for kw in range(3):
            c = 3 * kh + kw
            full[c % 2, c // 2] = part[:, kw * CHANS : (kw + 1) * CHANS]

    def taps(kh):
        return dw[kh].reshape(3 * CHANS, OUTS)

    out = nn(m4[1], taps(1)) + nn(m4[2], taps(2)) + db[...]
    down_grad(1)
    down_grad(2)

    @pl.when(r > 0)
    def _():
        mix_down.wait_recv()

    down_grad(0)
    cs[0:4] = full[1 - core, 0:4].astype(BF)
    pair_one = remote(cs.at[0:4], cr.at[0:4], c_s.at[0], c_r.at[0], rows=mate)
    pair_two = remote(cs.at[4:PAIRS], cr.at[4:PAIRS], c_s.at[1], c_r.at[1], rows=mate)
    pair_one.start()
    block_out[0, 0] = (out + nn(m4[0], taps(0))).astype(BF)

    gathered(stat_b, sb_s, sb_r)
    totals = jnp.sum(stat_b[...], axis=0)
    tot_gp = totals[0:1]
    tot_gpn = totals[1:2]
    means = group_sum(
        jnp.broadcast_to(gain_ref[...], (8, CHANS)) * totals
    ) / n_total
    m1, m2 = means[0:1], means[1:2]
    m1w, m2w = twice(m1), twice(m2)
    for a in range(2):
        grad = (rstd2 * (gpre[a] * gain2 - m1w - hid[a] * m2w)).astype(BF)
        g4[a + 1, :, CHANS : 3 * CHANS] = grad

    @pl.when(r < last)
    def _():
        g_down.start()

    @pl.when(r > 0)
    def _():
        g_up.start()

    n_channel = float(2 * cols * rows_n)
    tot_normed = (channel_sum - n_channel * mean) * rstd
    tot_bias = rstd * (gain_ref[...] * tot_gp - n_channel * m1 - m2 * tot_normed)
    mine[0:1, :] = tot_bias
    mine[1:2, :] = tot_gpn
    mine[2:3, :] = tot_gp
    mine[3:4, :] = totals[2:3]
    mine[4:5, :] = totals[3:4]
    mine[5:8, :] = jnp.zeros((3, CHANS), F32)

    def row_send(low, high):
        for i in range(1, slots):
            to = lax.rem(slot + i, slots)

            @pl.when((to >= low) & (to < high))
            def _():
                remote(
                    rs.at[lax.min(to, PAIRS - 1)],
                    rr.at[slot],
                    r_s.at[to],
                    r_r.at[slot],
                    rows=2 * to + core,
                ).start()

    def pair_sum(low, high):
        for k in range(low, high):
            both = full[core, k] + cr[k].astype(F32)
            full[core, k] = both
            rs[k] = both.astype(BF)
        row_send(low, high)

    pair_one.wait()
    pair_sum(0, 4)

    sub = lax.broadcasted_iota(jnp.int32, (CHANS, CHANS), 0) % 8
    conv_taps = []
    for kh in range(3):
        part = tn(g4[1, :, CHANS : 3 * CHANS], x4[kh]) + tn(
            g4[2, :, CHANS : 3 * CHANS], x4[kh + 1]
        )
        for kw in range(3):
            conv_taps.append(
                part[:CHANS, kw * CHANS : (kw + 1) * CHANS]
                + part[CHANS:, (kw + 1) * CHANS : (kw + 2) * CHANS]
            )
    conv_taps.append(jnp.zeros((CHANS, CHANS), F32))
    for k in range(5):
        c = DOWN_CHUNKS + k
        one, two = conv_taps[2 * k], conv_taps[2 * k + 1]
        full[c % 2, c // 2, :CHANS] = jnp.where(sub < 4, one, pltpu.roll(two, 4, 0))
        full[c % 2, c // 2, CHANS:] = jnp.where(sub < 4, pltpu.roll(one, CHANS - 4, 0), two)
    cs[4:PAIRS] = full[1 - core, 4:PAIRS].astype(BF)
    pair_two.start()

    def sides(f):
        grad = g4[f, :, CHANS : 3 * CHANS].astype(F32)
        g4[f, :, :CHANS] = shifted(grad[:, CHANS:], -1).astype(BF)
        g4[f, :, 3 * CHANS :] = shifted(grad[:, :CHANS], 1).astype(BF)

    sides(1)
    sides(2)
    gmix[0] += nt(g4[1], wb[1]) + nt(g4[2], wb[0])
    gmix[1] += nt(g4[1], wb[2]) + nt(g4[2], wb[1])

    pair_two.wait()
    pair_sum(4, PAIRS)

    def put_row(a):
        tall[pl.ds(8, half, stride=2), :] = gmix[a, :, :CHANS]
        tall[pl.ds(9, half, stride=2), :] = gmix[a, :, CHANS:]
        gimg_out[0, a] = tall[8 : cols + 8, :].astype(BF)

    @pl.when(r > 0)
    def _():
        g_down.wait_recv()
        sides(0)

    gmix[0] += nt(g4[0], wb[2])
    put_row(0)

    @pl.when(r < last)
    def _():
        g_up.wait_recv()
        sides(3)

    gmix[1] += nt(g4[3], wb[0])
    put_row(1)

    @pl.when(slot < PAIRS)
    def _():
        def take(i, total):
            other = lax.rem(slot + i, slots)
            remote(
                rs.at[0], rr.at[other], r_s.at[other], r_r.at[other], rows=2 * other + core
            ).wait_recv()
            return total + rr[other].astype(F32)

        red[...] = lax.fori_loop(1, slots, take, full[core, lax.min(slot, PAIRS - 1)])

    @pl.when(slot == PAIRS)
    def _():
        red[...] = jnp.broadcast_to(mine[...][None], (32, 8, CHANS)).reshape(256, CHANS)

    def place(e):
        row = jnp.where(r < DOWN_CHUNKS, e, lax.rem(e, 2) * 16 + lax.div(e, 2))
        return pl.ds(pl.multiple_of(row * 8, 8), 8)

    def to_owner(i, c):
        to = lax.rem(d + i, dp_n)
        remote(red.at[place(to)], dr.at[d], d_s.at[to], d_r.at[d], dp=to).start()
        return c

    lax.fori_loop(1, dp_n, to_owner, 0)
    dr[d] = red[place(d), :]

    def from_peer(i, c):
        other = lax.rem(d + i, dp_n)
        remote(red.at[place(other)], dr.at[other], d_s.at[other], d_r.at[other], dp=other).wait()
        return c

    lax.fori_loop(1, dp_n, from_peer, 0)
    gout[r] = jnp.sum(dr[...], axis=0)
    spread(gout, o_s, o_r)
    gathered(gout, o_s, o_r)

    @pl.when(r < last)
    def _():
        img_down.wait_send()
        mix_down.wait_send()
        g_down.wait_send()

    @pl.when(r > 0)
    def _():
        img_up.wait_send()
        cot_up.wait_send()
        g_up.wait_send()

    for i in range(1, slots):
        to = lax.rem(slot + i, slots)

        @pl.when(to < PAIRS)
        def _():
            remote(rs.at[0], rr.at[slot], r_s.at[to], r_r.at[slot], rows=2 * to + core).wait_send()


def shards(
    images, conv_weight, conv_bias, norm_gain, norm_shift, down_weight, down_bias, cotangent
):
    rows_n = lax.axis_size("rows")
    dp_n = lax.axis_size("dp")
    _, local_rows, cols, chans = images.shape
    half = cols // 2
    vmem = pl.BlockSpec(memory_space=pltpu.VMEM)
    dma = pltpu.SemaphoreType.DMA
    scratch = [
        pltpu.VMEM((half + 16, OUTS), F32),
        pltpu.VMEM((cols + 16, CHANS), F32),
        pltpu.VMEM((2, cols, CHANS), BF),
        pltpu.VMEM((half, OUTS), BF),
        pltpu.VMEM((4, half, 4 * CHANS), BF),
        pltpu.VMEM((3, half, 3 * CHANS), BF),
        pltpu.VMEM((4, half, 4 * CHANS), BF),
        pltpu.VMEM((3, 4 * CHANS, 2 * CHANS), BF),
        pltpu.VMEM((3, 2 * CHANS, 4 * CHANS), BF),
        pltpu.VMEM((2, half, 2 * CHANS), F32),
        pltpu.VMEM((2, half, 2 * CHANS), F32),
        pltpu.VMEM((2, half, 2 * CHANS), F32),
        pltpu.VMEM((rows_n, 8, CHANS), F32),
        pltpu.VMEM((rows_n, 8, CHANS), F32),
        pltpu.VMEM((8, CHANS), F32),
        pltpu.VMEM((2, PAIRS, OUTS, CHANS), F32),
        pltpu.VMEM((PAIRS, OUTS, CHANS), BF),
        pltpu.VMEM((PAIRS, OUTS, CHANS), BF),
        pltpu.VMEM((PAIRS, OUTS, CHANS), BF),
        pltpu.VMEM((rows_n // 2, OUTS, CHANS), BF),
        pltpu.VMEM((OUTS, CHANS), F32),
        pltpu.VMEM((dp_n, 8, CHANS), F32),
        dma((2,)),
        dma((2,)),
        dma,
        dma,
        dma,
        dma,
        dma((2,)),
        dma((2,)),
        dma((rows_n,)),
        dma((rows_n,)),
        dma((rows_n,)),
        dma((rows_n,)),
        dma((2,)),
        dma((2,)),
        dma((rows_n // 2,)),
        dma((rows_n // 2,)),
        dma((dp_n,)),
        dma((dp_n,)),
        dma((rows_n,)),
        dma((rows_n,)),
    ]

    def body(*refs):
        kernel(rows_n, dp_n, *refs)

    block, grad_image, table = pl.pallas_call(
        body,
        out_shape=(
            jax.ShapeDtypeStruct((1, 1, half, OUTS), BF),
            jax.ShapeDtypeStruct((1, local_rows, cols, chans), BF),
            jax.ShapeDtypeStruct((rows_n, 8, CHANS), F32),
        ),
        in_specs=[vmem] * 8,
        out_specs=(vmem, vmem, vmem),
        scratch_shapes=scratch,
        compiler_params=pltpu.CompilerParams(
            collective_id=0, has_side_effects=True, vmem_limit_bytes=40 * 1024 * 1024
        ),
        name="step",
    )(
        images,
        conv_weight,
        conv_bias.reshape(1, CHANS),
        norm_gain.reshape(1, CHANS),
        norm_shift.reshape(1, CHANS),
        down_weight,
        down_bias.reshape(1, OUTS),
        cotangent.reshape(1, half, OUTS),
    )
    d = lax.axis_index("dp")
    down_part = jnp.swapaxes(table[:DOWN_CHUNKS], 1, 2).reshape(3, 3, CHANS, 8)
    conv_part = jnp.swapaxes(
        table[DOWN_CHUNKS:14].reshape(10, 4, CHANS)[:9], 1, 2
    ).reshape(3, 3, CHANS, 4)
    vectors = table[14]
    narrow = lax.dynamic_slice(vectors, (0, 4 * d), (3, 4))
    wide = lax.dynamic_slice(vectors[3:5].reshape(OUTS), (8 * d,), (8,))
    return block, grad_image, conv_part, narrow[0], narrow[1], narrow[2], down_part, wide


def solution(mesh):
    spread = P("dp", "rows", None, None)
    in_specs = (spread, P(), P(), P(), P(), P(), P(), spread)
    out_specs = (
        spread,
        spread,
        P(None, None, None, "dp"),
        P("dp"),
        P("dp"),
        P("dp"),
        P(None, None, None, "dp"),
        P("dp"),
    )
    return jax.shard_map(shards, mesh=mesh, in_specs=in_specs, out_specs=out_specs, check_vma=False)
```

```python
import jax
import jax.numpy as jnp
from jax import lax
from jax.experimental import pallas as pl
from jax.experimental.pallas import tpu as pltpu
from jax.sharding import PartitionSpec as P

GROUPS = 32
CHANS = 128
OUTS = 256
BF = jnp.bfloat16
F32 = jnp.float32
MESH = pl.DeviceIdType.MESH
EPS = 1e-05
TAPS = 9
LATE = 6


def nn(a, b):
    return lax.dot_general(a, b, (((1,), (0,)), ((), ())), preferred_element_type=F32)


def nt(a, b):
    return lax.dot_general(a, b, (((1,), (1,)), ((), ())), preferred_element_type=F32)


def tn(a, b):
    return lax.dot_general(a, b, (((0,), (0,)), ((), ())), preferred_element_type=F32)


def group_sum(x):
    lane = lax.broadcasted_iota(jnp.int32, x.shape, 1)
    x = x + jnp.where(lane % 2 == 0, pltpu.roll(x, CHANS - 1, 1), pltpu.roll(x, 1, 1))
    return x + jnp.where(lane % 4 < 2, pltpu.roll(x, CHANS - 2, 1), pltpu.roll(x, 2, 1))


def twice(x):
    return jnp.concatenate([x, x], axis=1)


def fold(x):
    return x[:, :CHANS] + x[:, CHANS:]


def kernel(
    rows_n,
    dp_n,
    img_hbm,
    cw_hbm,
    cb_hbm,
    gain_hbm,
    shift_hbm,
    dw_hbm,
    db_hbm,
    cot_hbm,
    block_out,
    gimg_out,
    gout,
    img,
    cw,
    cb,
    gain_ref,
    shift_ref,
    dw,
    db,
    cot,
    block_v,
    gimg_v,
    wide,
    tall,
    edge_img,
    edge_cot,
    x4,
    m4,
    g4,
    wf,
    wb,
    hid,
    gpre,
    gmix,
    stat_a,
    stat_b,
    mine,
    early,
    late,
    cs,
    cr,
    cs2,
    cr2,
    rs,
    rr,
    rs2,
    rr2,
    red1,
    red2,
    red,
    dr,
    load_sem,
    store_sem,
    img_s,
    img_r,
    cot_s,
    cot_r,
    mix_s,
    mix_r,
    g_s,
    g_r,
    sa_s,
    sa_r,
    sb_s,
    sb_r,
    c_s,
    c_r,
    r_s,
    r_r,
    q_s,
    q_r,
    d_s,
    d_r,
    o_s,
    o_r,
):
    r = lax.axis_index("rows")
    d = lax.axis_index("dp")
    core = lax.rem(r, 2)
    slot = lax.div(r, 2)
    mate = r + 1 - 2 * core
    half = cot.shape[0]
    cols = 2 * half
    n_local = float(2 * cols * (CHANS // GROUPS))
    n_total = n_local * rows_n
    last = rows_n - 1
    slots = rows_n // 2

    def remote(src, dst, send, recv, **where):
        return pltpu.make_async_remote_copy(
            src_ref=src,
            dst_ref=dst,
            send_sem=send,
            recv_sem=recv,
            device_id=where,
            device_id_type=MESH,
        )

    loads = [
        pltpu.make_async_copy(src, dst, load_sem.at[k])
        for k, (src, dst) in enumerate(
            (
                (img_hbm.at[0], img),
                (cw_hbm, cw),
                (cot_hbm.at[0], cot),
                (dw_hbm, dw),
                (cb_hbm, cb),
                (gain_hbm, gain_ref),
                (shift_hbm, shift_ref),
                (db_hbm, db),
            )
        )
    ]
    for load in loads:
        load.start()

    x_at, y_at = lax.div(r, 4), lax.rem(slot, 2)
    hops = sorted(
        ((min(dx, 4 - dx) + dy, dc, dx, dy) for dx in range(4) for dy in range(2) for dc in range(2)),
        reverse=True,
    )
    row_peers = [
        lax.rem(x_at + dx, 4) * 4
        + (y_at if dy == 0 else 1 - y_at) * 2
        + (core if dc == 0 else 1 - core)
        for _, dc, dx, dy in hops[:-1]
    ]
    if dp_n == 32:
        z_at, h_at = lax.div(d, 4), lax.rem(d, 4)
        hops = sorted(
            ((min(dz, 8 - dz) + 2 * min(dh, 4 - dh), dz, dh) for dz in range(8) for dh in range(4)),
            reverse=True,
        )
        dp_peers = [
            lax.rem(z_at + dz, 8) * 4 + lax.rem(h_at + dh, 4) for _, dz, dh in hops[:-1]
        ]
    else:
        dp_peers = [lax.rem(d + i, dp_n) for i in range(1, dp_n)]

    barrier = pltpu.get_barrier_semaphore()
    for to in dp_peers:
        pl.semaphore_signal(barrier, inc=1, device_id={"dp": to}, device_id_type=MESH)
    for to in row_peers:
        pl.semaphore_signal(barrier, inc=1, device_id={"rows": to}, device_id_type=MESH)

    pl.semaphore_wait(barrier, rows_n + dp_n - 2)
    up = lax.max(r - 1, 0)
    down = lax.min(r + 1, last)
    mid = pl.ds(CHANS, 2 * CHANS)
    img_down = remote(img_hbm.at[0, 1], edge_img.at[0], img_s.at[0], img_r.at[0], rows=down)
    img_up = remote(img_hbm.at[0, 0], edge_img.at[1], img_s.at[1], img_r.at[1], rows=up)
    cot_up = remote(cot_hbm.at[0], edge_cot, cot_s, cot_r, rows=up)
    mix_down = remote(m4.at[2, :, mid], m4.at[0, :, mid], mix_s, mix_r, rows=down)
    g_down = remote(g4.at[2, :, mid], g4.at[0, :, mid], g_s.at[0], g_r.at[0], rows=down)
    g_up = remote(g4.at[1, :, mid], g4.at[3, :, mid], g_s.at[1], g_r.at[1], rows=up)

    @pl.when(r < last)
    def _():
        img_down.start()

    @pl.when(r > 0)
    def _():
        img_up.start()

    loads[1].wait()
    zero_block = jnp.zeros((CHANS, CHANS), BF)
    for kh in range(3):
        for kw in range(3):
            tap = cw[kh, kw]
            wf[kh, kw * CHANS : (kw + 1) * CHANS, :CHANS] = tap
            wf[kh, (kw + 1) * CHANS : (kw + 2) * CHANS, CHANS:] = tap
            wb[kh, :CHANS, (2 - kw) * CHANS : (3 - kw) * CHANS] = tap
            wb[kh, CHANS:, (3 - kw) * CHANS : (4 - kw) * CHANS] = tap
        wf[kh, 3 * CHANS :, :CHANS] = zero_block
        wf[kh, :CHANS, CHANS:] = zero_block
        wb[kh, :CHANS, 3 * CHANS :] = zero_block
        wb[kh, CHANS:, :CHANS] = zero_block

    tall[:8, :] = jnp.zeros((8, CHANS), F32)
    tall[cols + 8 :, :] = jnp.zeros((8, CHANS), F32)
    wide[:8, :] = jnp.zeros((8, OUTS), F32)
    wide[half + 8 :, :] = jnp.zeros((8, OUTS), F32)

    def split_columns(row, f):
        tall[8 : cols + 8, :] = row.astype(F32)
        for k, start in enumerate((7, 8, 9, 10)):
            x4[f, :, k * CHANS : (k + 1) * CHANS] = tall[pl.ds(start, half, stride=2), :].astype(BF)

    def shifted(x, by):
        width = x.shape[1]
        wide[8 : half + 8, :width] = x
        return wide[8 + by : half + 8 + by, :width]

    @pl.when(r == 0)
    def _():
        edge_img[0] = jnp.zeros(edge_img.shape[1:], BF)
        m4[0] = jnp.zeros(m4.shape[1:], BF)
        g4[0] = jnp.zeros(g4.shape[1:], BF)

    @pl.when(r == last)
    def _():
        edge_img[1] = jnp.zeros(edge_img.shape[1:], BF)
        edge_cot[...] = jnp.zeros(edge_cot.shape, BF)
        g4[3] = jnp.zeros(g4.shape[1:], BF)

    for k in (0, 2, 3, 4, 5, 6, 7):
        loads[k].wait()
    for a in range(2):
        split_columns(img[a], a + 1)

    bias = twice(cb[...])
    hid[0] = nn(x4[1], wf[1]) + nn(x4[2], wf[2]) + bias
    hid[1] = nn(x4[1], wf[0]) + nn(x4[2], wf[1]) + bias

    @pl.when(r > 0)
    def _():
        img_down.wait_recv()

    split_columns(edge_img[0], 0)
    hid[0] += nn(x4[0], wf[0])

    @pl.when(r < last)
    def _():
        img_up.wait_recv()

    @pl.when(r > 0)
    def _():
        cot_up.start()

    split_columns(edge_img[1], 3)
    hid[1] += nn(x4[3], wf[2])

    def spread(table, send, recv):
        for to in row_peers:
            remote(table.at[r], table.at[r], send.at[to], recv.at[r], rows=to).start()

    def gathered(table, send, recv):
        for other in row_peers:
            remote(table.at[other], table.at[other], send.at[other], recv.at[other], rows=other).wait()

    def colsum(x):
        return jnp.sum(x, axis=0, keepdims=True)

    own_sum = fold(colsum(hid[0]) + colsum(hid[1]))
    own_mean = twice(group_sum(jnp.broadcast_to(own_sum, (8, CHANS)))[:1] / n_local)
    off0 = hid[0] - own_mean
    off1 = hid[1] - own_mean
    own_sq = fold(colsum(off0 * off0) + colsum(off1 * off1))
    stat_a[r, 0:1, :] = own_sum
    stat_a[r, 1:2, :] = own_sq
    stat_a[r, 2:8, :] = jnp.zeros((6, CHANS), F32)
    spread(stat_a, sa_s, sa_r)

    @pl.when(r < last)
    def _():
        cot_up.wait_recv()

    def pull(grad, lead, kh):
        both = dw[kh, 1:3].reshape(2 * CHANS, OUTS)
        return nt(grad, both), nt(lead, dw[kh, 0])

    own_cot = cot[...]
    own_cot32 = own_cot.astype(F32)
    cot_sum = colsum(own_cot32)
    lead_cot = shifted(own_cot32, 1).astype(BF)
    whole, odd = pull(own_cot, lead_cot, 1)
    gmix[0] = whole
    gmix[0, :, CHANS:] += odd
    whole, odd = pull(own_cot, lead_cot, 2)
    gmix[1] = whole
    gmix[1, :, CHANS:] += odd
    below = edge_cot[...]
    whole, odd = pull(below, shifted(below.astype(F32), 1).astype(BF), 0)
    gmix[1] += whole
    gmix[1, :, CHANS:] += odd

    gathered(stat_a, sa_s, sa_r)
    table = stat_a[...]
    groups = group_sum(table.reshape(rows_n * 8, CHANS)).reshape(rows_n, 8, CHANS)
    group_tot = jnp.sum(groups, axis=0)
    mean = group_tot[0:1] / n_total
    dev = groups / n_local - mean.reshape(1, 1, CHANS)
    spread_sq = jnp.sum(dev * dev, axis=0)[0:1] * n_local
    rstd = lax.rsqrt((group_tot[1:2] + spread_sq) / n_total + EPS)
    channel_sum = jnp.sum(table, axis=0)[0:1]
    mean2, rstd2 = twice(mean), twice(rstd)
    gain2, shift2 = twice(gain_ref[...]), twice(shift_ref[...])

    sum_gp = jnp.zeros((1, 2 * CHANS), F32)
    sum_gpn = jnp.zeros((1, 2 * CHANS), F32)
    for a in (1, 0):
        normed = (hid[a] - mean2) * rstd2
        pre = normed * gain2 + shift2
        sig = jax.nn.sigmoid(pre)
        mixed = (x4[a + 1, :, CHANS : 3 * CHANS].astype(F32) + pre * sig).astype(BF)
        m4[a + 1, :, CHANS:] = mixed
        m4[a + 1, :, :CHANS] = shifted(mixed[:, CHANS:].astype(F32), -1).astype(BF)
        gp = gmix[a] * sig * (1.0 + pre * (1.0 - sig))
        hid[a] = normed
        gpre[a] = gp
        sum_gp += colsum(gp)
        sum_gpn += colsum(gp * normed)

    stat_b[r, 0:1, :] = fold(sum_gp)
    stat_b[r, 1:2, :] = fold(sum_gpn)
    stat_b[r, 2:3, :] = cot_sum[:, :CHANS]
    stat_b[r, 3:4, :] = cot_sum[:, CHANS:]
    stat_b[r, 4:8, :] = jnp.zeros((4, CHANS), F32)
    spread(stat_b, sb_s, sb_r)

    @pl.when(r < last)
    def _():
        mix_down.start()

    sub = lax.broadcasted_iota(jnp.int32, (CHANS, CHANS), 0) % 8

    def down_grad(kh):
        part = tn(own_cot, m4[kh])
        for kw in range(3):
            tap = 3 * kh + kw
            tiles = part[:, kw * CHANS : (kw + 1) * CHANS].reshape(16, 2, 8, CHANS)
            one = tiles[:, 0].reshape(CHANS, CHANS)
            two = tiles[:, 1].reshape(CHANS, CHANS)
            low = jnp.where(sub < 4, one, pltpu.roll(two, 4, 0))
            high = jnp.where(sub < 4, pltpu.roll(one, CHANS - 4, 0), two)
            if tap < 8:
                early[0, tap] = low
                early[1, tap] = high
            else:
                late[1, 4] = low
                late[0, 5] = high

    def taps(kh):
        return dw[kh].reshape(3 * CHANS, OUTS)

    out = nn(m4[1], taps(1)) + nn(m4[2], taps(2)) + db[...]
    down_grad(1)
    down_grad(2)

    @pl.when(r > 0)
    def _():
        mix_down.wait_recv()
        m4[0, :, :CHANS] = shifted(m4[0, :, 2 * CHANS :].astype(F32), -1).astype(BF)

    down_grad(0)
    cs[...] = early[1 - core].astype(BF)
    pair_one = remote(cs, cr, c_s.at[0], c_r.at[0], rows=mate)
    pair_two = remote(cs2, cr2, c_s.at[1], c_r.at[1], rows=mate)
    pair_one.start()
    block_v[...] = (out + nn(m4[0], taps(0))).astype(BF)
    block_store = pltpu.make_async_copy(block_v, block_out.at[0, 0], store_sem.at[0])
    block_store.start()

    gathered(stat_b, sb_s, sb_r)
    totals = jnp.sum(stat_b[...], axis=0)
    tot_gp = totals[0:1]
    tot_gpn = totals[1:2]
    means = group_sum(
        jnp.broadcast_to(gain_ref[...], (8, CHANS)) * totals
    ) / n_total
    m1, m2 = means[0:1], means[1:2]
    m1w, m2w = twice(m1), twice(m2)
    for a in range(2):
        grad = (rstd2 * (gpre[a] * gain2 - m1w - hid[a] * m2w)).astype(BF)
        g4[a + 1, :, CHANS : 3 * CHANS] = grad

    n_channel = float(2 * cols * rows_n)
    tot_normed = (channel_sum - n_channel * mean) * rstd
    tot_bias = rstd * (gain_ref[...] * tot_gp - n_channel * m1 - m2 * tot_normed)
    mine[...] = jnp.zeros(mine.shape, F32)
    for k in (0, 4):
        mine[0, k : k + 1, :] = tot_bias
        mine[0, k + 1 : k + 2, :] = tot_gpn
        mine[0, k + 2 : k + 3, :] = tot_gp
        mine[1, k : k + 1, :] = totals[2:3]
        mine[1, k + 1 : k + 2, :] = totals[3:4]

    slot_peers = [
        lax.rem(x_at + dx, 4) * 2 + (y_at if dy == 0 else 1 - y_at)
        for dx, dy in ((2, 1), (2, 0), (1, 1), (3, 1), (1, 0), (3, 0), (0, 1))
    ]

    def early_send(to):
        return remote(rs.at[to], rr.at[slot], r_s.at[to], r_r.at[slot], rows=2 * to + core)

    def late_send(to):
        return remote(
            rs2.at[lax.min(to, LATE - 1)], rr2.at[slot], q_s.at[to], q_r.at[slot], rows=2 * to + core
        )

    pair_one.wait()
    both = early[core] + cr[...].astype(F32)
    early[core] = both
    rs[...] = both.astype(BF)
    for to in slot_peers:
        early_send(to).start()

    for kh in range(3):
        part = tn(g4[1, :, CHANS : 3 * CHANS], x4[kh]) + tn(
            g4[2, :, CHANS : 3 * CHANS], x4[kh + 1]
        )
        for kw in range(3):
            tap = 3 * kh + kw
            late[tap % 2, tap // 2] = (
                part[:CHANS, kw * CHANS : (kw + 1) * CHANS]
                + part[CHANS:, (kw + 1) * CHANS : (kw + 2) * CHANS]
            )
    late[1, 5] = jnp.zeros((CHANS, CHANS), F32)
    cs2[...] = late[1 - core].astype(BF)
    pair_two.start()

    def sides(f):
        grad = g4[f, :, CHANS : 3 * CHANS].astype(F32)
        g4[f, :, :CHANS] = shifted(grad[:, CHANS:], -1).astype(BF)
        g4[f, :, 3 * CHANS :] = shifted(grad[:, :CHANS], 1).astype(BF)

    pair_two.wait()
    both = late[core] + cr2[...].astype(F32)
    late[core] = both
    rs2[...] = both.astype(BF)
    for to in slot_peers:

        @pl.when(to < LATE)
        def _():
            late_send(to).start()

    @pl.when(r < last)
    def _():
        g_down.start()

    @pl.when(r > 0)
    def _():
        g_up.start()

    sides(1)
    sides(2)
    gmix[0] += nt(g4[1], wb[1]) + nt(g4[2], wb[0])
    gmix[1] += nt(g4[1], wb[2]) + nt(g4[2], wb[1])

    total = early[core, slot]
    for other in slot_peers:
        remote(rs.at[0], rr.at[other], r_s.at[other], r_r.at[other], rows=2 * other + core).wait_recv()
        total = total + rr[other].astype(F32)
    red1[...] = total

    @pl.when(slot < LATE)
    def _():
        for other in slot_peers:
            remote(rs2.at[0], rr2.at[other], q_s.at[other], q_r.at[other], rows=2 * other + core).wait_recv()
        total = late[core, lax.min(slot, LATE - 1)]
        for other in slot_peers:
            total = total + rr2[other].astype(F32)
        red2[...] = total

    @pl.when(slot >= LATE)
    def _():
        red2[...] = jnp.broadcast_to(mine[core][None], (16, 8, CHANS)).reshape(CHANS, CHANS)

    one, two = red1[...], red2[...]
    red[:CHANS] = jnp.where(sub < 4, one, pltpu.roll(two, 4, 0))
    red[CHANS:] = jnp.where(sub < 4, pltpu.roll(one, CHANS - 4, 0), two)

    def place(e):
        row = lax.rem(e, 2) * 16 + lax.div(e, 2)
        return pl.ds(pl.multiple_of(row * 8, 8), 8)

    for to in dp_peers:
        remote(red.at[place(to)], dr.at[d], d_s.at[to], d_r.at[d], dp=to).start()
    dr[d] = red[place(d), :]

    def put_row(a):
        tall[pl.ds(8, half, stride=2), :] = gmix[a, :, :CHANS]
        tall[pl.ds(9, half, stride=2), :] = gmix[a, :, CHANS:]
        gimg_v[a] = tall[8 : cols + 8, :].astype(BF)

    @pl.when(r > 0)
    def _():
        g_down.wait_recv()
        sides(0)

    gmix[0] += nt(g4[0], wb[2])
    put_row(0)

    @pl.when(r < last)
    def _():
        g_up.wait_recv()
        sides(3)

    gmix[1] += nt(g4[3], wb[0])
    put_row(1)
    gimg_store = pltpu.make_async_copy(gimg_v, gimg_out.at[0], store_sem.at[1])
    gimg_store.start()

    for other in dp_peers:
        remote(red.at[place(other)], dr.at[other], d_s.at[other], d_r.at[other], dp=other).wait()
    gout[r] = jnp.sum(dr[...], axis=0)
    spread(gout, o_s, o_r)
    gathered(gout, o_s, o_r)

    @pl.when(r < last)
    def _():
        img_down.wait_send()
        mix_down.wait_send()
        g_down.wait_send()

    @pl.when(r > 0)
    def _():
        img_up.wait_send()
        cot_up.wait_send()
        g_up.wait_send()

    for to in slot_peers:
        early_send(to).wait_send()

        @pl.when(to < LATE)
        def _():
            late_send(to).wait_send()

    block_store.wait()
    gimg_store.wait()


def finish(
    block, gimg, table, block_out, gimg_out, conv_out, bias_out, gain_out, shift_out, down_out, db_out,
    conv_v, down_v, bias_v, gain_v, shift_v, db_v, sems,
):
    copies = [
        pltpu.make_async_copy(src, dst, sems.at[k])
        for k, (src, dst) in enumerate(
            (
                (block, block_out),
                (gimg, gimg_out),
                (conv_v, conv_out),
                (down_v, down_out),
                (bias_v, bias_out),
                (gain_v, gain_out),
                (shift_v, shift_out),
                (db_v, db_out),
            )
        )
    ]
    copies[0].start()
    copies[1].start()
    for tap in range(TAPS):
        conv_v[tap] = table[tap, 4:8]
        if tap < 8:
            down_v[tap, 0:4] = table[2 * tap, 0:4]
            down_v[tap, 4:8] = table[2 * tap + 1, 0:4]
    down_v[8, 0:4] = table[9, 4:8]
    down_v[8, 4:8] = table[10, 4:8]
    d = lax.axis_index("dp")
    narrow = pltpu.roll(table[12], lax.rem(CHANS - 4 * d, CHANS), 1)
    bias_v[...] = narrow[4:5, :4]
    gain_v[...] = narrow[5:6, :4]
    shift_v[...] = narrow[6:7, :4]
    wide = pltpu.roll(table[13], lax.rem(2 * CHANS - 8 * d, CHANS), 1)
    db_v[...] = jnp.where(d < 16, wide[4:5, :8], wide[5:6, :8])
    for copy in copies[2:]:
        copy.start()
    for copy in copies:
        copy.wait()


def shards(
    images, conv_weight, conv_bias, norm_gain, norm_shift, down_weight, down_bias, cotangent
):
    rows_n = lax.axis_size("rows")
    dp_n = lax.axis_size("dp")
    _, local_rows, cols, chans = images.shape
    half = cols // 2
    vmem = pl.BlockSpec(memory_space=pltpu.VMEM)
    dma = pltpu.SemaphoreType.DMA
    anywhere = pl.BlockSpec(memory_space=pl.ANY)
    unit = (CHANS, CHANS)
    slots = rows_n // 2
    scratch = [
        pltpu.VMEM((local_rows, cols, chans), BF),
        pltpu.VMEM(conv_weight.shape, BF),
        pltpu.VMEM((1, CHANS), F32),
        pltpu.VMEM((1, CHANS), F32),
        pltpu.VMEM((1, CHANS), F32),
        pltpu.VMEM(down_weight.shape, BF),
        pltpu.VMEM((1, OUTS), F32),
        pltpu.VMEM((half, OUTS), BF),
        pltpu.VMEM((half, OUTS), BF),
        pltpu.VMEM((local_rows, cols, chans), BF),
        pltpu.VMEM((half + 16, OUTS), F32),
        pltpu.VMEM((cols + 16, CHANS), F32),
        pltpu.VMEM((2, cols, CHANS), BF),
        pltpu.VMEM((half, OUTS), BF),
        pltpu.VMEM((4, half, 4 * CHANS), BF),
        pltpu.VMEM((3, half, 3 * CHANS), BF),
        pltpu.VMEM((4, half, 4 * CHANS), BF),
        pltpu.VMEM((3, 4 * CHANS, 2 * CHANS), BF),
        pltpu.VMEM((3, 2 * CHANS, 4 * CHANS), BF),
        pltpu.VMEM((2, half, 2 * CHANS), F32),
        pltpu.VMEM((2, half, 2 * CHANS), F32),
        pltpu.VMEM((2, half, 2 * CHANS), F32),
        pltpu.VMEM((rows_n, 8, CHANS), F32),
        pltpu.VMEM((rows_n, 8, CHANS), F32),
        pltpu.VMEM((2, 8, CHANS), F32),
        pltpu.VMEM((2, slots) + unit, F32),
        pltpu.VMEM((2, LATE) + unit, F32),
        pltpu.VMEM((slots,) + unit, BF),
        pltpu.VMEM((slots,) + unit, BF),
        pltpu.VMEM((LATE,) + unit, BF),
        pltpu.VMEM((LATE,) + unit, BF),
        pltpu.VMEM((slots,) + unit, BF),
        pltpu.VMEM((slots,) + unit, BF),
        pltpu.VMEM((LATE,) + unit, BF),
        pltpu.VMEM((slots,) + unit, BF),
        pltpu.VMEM(unit, F32),
        pltpu.VMEM(unit, F32),
        pltpu.VMEM((OUTS, CHANS), F32),
        pltpu.VMEM((dp_n, 8, CHANS), F32),
        dma((8,)),
        dma((2,)),
        dma((2,)),
        dma((2,)),
        dma,
        dma,
        dma,
        dma,
        dma((2,)),
        dma((2,)),
        dma((rows_n,)),
        dma((rows_n,)),
        dma((rows_n,)),
        dma((rows_n,)),
        dma((2,)),
        dma((2,)),
        dma((slots,)),
        dma((slots,)),
        dma((slots,)),
        dma((slots,)),
        dma((dp_n,)),
        dma((dp_n,)),
        dma((rows_n,)),
        dma((rows_n,)),
    ]

    def body(*refs):
        kernel(rows_n, dp_n, *refs)

    block, grad_image, table = pl.pallas_call(
        body,
        out_shape=(
            jax.ShapeDtypeStruct((1, 1, half, OUTS), BF),
            jax.ShapeDtypeStruct((1, local_rows, cols, chans), BF),
            jax.ShapeDtypeStruct((rows_n, 8, CHANS), F32),
        ),
        in_specs=[anywhere] * 8,
        out_specs=(anywhere, anywhere, vmem),
        scratch_shapes=scratch,
        compiler_params=pltpu.CompilerParams(
            collective_id=0, has_side_effects=True, vmem_limit_bytes=56 * 1024 * 1024
        ),
        name="step",
    )(
        images,
        conv_weight,
        conv_bias.reshape(1, CHANS),
        norm_gain.reshape(1, CHANS),
        norm_shift.reshape(1, CHANS),
        down_weight,
        down_bias.reshape(1, OUTS),
        cotangent.reshape(1, half, OUTS),
    )
    shape = jax.ShapeDtypeStruct
    outs = pl.pallas_call(
        finish,
        out_shape=(
            shape(block.shape, BF),
            shape(grad_image.shape, BF),
            shape((TAPS, 4, CHANS), F32),
            shape((1, 4), F32),
            shape((1, 4), F32),
            shape((1, 4), F32),
            shape((TAPS, 8, CHANS), F32),
            shape((1, 8), F32),
        ),
        in_specs=[anywhere, anywhere, vmem],
        out_specs=[anywhere] * 8,
        scratch_shapes=[
            pltpu.VMEM((TAPS, 4, CHANS), F32),
            pltpu.VMEM((TAPS, 8, CHANS), F32),
            pltpu.VMEM((1, 4), F32),
            pltpu.VMEM((1, 4), F32),
            pltpu.VMEM((1, 4), F32),
            pltpu.VMEM((1, 8), F32),
            dma((8,)),
        ],
        name="finish",
    )(block, grad_image, table)
    block, grad_image, conv_t, bias, gain, shift, down_t, down_bias_grad = outs
    return (
        block,
        grad_image,
        jnp.swapaxes(conv_t, 1, 2).reshape(3, 3, CHANS, 4),
        bias.reshape(4),
        gain.reshape(4),
        shift.reshape(4),
        jnp.swapaxes(down_t, 1, 2).reshape(3, 3, CHANS, 8),
        down_bias_grad.reshape(8),
    )


def solution(mesh):
    spread = P("dp", "rows", None, None)
    in_specs = (spread, P(), P(), P(), P(), P(), P(), spread)
    out_specs = (
        spread,
        spread,
        P(None, None, None, "dp"),
        P("dp"),
        P("dp"),
        P("dp"),
        P(None, None, None, "dp"),
        P("dp"),
    )
    return jax.shard_map(shards, mesh=mesh, in_specs=in_specs, out_specs=out_specs, check_vma=False)
```

```python
import jax
import jax.numpy as jnp
from jax import lax
from jax.experimental import pallas as pl
from jax.experimental.pallas import tpu as pltpu
from jax.sharding import PartitionSpec as P

GROUPS = 32
CHANS = 128
OUTS = 256
BF = jnp.bfloat16
F32 = jnp.float32
MESH = pl.DeviceIdType.MESH
EPS = 1e-05
TAPS = 9
LATE = 6


def nn(a, b):
    return lax.dot_general(a, b, (((1,), (0,)), ((), ())), preferred_element_type=F32)


def nt(a, b):
    return lax.dot_general(a, b, (((1,), (1,)), ((), ())), preferred_element_type=F32)


def tn(a, b):
    return lax.dot_general(a, b, (((0,), (0,)), ((), ())), preferred_element_type=F32)


def group_sum(x):
    lane = lax.broadcasted_iota(jnp.int32, x.shape, 1)
    x = x + jnp.where(lane % 2 == 0, pltpu.roll(x, CHANS - 1, 1), pltpu.roll(x, 1, 1))
    return x + jnp.where(lane % 4 < 2, pltpu.roll(x, CHANS - 2, 1), pltpu.roll(x, 2, 1))


def twice(x):
    return jnp.concatenate([x, x], axis=1)


def fold(x):
    return x[:, :CHANS] + x[:, CHANS:]


def kernel(
    rows_n,
    dp_n,
    img_hbm,
    cw_hbm,
    cb_hbm,
    gain_hbm,
    shift_hbm,
    dw_hbm,
    db_hbm,
    cot_hbm,
    block_out,
    gimg_out,
    gout,
    img,
    cw,
    cb,
    gain_ref,
    shift_ref,
    dw,
    db,
    cot,
    wide,
    tall,
    edge_img,
    edge_cot,
    x4,
    m4,
    g4,
    wf,
    wb,
    hid,
    gpre,
    gmix,
    stat_a,
    stat_b,
    mine,
    early,
    late,
    cs,
    cr,
    cs2,
    cr2,
    rs,
    rr,
    rs2,
    rr2,
    red1,
    red2,
    red,
    dr,
    load_sem,
    img_s,
    img_r,
    cot_s,
    cot_r,
    mix_s,
    mix_r,
    g_s,
    g_r,
    sa_s,
    sa_r,
    sb_s,
    sb_r,
    c_s,
    c_r,
    r_s,
    r_r,
    q_s,
    q_r,
    d_s,
    d_r,
    o_s,
    o_r,
):
    r = lax.axis_index("rows")
    d = lax.axis_index("dp")
    core = lax.rem(r, 2)
    slot = lax.div(r, 2)
    mate = r + 1 - 2 * core
    half = cot.shape[0]
    cols = 2 * half
    n_local = float(2 * cols * (CHANS // GROUPS))
    n_total = n_local * rows_n
    last = rows_n - 1
    slots = rows_n // 2

    def remote(src, dst, send, recv, **where):
        return pltpu.make_async_remote_copy(
            src_ref=src,
            dst_ref=dst,
            send_sem=send,
            recv_sem=recv,
            device_id=where,
            device_id_type=MESH,
        )

    loads = [
        pltpu.make_async_copy(src, dst, load_sem.at[k])
        for k, (src, dst) in enumerate(
            (
                (img_hbm.at[0], img),
                (cw_hbm, cw),
                (cot_hbm.at[0], cot),
                (dw_hbm, dw),
                (cb_hbm, cb),
                (gain_hbm, gain_ref),
                (shift_hbm, shift_ref),
                (db_hbm, db),
            )
        )
    ]
    for load in loads:
        load.start()

    x_at, y_at = lax.div(r, 4), lax.rem(slot, 2)
    hops = sorted(
        ((min(dx, 4 - dx) + dy, dc, dx, dy) for dx in range(4) for dy in range(2) for dc in range(2)),
        reverse=True,
    )
    row_peers = [
        lax.rem(x_at + dx, 4) * 4
        + (y_at if dy == 0 else 1 - y_at) * 2
        + (core if dc == 0 else 1 - core)
        for _, dc, dx, dy in hops[:-1]
    ]
    if dp_n == 32:
        z_at, h_at = lax.div(d, 4), lax.rem(d, 4)
        hops = sorted(
            ((min(dz, 8 - dz) + 2 * min(dh, 4 - dh), dz, dh) for dz in range(8) for dh in range(4)),
            reverse=True,
        )
        dp_peers = [
            lax.rem(z_at + dz, 8) * 4 + lax.rem(h_at + dh, 4) for _, dz, dh in hops[:-1]
        ]
    else:
        dp_peers = [lax.rem(d + i, dp_n) for i in range(1, dp_n)]

    barrier = pltpu.get_barrier_semaphore()
    for to in dp_peers:
        pl.semaphore_signal(barrier, inc=1, device_id={"dp": to}, device_id_type=MESH)
    for to in row_peers:
        pl.semaphore_signal(barrier, inc=1, device_id={"rows": to}, device_id_type=MESH)

    pl.semaphore_wait(barrier, rows_n + dp_n - 2)
    up = lax.max(r - 1, 0)
    down = lax.min(r + 1, last)
    mid = pl.ds(CHANS, 2 * CHANS)
    img_down = remote(img_hbm.at[0, 1], edge_img.at[0], img_s.at[0], img_r.at[0], rows=down)
    img_up = remote(img_hbm.at[0, 0], edge_img.at[1], img_s.at[1], img_r.at[1], rows=up)
    cot_up = remote(cot_hbm.at[0], edge_cot, cot_s, cot_r, rows=up)
    mix_down = remote(m4.at[2, :, mid], m4.at[0, :, mid], mix_s, mix_r, rows=down)
    g_down = remote(g4.at[2, :, mid], g4.at[0, :, mid], g_s.at[0], g_r.at[0], rows=down)
    g_up = remote(g4.at[1, :, mid], g4.at[3, :, mid], g_s.at[1], g_r.at[1], rows=up)

    @pl.when(r < last)
    def _():
        img_down.start()

    @pl.when(r > 0)
    def _():
        img_up.start()

    loads[1].wait()
    zero_block = jnp.zeros((CHANS, CHANS), BF)
    for kh in range(3):
        for kw in range(3):
            tap = cw[kh, kw]
            wf[kh, kw * CHANS : (kw + 1) * CHANS, :CHANS] = tap
            wf[kh, (kw + 1) * CHANS : (kw + 2) * CHANS, CHANS:] = tap
            wb[kh, :CHANS, (2 - kw) * CHANS : (3 - kw) * CHANS] = tap
            wb[kh, CHANS:, (3 - kw) * CHANS : (4 - kw) * CHANS] = tap
        wf[kh, 3 * CHANS :, :CHANS] = zero_block
        wf[kh, :CHANS, CHANS:] = zero_block
        wb[kh, :CHANS, 3 * CHANS :] = zero_block
        wb[kh, CHANS:, :CHANS] = zero_block

    tall[:8, :] = jnp.zeros((8, CHANS), F32)
    tall[cols + 8 :, :] = jnp.zeros((8, CHANS), F32)
    wide[:8, :] = jnp.zeros((8, OUTS), F32)
    wide[half + 8 :, :] = jnp.zeros((8, OUTS), F32)

    def split_columns(row, f):
        tall[8 : cols + 8, :] = row.astype(F32)
        for k, start in enumerate((7, 8, 9, 10)):
            x4[f, :, k * CHANS : (k + 1) * CHANS] = tall[pl.ds(start, half, stride=2), :].astype(BF)

    def shifted(x, by):
        width = x.shape[1]
        wide[8 : half + 8, :width] = x
        return wide[8 + by : half + 8 + by, :width]

    @pl.when(r == 0)
    def _():
        edge_img[0] = jnp.zeros(edge_img.shape[1:], BF)
        m4[0] = jnp.zeros(m4.shape[1:], BF)
        g4[0] = jnp.zeros(g4.shape[1:], BF)

    @pl.when(r == last)
    def _():
        edge_img[1] = jnp.zeros(edge_img.shape[1:], BF)
        edge_cot[...] = jnp.zeros(edge_cot.shape, BF)
        g4[3] = jnp.zeros(g4.shape[1:], BF)

    for k in (0, 2, 3, 4, 5, 6, 7):
        loads[k].wait()
    for a in range(2):
        split_columns(img[a], a + 1)

    bias = twice(cb[...])
    hid[0] = nn(x4[1], wf[1]) + nn(x4[2], wf[2]) + bias
    hid[1] = nn(x4[1], wf[0]) + nn(x4[2], wf[1]) + bias

    @pl.when(r > 0)
    def _():
        img_down.wait_recv()

    split_columns(edge_img[0], 0)
    hid[0] += nn(x4[0], wf[0])

    @pl.when(r < last)
    def _():
        img_up.wait_recv()

    @pl.when(r > 0)
    def _():
        cot_up.start()

    split_columns(edge_img[1], 3)
    hid[1] += nn(x4[3], wf[2])

    def spread(table, send, recv):
        for to in row_peers:
            remote(table.at[r], table.at[r], send.at[to], recv.at[r], rows=to).start()

    def gathered(table, send, recv):
        for other in row_peers:
            remote(table.at[other], table.at[other], send.at[other], recv.at[other], rows=other).wait()

    def colsum(x):
        return jnp.sum(x, axis=0, keepdims=True)

    own_sum = fold(colsum(hid[0]) + colsum(hid[1]))
    own_mean = twice(group_sum(jnp.broadcast_to(own_sum, (8, CHANS)))[:1] / n_local)
    off0 = hid[0] - own_mean
    off1 = hid[1] - own_mean
    own_sq = fold(colsum(off0 * off0) + colsum(off1 * off1))
    stat_a[r, 0:1, :] = own_sum
    stat_a[r, 1:2, :] = own_sq
    stat_a[r, 2:8, :] = jnp.zeros((6, CHANS), F32)
    spread(stat_a, sa_s, sa_r)

    @pl.when(r < last)
    def _():
        cot_up.wait_recv()

    def pull(grad, lead, kh):
        both = dw[kh, 1:3].reshape(2 * CHANS, OUTS)
        return nt(grad, both), nt(lead, dw[kh, 0])

    own_cot = cot[...]
    own_cot32 = own_cot.astype(F32)
    cot_sum = colsum(own_cot32)
    lead_cot = shifted(own_cot32, 1).astype(BF)
    whole, odd = pull(own_cot, lead_cot, 1)
    gmix[0] = whole
    gmix[0, :, CHANS:] += odd
    whole, odd = pull(own_cot, lead_cot, 2)
    gmix[1] = whole
    gmix[1, :, CHANS:] += odd
    below = edge_cot[...]
    whole, odd = pull(below, shifted(below.astype(F32), 1).astype(BF), 0)
    gmix[1] += whole
    gmix[1, :, CHANS:] += odd

    gathered(stat_a, sa_s, sa_r)
    table = stat_a[...]
    groups = group_sum(table.reshape(rows_n * 8, CHANS)).reshape(rows_n, 8, CHANS)
    group_tot = jnp.sum(groups, axis=0)
    mean = group_tot[0:1] / n_total
    dev = groups / n_local - mean.reshape(1, 1, CHANS)
    spread_sq = jnp.sum(dev * dev, axis=0)[0:1] * n_local
    rstd = lax.rsqrt((group_tot[1:2] + spread_sq) / n_total + EPS)
    channel_sum = jnp.sum(table, axis=0)[0:1]
    mean2, rstd2 = twice(mean), twice(rstd)
    gain2, shift2 = twice(gain_ref[...]), twice(shift_ref[...])

    sum_gp = jnp.zeros((1, 2 * CHANS), F32)
    sum_gpn = jnp.zeros((1, 2 * CHANS), F32)
    for a in (1, 0):
        normed = (hid[a] - mean2) * rstd2
        pre = normed * gain2 + shift2
        sig = jax.nn.sigmoid(pre)
        mixed = (x4[a + 1, :, CHANS : 3 * CHANS].astype(F32) + pre * sig).astype(BF)
        m4[a + 1, :, CHANS:] = mixed
        m4[a + 1, :, :CHANS] = shifted(mixed[:, CHANS:].astype(F32), -1).astype(BF)
        gp = gmix[a] * sig * (1.0 + pre * (1.0 - sig))
        hid[a] = normed
        gpre[a] = gp
        sum_gp += colsum(gp)
        sum_gpn += colsum(gp * normed)

    stat_b[r, 0:1, :] = fold(sum_gp)
    stat_b[r, 1:2, :] = fold(sum_gpn)
    stat_b[r, 2:3, :] = cot_sum[:, :CHANS]
    stat_b[r, 3:4, :] = cot_sum[:, CHANS:]
    stat_b[r, 4:8, :] = jnp.zeros((4, CHANS), F32)
    spread(stat_b, sb_s, sb_r)

    @pl.when(r < last)
    def _():
        mix_down.start()

    sub = lax.broadcasted_iota(jnp.int32, (CHANS, CHANS), 0) % 8

    def down_grad(kh):
        part = tn(own_cot, m4[kh])
        for kw in range(3):
            tap = 3 * kh + kw
            tiles = part[:, kw * CHANS : (kw + 1) * CHANS].reshape(16, 2, 8, CHANS)
            one = tiles[:, 0].reshape(CHANS, CHANS)
            two = tiles[:, 1].reshape(CHANS, CHANS)
            low = jnp.where(sub < 4, one, pltpu.roll(two, 4, 0))
            high = jnp.where(sub < 4, pltpu.roll(one, CHANS - 4, 0), two)
            if tap < 8:
                early[0, tap] = low
                early[1, tap] = high
            else:
                late[1, 4] = low
                late[0, 5] = high

    def taps(kh):
        return dw[kh].reshape(3 * CHANS, OUTS)

    out = nn(m4[1], taps(1)) + nn(m4[2], taps(2)) + db[...]
    down_grad(1)
    down_grad(2)

    @pl.when(r > 0)
    def _():
        mix_down.wait_recv()
        m4[0, :, :CHANS] = shifted(m4[0, :, 2 * CHANS :].astype(F32), -1).astype(BF)

    down_grad(0)
    cs[...] = early[1 - core].astype(BF)
    pair_one = remote(cs, cr, c_s.at[0], c_r.at[0], rows=mate)
    pair_two = remote(cs2, cr2, c_s.at[1], c_r.at[1], rows=mate)
    pair_one.start()
    block_out[0, 0] = (out + nn(m4[0], taps(0))).astype(BF)

    gathered(stat_b, sb_s, sb_r)
    totals = jnp.sum(stat_b[...], axis=0)
    tot_gp = totals[0:1]
    tot_gpn = totals[1:2]
    means = group_sum(
        jnp.broadcast_to(gain_ref[...], (8, CHANS)) * totals
    ) / n_total
    m1, m2 = means[0:1], means[1:2]
    m1w, m2w = twice(m1), twice(m2)
    for a in range(2):
        grad = (rstd2 * (gpre[a] * gain2 - m1w - hid[a] * m2w)).astype(BF)
        g4[a + 1, :, CHANS : 3 * CHANS] = grad

    n_channel = float(2 * cols * rows_n)
    tot_normed = (channel_sum - n_channel * mean) * rstd
    tot_bias = rstd * (gain_ref[...] * tot_gp - n_channel * m1 - m2 * tot_normed)
    mine[...] = jnp.zeros(mine.shape, F32)
    for k in (0, 4):
        mine[0, k : k + 1, :] = tot_bias
        mine[0, k + 1 : k + 2, :] = tot_gpn
        mine[0, k + 2 : k + 3, :] = tot_gp
        mine[1, k : k + 1, :] = totals[2:3]
        mine[1, k + 1 : k + 2, :] = totals[3:4]

    slot_peers = [
        lax.rem(x_at + dx, 4) * 2 + (y_at if dy == 0 else 1 - y_at)
        for dx, dy in ((2, 1), (2, 0), (1, 1), (3, 1), (1, 0), (3, 0), (0, 1))
    ]

    def early_send(to):
        return remote(rs.at[to], rr.at[slot], r_s.at[to], r_r.at[slot], rows=2 * to + core)

    def late_send(to):
        return remote(
            rs2.at[lax.min(to, LATE - 1)], rr2.at[slot], q_s.at[to], q_r.at[slot], rows=2 * to + core
        )

    pair_one.wait()
    both = early[core] + cr[...].astype(F32)
    early[core] = both
    rs[...] = both.astype(BF)
    for to in slot_peers:
        early_send(to).start()

    for kh in range(3):
        part = tn(g4[1, :, CHANS : 3 * CHANS], x4[kh]) + tn(
            g4[2, :, CHANS : 3 * CHANS], x4[kh + 1]
        )
        for kw in range(3):
            tap = 3 * kh + kw
            late[tap % 2, tap // 2] = (
                part[:CHANS, kw * CHANS : (kw + 1) * CHANS]
                + part[CHANS:, (kw + 1) * CHANS : (kw + 2) * CHANS]
            )
    late[1, 5] = jnp.zeros((CHANS, CHANS), F32)
    cs2[...] = late[1 - core].astype(BF)
    pair_two.start()

    def sides(f):
        grad = g4[f, :, CHANS : 3 * CHANS].astype(F32)
        g4[f, :, :CHANS] = shifted(grad[:, CHANS:], -1).astype(BF)
        g4[f, :, 3 * CHANS :] = shifted(grad[:, :CHANS], 1).astype(BF)

    pair_two.wait()
    both = late[core] + cr2[...].astype(F32)
    late[core] = both
    rs2[...] = both.astype(BF)
    for to in slot_peers:

        @pl.when(to < LATE)
        def _():
            late_send(to).start()

    @pl.when(r < last)
    def _():
        g_down.start()

    @pl.when(r > 0)
    def _():
        g_up.start()

    sides(1)
    sides(2)
    gmix[0] += nt(g4[1], wb[1]) + nt(g4[2], wb[0])
    gmix[1] += nt(g4[1], wb[2]) + nt(g4[2], wb[1])

    total = early[core, slot]
    for other in slot_peers:
        remote(rs.at[0], rr.at[other], r_s.at[other], r_r.at[other], rows=2 * other + core).wait_recv()
        total = total + rr[other].astype(F32)
    red1[...] = total

    @pl.when(slot < LATE)
    def _():
        for other in slot_peers:
            remote(rs2.at[0], rr2.at[other], q_s.at[other], q_r.at[other], rows=2 * other + core).wait_recv()
        total = late[core, lax.min(slot, LATE - 1)]
        for other in slot_peers:
            total = total + rr2[other].astype(F32)
        red2[...] = total

    @pl.when(slot >= LATE)
    def _():
        red2[...] = jnp.broadcast_to(mine[core][None], (16, 8, CHANS)).reshape(CHANS, CHANS)

    one, two = red1[...], red2[...]
    red[:CHANS] = jnp.where(sub < 4, one, pltpu.roll(two, 4, 0))
    red[CHANS:] = jnp.where(sub < 4, pltpu.roll(one, CHANS - 4, 0), two)

    def place(e):
        row = lax.rem(e, 2) * 16 + lax.div(e, 2)
        return pl.ds(pl.multiple_of(row * 8, 8), 8)

    for to in dp_peers:
        remote(red.at[place(to)], dr.at[d], d_s.at[to], d_r.at[d], dp=to).start()
    dr[d] = red[place(d), :]

    def put_row(a):
        tall[pl.ds(8, half, stride=2), :] = gmix[a, :, :CHANS]
        tall[pl.ds(9, half, stride=2), :] = gmix[a, :, CHANS:]
        gimg_out[0, a] = tall[8 : cols + 8, :].astype(BF)

    @pl.when(r > 0)
    def _():
        g_down.wait_recv()
        sides(0)

    gmix[0] += nt(g4[0], wb[2])
    put_row(0)

    @pl.when(r < last)
    def _():
        g_up.wait_recv()
        sides(3)

    gmix[1] += nt(g4[3], wb[0])
    put_row(1)

    for other in dp_peers:
        remote(red.at[place(other)], dr.at[other], d_s.at[other], d_r.at[other], dp=other).wait()
    gout[r] = jnp.sum(dr[...], axis=0)
    spread(gout, o_s, o_r)
    gathered(gout, o_s, o_r)

    @pl.when(r < last)
    def _():
        img_down.wait_send()
        mix_down.wait_send()
        g_down.wait_send()

    @pl.when(r > 0)
    def _():
        img_up.wait_send()
        cot_up.wait_send()
        g_up.wait_send()

    for to in slot_peers:
        early_send(to).wait_send()

        @pl.when(to < LATE)
        def _():
            late_send(to).wait_send()


def finish(
    block, gimg, table, block_out, gimg_out, conv_out, bias_out, gain_out, shift_out, down_out, db_out,
    conv_v, down_v, bias_v, gain_v, shift_v, db_v, sems,
):
    copies = [
        pltpu.make_async_copy(src, dst, sems.at[k])
        for k, (src, dst) in enumerate(
            (
                (block, block_out),
                (gimg, gimg_out),
                (conv_v, conv_out),
                (down_v, down_out),
                (bias_v, bias_out),
                (gain_v, gain_out),
                (shift_v, shift_out),
                (db_v, db_out),
            )
        )
    ]
    copies[0].start()
    copies[1].start()
    for tap in range(TAPS):
        conv_v[tap] = table[tap, 4:8]
        if tap < 8:
            down_v[tap, 0:4] = table[2 * tap, 0:4]
            down_v[tap, 4:8] = table[2 * tap + 1, 0:4]
    down_v[8, 0:4] = table[9, 4:8]
    down_v[8, 4:8] = table[10, 4:8]
    d = lax.axis_index("dp")
    narrow = pltpu.roll(table[12], lax.rem(CHANS - 4 * d, CHANS), 1)
    bias_v[...] = narrow[4:5, :4]
    gain_v[...] = narrow[5:6, :4]
    shift_v[...] = narrow[6:7, :4]
    wide = pltpu.roll(table[13], lax.rem(2 * CHANS - 8 * d, CHANS), 1)
    db_v[...] = jnp.where(d < 16, wide[4:5, :8], wide[5:6, :8])
    for copy in copies[2:]:
        copy.start()
    for copy in copies:
        copy.wait()


def shards(
    images, conv_weight, conv_bias, norm_gain, norm_shift, down_weight, down_bias, cotangent
):
    rows_n = lax.axis_size("rows")
    dp_n = lax.axis_size("dp")
    _, local_rows, cols, chans = images.shape
    half = cols // 2
    vmem = pl.BlockSpec(memory_space=pltpu.VMEM)
    dma = pltpu.SemaphoreType.DMA
    anywhere = pl.BlockSpec(memory_space=pltpu.HBM)
    unit = (CHANS, CHANS)
    slots = rows_n // 2
    scratch = [
        pltpu.VMEM((local_rows, cols, chans), BF),
        pltpu.VMEM(conv_weight.shape, BF),
        pltpu.VMEM((1, CHANS), F32),
        pltpu.VMEM((1, CHANS), F32),
        pltpu.VMEM((1, CHANS), F32),
        pltpu.VMEM(down_weight.shape, BF),
        pltpu.VMEM((1, OUTS), F32),
        pltpu.VMEM((half, OUTS), BF),
        pltpu.VMEM((half + 16, OUTS), F32),
        pltpu.VMEM((cols + 16, CHANS), F32),
        pltpu.VMEM((2, cols, CHANS), BF),
        pltpu.VMEM((half, OUTS), BF),
        pltpu.VMEM((4, half, 4 * CHANS), BF),
        pltpu.VMEM((3, half, 3 * CHANS), BF),
        pltpu.VMEM((4, half, 4 * CHANS), BF),
        pltpu.VMEM((3, 4 * CHANS, 2 * CHANS), BF),
        pltpu.VMEM((3, 2 * CHANS, 4 * CHANS), BF),
        pltpu.VMEM((2, half, 2 * CHANS), F32),
        pltpu.VMEM((2, half, 2 * CHANS), F32),
        pltpu.VMEM((2, half, 2 * CHANS), F32),
        pltpu.VMEM((rows_n, 8, CHANS), F32),
        pltpu.VMEM((rows_n, 8, CHANS), F32),
        pltpu.VMEM((2, 8, CHANS), F32),
        pltpu.VMEM((2, slots) + unit, F32),
        pltpu.VMEM((2, LATE) + unit, F32),
        pltpu.VMEM((slots,) + unit, BF),
        pltpu.VMEM((slots,) + unit, BF),
        pltpu.VMEM((LATE,) + unit, BF),
        pltpu.VMEM((LATE,) + unit, BF),
        pltpu.VMEM((slots,) + unit, BF),
        pltpu.VMEM((slots,) + unit, BF),
        pltpu.VMEM((LATE,) + unit, BF),
        pltpu.VMEM((slots,) + unit, BF),
        pltpu.VMEM(unit, F32),
        pltpu.VMEM(unit, F32),
        pltpu.VMEM((OUTS, CHANS), F32),
        pltpu.VMEM((dp_n, 8, CHANS), F32),
        dma((8,)),
        dma((2,)),
        dma((2,)),
        dma,
        dma,
        dma,
        dma,
        dma((2,)),
        dma((2,)),
        dma((rows_n,)),
        dma((rows_n,)),
        dma((rows_n,)),
        dma((rows_n,)),
        dma((2,)),
        dma((2,)),
        dma((slots,)),
        dma((slots,)),
        dma((slots,)),
        dma((slots,)),
        dma((dp_n,)),
        dma((dp_n,)),
        dma((rows_n,)),
        dma((rows_n,)),
    ]

    def body(*refs):
        kernel(rows_n, dp_n, *refs)

    block, grad_image, table = pl.pallas_call(
        body,
        out_shape=(
            jax.ShapeDtypeStruct((1, 1, half, OUTS), BF),
            jax.ShapeDtypeStruct((1, local_rows, cols, chans), BF),
            jax.ShapeDtypeStruct((rows_n, 8, CHANS), F32),
        ),
        in_specs=[anywhere] * 8,
        out_specs=(vmem, vmem, vmem),
        scratch_shapes=scratch,
        compiler_params=pltpu.CompilerParams(
            collective_id=0, has_side_effects=True, vmem_limit_bytes=40 * 1024 * 1024
        ),
        name="step",
    )(*(pltpu.with_memory_space_constraint(x, pltpu.HBM) for x in (
        images,
        conv_weight,
        conv_bias.reshape(1, CHANS),
        norm_gain.reshape(1, CHANS),
        norm_shift.reshape(1, CHANS),
        down_weight,
        down_bias.reshape(1, OUTS),
        cotangent.reshape(1, half, OUTS),
    )))
    shape = jax.ShapeDtypeStruct
    outs = pl.pallas_call(
        finish,
        out_shape=(
            shape(block.shape, BF),
            shape(grad_image.shape, BF),
            shape((TAPS, 4, CHANS), F32),
            shape((1, 4), F32),
            shape((1, 4), F32),
            shape((1, 4), F32),
            shape((TAPS, 8, CHANS), F32),
            shape((1, 8), F32),
        ),
        in_specs=[vmem, vmem, vmem],
        out_specs=[anywhere] * 8,
        scratch_shapes=[
            pltpu.VMEM((TAPS, 4, CHANS), F32),
            pltpu.VMEM((TAPS, 8, CHANS), F32),
            pltpu.VMEM((1, 4), F32),
            pltpu.VMEM((1, 4), F32),
            pltpu.VMEM((1, 4), F32),
            pltpu.VMEM((1, 8), F32),
            dma((8,)),
        ],
        compiler_params=pltpu.CompilerParams(vmem_limit_bytes=4 * 1024 * 1024),
        name="finish",
    )(block, grad_image, table)
    block, grad_image, conv_t, bias, gain, shift, down_t, down_bias_grad = outs
    return (
        block,
        grad_image,
        jnp.swapaxes(conv_t, 1, 2).reshape(3, 3, CHANS, 4),
        bias.reshape(4),
        gain.reshape(4),
        shift.reshape(4),
        jnp.swapaxes(down_t, 1, 2).reshape(3, 3, CHANS, 8),
        down_bias_grad.reshape(8),
    )


def solution(mesh):
    spread = P("dp", "rows", None, None)
    in_specs = (spread, P(), P(), P(), P(), P(), P(), spread)
    out_specs = (
        spread,
        spread,
        P(None, None, None, "dp"),
        P("dp"),
        P("dp"),
        P("dp"),
        P(None, None, None, "dp"),
        P("dp"),
    )
    return jax.shard_map(shards, mesh=mesh, in_specs=in_specs, out_specs=out_specs, check_vma=False)
```

```python
import jax
import jax.numpy as jnp
from jax import lax
from jax.experimental import pallas as pl
from jax.experimental.pallas import tpu as pltpu
from jax.sharding import PartitionSpec as P

GROUPS = 32
CHANS = 128
OUTS = 256
BF = jnp.bfloat16
F32 = jnp.float32
MESH = pl.DeviceIdType.MESH
EPS = 1e-05
TAPS = 9
EARLY = 6


def nn(a, b):
    return lax.dot_general(a, b, (((1,), (0,)), ((), ())), preferred_element_type=F32)


def nt(a, b):
    return lax.dot_general(a, b, (((1,), (1,)), ((), ())), preferred_element_type=F32)


def tn(a, b):
    return lax.dot_general(a, b, (((0,), (0,)), ((), ())), preferred_element_type=F32)


def group_sum(x):
    lane = lax.broadcasted_iota(jnp.int32, x.shape, 1)
    x = x + jnp.where(lane % 2 == 0, pltpu.roll(x, CHANS - 1, 1), pltpu.roll(x, 1, 1))
    return x + jnp.where(lane % 4 < 2, pltpu.roll(x, CHANS - 2, 1), pltpu.roll(x, 2, 1))


def twice(x):
    return jnp.concatenate([x, x], axis=1)


def fold(x):
    return x[:, :CHANS] + x[:, CHANS:]


def kernel(
    rows_n,
    dp_n,
    img_hbm,
    cw_hbm,
    cb_hbm,
    gain_hbm,
    shift_hbm,
    dw_hbm,
    db_hbm,
    cot_hbm,
    block_out,
    gimg_out,
    gout,
    img,
    cw,
    cb,
    gain_ref,
    shift_ref,
    dw,
    db,
    cot,
    wide,
    tall,
    edge_img,
    edge_cot,
    x4,
    m4,
    g4,
    wf,
    wb,
    hid,
    gpre,
    gmix,
    hold,
    stat_a,
    stat_b,
    mine,
    early,
    late,
    cs,
    cr,
    cs2,
    cr2,
    rs,
    rr,
    rs2,
    rr2,
    red1,
    red2,
    red,
    dr,
    load_sem,
    img_s,
    img_r,
    cot_s,
    cot_r,
    mix_s,
    mix_r,
    g_s,
    g_r,
    sa_s,
    sa_r,
    sb_s,
    sb_r,
    c_s,
    c_r,
    r_s,
    r_r,
    q_s,
    q_r,
    d_s,
    d_r,
    o_s,
    o_r,
):
    r = lax.axis_index("rows")
    d = lax.axis_index("dp")
    core = lax.rem(r, 2)
    slot = lax.div(r, 2)
    mate = r + 1 - 2 * core
    half = cot.shape[0]
    cols = 2 * half
    n_local = float(2 * cols * (CHANS // GROUPS))
    n_total = n_local * rows_n
    last = rows_n - 1
    slots = rows_n // 2

    def remote(src, dst, send, recv, **where):
        return pltpu.make_async_remote_copy(
            src_ref=src,
            dst_ref=dst,
            send_sem=send,
            recv_sem=recv,
            device_id=where,
            device_id_type=MESH,
        )

    loads = [
        pltpu.make_async_copy(src, dst, load_sem.at[k])
        for k, (src, dst) in enumerate(
            (
                (img_hbm.at[0], img),
                (cw_hbm, cw),
                (cot_hbm.at[0], cot),
                (dw_hbm, dw),
                (cb_hbm, cb),
                (gain_hbm, gain_ref),
                (shift_hbm, shift_ref),
                (db_hbm, db),
            )
        )
    ]
    x_at, y_at = lax.div(r, 4), lax.rem(slot, 2)
    hops = sorted(
        ((min(dx, 4 - dx) + dy, dc, dx, dy) for dx in range(4) for dy in range(2) for dc in range(2)),
        reverse=True,
    )
    row_peers = [
        lax.rem(x_at + dx, 4) * 4
        + (y_at if dy == 0 else 1 - y_at) * 2
        + (core if dc == 0 else 1 - core)
        for _, dc, dx, dy in hops[:-1]
    ]
    if dp_n == 32:
        z_at, h_at = lax.div(d, 4), lax.rem(d, 4)
        hops = sorted(
            ((min(dz, 8 - dz) + 2 * min(dh, 4 - dh), dz, dh) for dz in range(8) for dh in range(4)),
            reverse=True,
        )
        dp_peers = [
            lax.rem(z_at + dz, 8) * 4 + lax.rem(h_at + dh, 4) for _, dz, dh in hops[:-1]
        ]
    else:
        dp_peers = [lax.rem(d + i, dp_n) for i in range(1, dp_n)]

    barrier = pltpu.get_barrier_semaphore()
    for to in dp_peers:
        pl.semaphore_signal(barrier, inc=1, device_id={"dp": to}, device_id_type=MESH)
    for to in row_peers:
        pl.semaphore_signal(barrier, inc=1, device_id={"rows": to}, device_id_type=MESH)

    for load in loads:
        load.start()

    pl.semaphore_wait(barrier, rows_n + dp_n - 2)
    up = lax.max(r - 1, 0)
    down = lax.min(r + 1, last)
    mid = pl.ds(CHANS, 2 * CHANS)
    img_down = remote(img_hbm.at[0, 1], edge_img.at[0], img_s.at[0], img_r.at[0], rows=down)
    img_up = remote(img_hbm.at[0, 0], edge_img.at[1], img_s.at[1], img_r.at[1], rows=up)
    cot_up = remote(cot_hbm.at[0], edge_cot, cot_s, cot_r, rows=up)
    mix_down = remote(m4.at[2, :, mid], m4.at[0, :, mid], mix_s, mix_r, rows=down)
    g_down = remote(g4.at[2, :, mid], g4.at[0, :, mid], g_s.at[0], g_r.at[0], rows=down)
    g_up = remote(g4.at[1, :, mid], g4.at[3, :, mid], g_s.at[1], g_r.at[1], rows=up)

    @pl.when(r < last)
    def _():
        img_down.start()

    @pl.when(r > 0)
    def _():
        img_up.start()
        cot_up.start()

    loads[1].wait()
    zero_block = jnp.zeros((CHANS, CHANS), BF)
    for kh in range(3):
        for kw in range(3):
            tap = cw[kh, kw]
            wf[kh, kw * CHANS : (kw + 1) * CHANS, :CHANS] = tap
            wf[kh, (kw + 1) * CHANS : (kw + 2) * CHANS, CHANS:] = tap
            wb[kh, :CHANS, (2 - kw) * CHANS : (3 - kw) * CHANS] = tap
            wb[kh, CHANS:, (3 - kw) * CHANS : (4 - kw) * CHANS] = tap
        wf[kh, 3 * CHANS :, :CHANS] = zero_block
        wf[kh, :CHANS, CHANS:] = zero_block
        wb[kh, :CHANS, 3 * CHANS :] = zero_block
        wb[kh, CHANS:, :CHANS] = zero_block

    tall[:8, :] = jnp.zeros((8, CHANS), F32)
    tall[cols + 8 :, :] = jnp.zeros((8, CHANS), F32)
    wide[:8, :] = jnp.zeros((8, OUTS), F32)
    wide[half + 8 :, :] = jnp.zeros((8, OUTS), F32)

    def split_columns(row, f):
        tall[8 : cols + 8, :] = row.astype(F32)
        for k, start in enumerate((7, 8, 9, 10)):
            x4[f, :, k * CHANS : (k + 1) * CHANS] = tall[pl.ds(start, half, stride=2), :].astype(BF)

    def shifted(x, by):
        width = x.shape[1]
        wide[8 : half + 8, :width] = x
        return wide[8 + by : half + 8 + by, :width]

    @pl.when(r == 0)
    def _():
        edge_img[0] = jnp.zeros(edge_img.shape[1:], BF)
        m4[0] = jnp.zeros(m4.shape[1:], BF)
        g4[0] = jnp.zeros(g4.shape[1:], BF)

    @pl.when(r == last)
    def _():
        edge_img[1] = jnp.zeros(edge_img.shape[1:], BF)
        edge_cot[...] = jnp.zeros(edge_cot.shape, BF)
        g4[3] = jnp.zeros(g4.shape[1:], BF)

    for k in (0, 2, 3, 4, 5, 6, 7):
        loads[k].wait()
    for a in range(2):
        split_columns(img[a], a + 1)

    bias = twice(cb[...])
    hid[0] = nn(x4[1], wf[1]) + nn(x4[2], wf[2]) + bias
    hid[1] = nn(x4[1], wf[0]) + nn(x4[2], wf[1]) + bias

    @pl.when(r > 0)
    def _():
        img_down.wait_recv()

    split_columns(edge_img[0], 0)
    hid[0] += nn(x4[0], wf[0])

    @pl.when(r < last)
    def _():
        img_up.wait_recv()

    split_columns(edge_img[1], 3)
    hid[1] += nn(x4[3], wf[2])

    def spread(table, send, recv):
        for to in row_peers:
            remote(table.at[r], table.at[r], send, recv, rows=to).start()

    def whole(table, send, recv):
        part = table.at[pl.ds(0, rows_n - 1)]
        return remote(part, part, send, recv, rows=mate)

    def colsum(x):
        return jnp.sum(x, axis=0, keepdims=True)

    own_sum = fold(colsum(hid[0]) + colsum(hid[1]))
    own_mean = twice(group_sum(jnp.broadcast_to(own_sum, (8, CHANS)))[:1] / n_local)
    off0 = hid[0] - own_mean
    off1 = hid[1] - own_mean
    own_sq = fold(colsum(off0 * off0) + colsum(off1 * off1))
    stat_a[r, 0:1, :] = own_sum
    stat_a[r, 1:2, :] = own_sq
    stat_a[r, 2:8, :] = jnp.zeros((6, CHANS), F32)
    spread(stat_a, sa_s, sa_r)

    @pl.when(r < last)
    def _():
        cot_up.wait_recv()

    def pull(grad, lead, kh):
        both = dw[kh, 1:3].reshape(2 * CHANS, OUTS)
        return nt(grad, both), nt(lead, dw[kh, 0])

    own_cot = cot[...]
    own_cot32 = own_cot.astype(F32)
    cot_sum = colsum(own_cot32)
    lead_cot = shifted(own_cot32, 1).astype(BF)
    full, odd = pull(own_cot, lead_cot, 1)
    gmix[0] = full
    gmix[0, :, CHANS:] += odd
    full, odd = pull(own_cot, lead_cot, 2)
    gmix[1] = full
    gmix[1, :, CHANS:] += odd
    below = edge_cot[...]
    full, odd = pull(below, shifted(below.astype(F32), 1).astype(BF), 0)
    gmix[1] += full
    gmix[1, :, CHANS:] += odd

    whole(stat_a, sa_s, sa_r).wait_recv()
    table = stat_a[...]
    groups = group_sum(table.reshape(rows_n * 8, CHANS)).reshape(rows_n, 8, CHANS)
    group_tot = jnp.sum(groups, axis=0)
    mean = group_tot[0:1] / n_total
    dev = groups / n_local - mean.reshape(1, 1, CHANS)
    spread_sq = jnp.sum(dev * dev, axis=0)[0:1] * n_local
    rstd = lax.rsqrt((group_tot[1:2] + spread_sq) / n_total + EPS)
    channel_sum = jnp.sum(table, axis=0)[0:1]
    mean2, rstd2 = twice(mean), twice(rstd)
    gain2, shift2 = twice(gain_ref[...]), twice(shift_ref[...])

    sum_gp = jnp.zeros((1, 2 * CHANS), F32)
    sum_gpn = jnp.zeros((1, 2 * CHANS), F32)
    for a in (1, 0):
        normed = (hid[a] - mean2) * rstd2
        pre = normed * gain2 + shift2
        sig = jax.nn.sigmoid(pre)
        mixed = (x4[a + 1, :, CHANS : 3 * CHANS].astype(F32) + pre * sig).astype(BF)
        m4[a + 1, :, CHANS:] = mixed
        gp = gmix[a] * sig * (1.0 + pre * (1.0 - sig))
        hid[a] = normed
        gpre[a] = gp
        sum_gp += colsum(gp)
        sum_gpn += colsum(gp * normed)

    stat_b[r, 0:1, :] = fold(sum_gp)
    stat_b[r, 1:2, :] = fold(sum_gpn)
    stat_b[r, 2:3, :] = cot_sum[:, :CHANS]
    stat_b[r, 3:4, :] = cot_sum[:, CHANS:]
    stat_b[r, 4:8, :] = jnp.zeros((4, CHANS), F32)
    spread(stat_b, sb_s, sb_r)

    @pl.when(r < last)
    def _():
        mix_down.start()

    sub = lax.broadcasted_iota(jnp.int32, (CHANS, CHANS), 0) % 8

    def down_grad(kh):
        part = tn(own_cot, m4[kh])
        for kw in range(3):
            tap = 3 * kh + kw
            tiles = part[:, kw * CHANS : (kw + 1) * CHANS].reshape(16, 2, 8, CHANS)
            one = tiles[:, 0].reshape(CHANS, CHANS)
            two = tiles[:, 1].reshape(CHANS, CHANS)
            low = jnp.where(sub < 4, one, pltpu.roll(two, 4, 0))
            high = jnp.where(sub < 4, pltpu.roll(one, CHANS - 4, 0), two)
            if tap >= 3:
                early[0, tap - 3] = low
                early[1, tap - 3] = high
            else:
                late[1, 4 + tap] = low
                late[0, 5 + tap] = high

    def taps(kh):
        return dw[kh].reshape(3 * CHANS, OUTS)

    for a in range(2):
        m4[a + 1, :, :CHANS] = shifted(m4[a + 1, :, 2 * CHANS :].astype(F32), -1).astype(BF)

    down_grad(1)
    down_grad(2)
    cs[...] = early[1 - core].astype(BF)
    pair_one = remote(cs, cr, c_s.at[0], c_r.at[0], rows=mate)
    pair_two = remote(cs2, cr2, c_s.at[1], c_r.at[1], rows=mate)
    pair_one.start()
    out = nn(m4[1], taps(1)) + nn(m4[2], taps(2)) + db[...]
    hold[...] = out

    slot_peers = [
        lax.rem(x_at + dx, 4) * 2 + (y_at if dy == 0 else 1 - y_at)
        for dx, dy in ((2, 1), (2, 0), (1, 1), (3, 1), (1, 0), (3, 0), (0, 1))
    ]

    def early_send(to):
        return remote(rs.at[lax.min(to, EARLY - 1)], rr.at[slot], r_s.at[to], r_r, rows=2 * to + core)

    def late_send(to):
        return remote(rs2.at[to], rr2.at[slot], q_s.at[to], q_r, rows=2 * to + core)

    pair_one.wait()
    both = early[core] + cr[...].astype(F32)
    early[core] = both
    rs[...] = both.astype(BF)
    for to in slot_peers:

        @pl.when(to < EARLY)
        def _():
            early_send(to).start()

    @pl.when(r > 0)
    def _():
        mix_down.wait_recv()
        m4[0, :, :CHANS] = shifted(m4[0, :, 2 * CHANS :].astype(F32), -1).astype(BF)

    down_grad(0)
    block_out[0, 0] = (hold[...] + nn(m4[0], taps(0))).astype(BF)

    whole(stat_b, sb_s, sb_r).wait_recv()
    totals = jnp.sum(stat_b[...], axis=0)
    tot_gp = totals[0:1]
    tot_gpn = totals[1:2]
    means = group_sum(
        jnp.broadcast_to(gain_ref[...], (8, CHANS)) * totals
    ) / n_total
    m1, m2 = means[0:1], means[1:2]
    m1w, m2w = twice(m1), twice(m2)
    for a in range(2):
        grad = (rstd2 * (gpre[a] * gain2 - m1w - hid[a] * m2w)).astype(BF)
        g4[a + 1, :, CHANS : 3 * CHANS] = grad

    n_channel = float(2 * cols * rows_n)
    tot_normed = (channel_sum - n_channel * mean) * rstd
    tot_bias = rstd * (gain_ref[...] * tot_gp - n_channel * m1 - m2 * tot_normed)
    mine[...] = jnp.zeros(mine.shape, F32)
    for k in (0, 4):
        mine[0, k : k + 1, :] = tot_bias
        mine[0, k + 1 : k + 2, :] = tot_gpn
        mine[0, k + 2 : k + 3, :] = tot_gp
        mine[1, k : k + 1, :] = totals[2:3]
        mine[1, k + 1 : k + 2, :] = totals[3:4]

    for kh in range(3):
        part = tn(g4[1, :, CHANS : 3 * CHANS], x4[kh]) + tn(
            g4[2, :, CHANS : 3 * CHANS], x4[kh + 1]
        )
        for kw in range(3):
            tap = 3 * kh + kw
            late[tap % 2, tap // 2] = (
                part[:CHANS, kw * CHANS : (kw + 1) * CHANS]
                + part[CHANS:, (kw + 1) * CHANS : (kw + 2) * CHANS]
            )
    late[1, 7] = jnp.zeros((CHANS, CHANS), F32)
    cs2[...] = late[1 - core].astype(BF)
    pair_two.start()

    def sides(f):
        grad = g4[f, :, CHANS : 3 * CHANS].astype(F32)
        g4[f, :, :CHANS] = shifted(grad[:, CHANS:], -1).astype(BF)
        g4[f, :, 3 * CHANS :] = shifted(grad[:, :CHANS], 1).astype(BF)

    pair_two.wait()
    both = late[core] + cr2[...].astype(F32)
    late[core] = both
    rs2[...] = both.astype(BF)
    for to in slot_peers:
        late_send(to).start()

    @pl.when(r < last)
    def _():
        g_down.start()

    @pl.when(r > 0)
    def _():
        g_up.start()

    sides(1)
    sides(2)
    gmix[0] += nt(g4[1], wb[1]) + nt(g4[2], wb[0])
    gmix[1] += nt(g4[1], wb[2]) + nt(g4[2], wb[1])

    others = pl.ds(0, slots - 1)

    @pl.when(slot < EARLY)
    def _():
        remote(rr.at[others], rr.at[others], r_s.at[slot], r_r, rows=mate).wait_recv()
        total = early[core, lax.min(slot, EARLY - 1)]
        for other in slot_peers:
            total = total + rr[other].astype(F32)
        red1[...] = total

    @pl.when(slot >= EARLY)
    def _():
        red1[...] = jnp.broadcast_to(mine[core][None], (16, 8, CHANS)).reshape(CHANS, CHANS)

    remote(rr2.at[others], rr2.at[others], q_s.at[slot], q_r, rows=mate).wait_recv()
    total = late[core, slot]
    for other in slot_peers:
        total = total + rr2[other].astype(F32)
    red2[...] = total

    one, two = red1[...], red2[...]
    red[:CHANS] = jnp.where(sub < 4, one, pltpu.roll(two, 4, 0))
    red[CHANS:] = jnp.where(sub < 4, pltpu.roll(one, CHANS - 4, 0), two)

    def place(e):
        row = lax.rem(e, 2) * 16 + lax.div(e, 2)
        return pl.ds(pl.multiple_of(row * 8, 8), 8)

    for to in dp_peers:
        remote(red.at[place(to)], dr.at[d], d_s, d_r, dp=to).start()
    dr[d] = red[place(d), :]

    def put_row(a):
        tall[pl.ds(8, half, stride=2), :] = gmix[a, :, :CHANS]
        tall[pl.ds(9, half, stride=2), :] = gmix[a, :, CHANS:]
        gimg_out[0, a] = tall[8 : cols + 8, :].astype(BF)

    @pl.when(r > 0)
    def _():
        g_down.wait_recv()
        sides(0)

    gmix[0] += nt(g4[0], wb[2])
    put_row(0)

    @pl.when(r < last)
    def _():
        g_up.wait_recv()
        sides(3)

    gmix[1] += nt(g4[3], wb[0])
    put_row(1)

    if dp_n > 1:
        part = dr.at[pl.ds(0, dp_n - 1)]
        dp_round = remote(part, part, d_s, d_r, rows=mate)
        dp_round.wait_recv()
    gout[r] = jnp.sum(dr[...], axis=0)
    spread(gout, o_s, o_r)
    whole(gout, o_s, o_r).wait()

    @pl.when(r < last)
    def _():
        img_down.wait_send()
        mix_down.wait_send()
        g_down.wait_send()

    @pl.when(r > 0)
    def _():
        img_up.wait_send()
        cot_up.wait_send()
        g_up.wait_send()

    whole(stat_a, sa_s, sa_r).wait_send()
    whole(stat_b, sb_s, sb_r).wait_send()
    if dp_n > 1:
        dp_round.wait_send()
    for to in slot_peers:
        late_send(to).wait_send()

        @pl.when(to < EARLY)
        def _():
            early_send(to).wait_send()


def finish(
    block, gimg, table, block_out, gimg_out, conv_out, bias_out, gain_out, shift_out, down_out, db_out,
    conv_v, down_v, bias_v, gain_v, shift_v, db_v, sems,
):
    copies = [
        pltpu.make_async_copy(src, dst, sems.at[k])
        for k, (src, dst) in enumerate(
            (
                (block, block_out),
                (gimg, gimg_out),
                (conv_v, conv_out),
                (down_v, down_out),
                (bias_v, bias_out),
                (gain_v, gain_out),
                (shift_v, shift_out),
                (db_v, db_out),
            )
        )
    ]
    copies[0].start()
    copies[1].start()
    for tap in range(TAPS):
        conv_v[tap] = table[tap, 4:8]
        if tap < 3:
            down_v[tap, 0:4] = table[9 + 2 * tap, 4:8]
            down_v[tap, 4:8] = table[10 + 2 * tap, 4:8]
        else:
            down_v[tap, 0:4] = table[2 * tap - 6, 0:4]
            down_v[tap, 4:8] = table[2 * tap - 5, 0:4]
    d = lax.axis_index("dp")
    narrow = pltpu.roll(table[12], lax.rem(CHANS - 4 * d, CHANS), 1)
    bias_v[...] = narrow[0:1, :4]
    gain_v[...] = narrow[1:2, :4]
    shift_v[...] = narrow[2:3, :4]
    wide = pltpu.roll(table[13], lax.rem(2 * CHANS - 8 * d, CHANS), 1)
    db_v[...] = jnp.where(d < 16, wide[0:1, :8], wide[1:2, :8])
    for copy in copies[2:]:
        copy.start()
    for copy in copies:
        copy.wait()


def shards(
    images, conv_weight, conv_bias, norm_gain, norm_shift, down_weight, down_bias, cotangent
):
    rows_n = lax.axis_size("rows")
    dp_n = lax.axis_size("dp")
    _, local_rows, cols, chans = images.shape
    half = cols // 2
    vmem = pl.BlockSpec(memory_space=pltpu.VMEM)
    dma = pltpu.SemaphoreType.DMA
    anywhere = pl.BlockSpec(memory_space=pltpu.HBM)
    unit = (CHANS, CHANS)
    slots = rows_n // 2
    scratch = [
        pltpu.VMEM((local_rows, cols, chans), BF),
        pltpu.VMEM(conv_weight.shape, BF),
        pltpu.VMEM((1, CHANS), F32),
        pltpu.VMEM((1, CHANS), F32),
        pltpu.VMEM((1, CHANS), F32),
        pltpu.VMEM(down_weight.shape, BF),
        pltpu.VMEM((1, OUTS), F32),
        pltpu.VMEM((half, OUTS), BF),
        pltpu.VMEM((half + 16, OUTS), F32),
        pltpu.VMEM((cols + 16, CHANS), F32),
        pltpu.VMEM((2, cols, CHANS), BF),
        pltpu.VMEM((half, OUTS), BF),
        pltpu.VMEM((4, half, 4 * CHANS), BF),
        pltpu.VMEM((3, half, 3 * CHANS), BF),
        pltpu.VMEM((4, half, 4 * CHANS), BF),
        pltpu.VMEM((3, 4 * CHANS, 2 * CHANS), BF),
        pltpu.VMEM((3, 2 * CHANS, 4 * CHANS), BF),
        pltpu.VMEM((2, half, 2 * CHANS), F32),
        pltpu.VMEM((2, half, 2 * CHANS), F32),
        pltpu.VMEM((2, half, 2 * CHANS), F32),
        pltpu.VMEM((half, OUTS), F32),
        pltpu.VMEM((rows_n, 8, CHANS), F32),
        pltpu.VMEM((rows_n, 8, CHANS), F32),
        pltpu.VMEM((2, 8, CHANS), F32),
        pltpu.VMEM((2, EARLY) + unit, F32),
        pltpu.VMEM((2, slots) + unit, F32),
        pltpu.VMEM((EARLY,) + unit, BF),
        pltpu.VMEM((EARLY,) + unit, BF),
        pltpu.VMEM((slots,) + unit, BF),
        pltpu.VMEM((slots,) + unit, BF),
        pltpu.VMEM((EARLY,) + unit, BF),
        pltpu.VMEM((slots,) + unit, BF),
        pltpu.VMEM((slots,) + unit, BF),
        pltpu.VMEM((slots,) + unit, BF),
        pltpu.VMEM(unit, F32),
        pltpu.VMEM(unit, F32),
        pltpu.VMEM((OUTS, CHANS), F32),
        pltpu.VMEM((dp_n, 8, CHANS), F32),
        dma((8,)),
        dma((2,)),
        dma((2,)),
        dma,
        dma,
        dma,
        dma,
        dma((2,)),
        dma((2,)),
        dma,
        dma,
        dma,
        dma,
        dma((2,)),
        dma((2,)),
        dma((slots,)),
        dma,
        dma((slots,)),
        dma,
        dma,
        dma,
        dma,
        dma,
    ]

    def body(*refs):
        kernel(rows_n, dp_n, *refs)

    block, grad_image, table = pl.pallas_call(
        body,
        out_shape=(
            jax.ShapeDtypeStruct((1, 1, half, OUTS), BF),
            jax.ShapeDtypeStruct((1, local_rows, cols, chans), BF),
            jax.ShapeDtypeStruct((rows_n, 8, CHANS), F32),
        ),
        in_specs=[anywhere] * 8,
        out_specs=(vmem, vmem, vmem),
        scratch_shapes=scratch,
        compiler_params=pltpu.CompilerParams(
            collective_id=0, has_side_effects=True, vmem_limit_bytes=40 * 1024 * 1024
        ),
        name="step",
    )(*(pltpu.with_memory_space_constraint(x, pltpu.HBM) for x in (
        images,
        conv_weight,
        conv_bias.reshape(1, CHANS),
        norm_gain.reshape(1, CHANS),
        norm_shift.reshape(1, CHANS),
        down_weight,
        down_bias.reshape(1, OUTS),
        cotangent.reshape(1, half, OUTS),
    )))
    shape = jax.ShapeDtypeStruct
    outs = pl.pallas_call(
        finish,
        out_shape=(
            shape(block.shape, BF),
            shape(grad_image.shape, BF),
            shape((TAPS, 4, CHANS), F32),
            shape((1, 4), F32),
            shape((1, 4), F32),
            shape((1, 4), F32),
            shape((TAPS, 8, CHANS), F32),
            shape((1, 8), F32),
        ),
        in_specs=[vmem, vmem, vmem],
        out_specs=[anywhere] * 8,
        scratch_shapes=[
            pltpu.VMEM((TAPS, 4, CHANS), F32),
            pltpu.VMEM((TAPS, 8, CHANS), F32),
            pltpu.VMEM((1, 4), F32),
            pltpu.VMEM((1, 4), F32),
            pltpu.VMEM((1, 4), F32),
            pltpu.VMEM((1, 8), F32),
            dma((8,)),
        ],
        compiler_params=pltpu.CompilerParams(vmem_limit_bytes=4 * 1024 * 1024),
        name="finish",
    )(block, grad_image, table)
    block, grad_image, conv_t, bias, gain, shift, down_t, down_bias_grad = outs
    return (
        block,
        grad_image,
        jnp.swapaxes(conv_t, 1, 2).reshape(3, 3, CHANS, 4),
        bias.reshape(4),
        gain.reshape(4),
        shift.reshape(4),
        jnp.swapaxes(down_t, 1, 2).reshape(3, 3, CHANS, 8),
        down_bias_grad.reshape(8),
    )


def solution(mesh):
    spread = P("dp", "rows", None, None)
    in_specs = (spread, P(), P(), P(), P(), P(), P(), spread)
    out_specs = (
        spread,
        spread,
        P(None, None, None, "dp"),
        P("dp"),
        P("dp"),
        P("dp"),
        P(None, None, None, "dp"),
        P("dp"),
    )
    return jax.shard_map(shards, mesh=mesh, in_specs=in_specs, out_specs=out_specs, check_vma=False)
```

```python
import jax
import jax.numpy as jnp
from jax import lax
from jax.experimental import pallas as pl
from jax.experimental.pallas import tpu as pltpu
from jax.sharding import PartitionSpec as P

GROUPS = 32
CHANS = 128
OUTS = 256
BF = jnp.bfloat16
F32 = jnp.float32
MESH = pl.DeviceIdType.MESH
EPS = 1e-05
TAPS = 9
EARLY = 6
FIRST = 5


def nn(a, b):
    return lax.dot_general(a, b, (((1,), (0,)), ((), ())), preferred_element_type=F32)


def nt(a, b):
    return lax.dot_general(a, b, (((1,), (1,)), ((), ())), preferred_element_type=F32)


def tn(a, b):
    return lax.dot_general(a, b, (((0,), (0,)), ((), ())), preferred_element_type=F32)


def group_sum(x):
    lane = lax.broadcasted_iota(jnp.int32, x.shape, 1)
    x = x + jnp.where(lane % 2 == 0, pltpu.roll(x, CHANS - 1, 1), pltpu.roll(x, 1, 1))
    return x + jnp.where(lane % 4 < 2, pltpu.roll(x, CHANS - 2, 1), pltpu.roll(x, 2, 1))


def twice(x):
    return jnp.concatenate([x, x], axis=1)


def fold(x):
    return x[:, :CHANS] + x[:, CHANS:]


def kernel(
    rows_n,
    dp_n,
    img_hbm,
    cw_hbm,
    cb_hbm,
    gain_hbm,
    shift_hbm,
    dw_hbm,
    db_hbm,
    cot_hbm,
    block_out,
    gimg_out,
    gout,
    img,
    cw,
    cb,
    gain_ref,
    shift_ref,
    dw,
    db,
    cot,
    wide,
    tall,
    edge_img,
    edge_cot,
    x4,
    m4,
    g4,
    wf,
    wb,
    hid,
    gpre,
    gmix,
    hold,
    stat_a,
    stat_b,
    mine,
    early,
    late,
    cs,
    cr,
    cs2,
    cr2,
    rs,
    rr,
    rs2,
    rr2,
    red1,
    red2,
    red,
    dr,
    load_sem,
    img_s,
    img_r,
    cot_s,
    cot_r,
    mix_s,
    mix_r,
    g_s,
    g_r,
    sa_s,
    sa_r,
    sb_s,
    sb_r,
    c_s,
    c_r,
    r_s,
    r_r,
    q_s,
    q_r,
    d_s,
    d_r,
    o_s,
    o_r,
    mates_in,
    dp_in,
):
    r = lax.axis_index("rows")
    d = lax.axis_index("dp")
    core = lax.rem(r, 2)
    slot = lax.div(r, 2)
    mate = r + 1 - 2 * core
    half = cot.shape[0]
    cols = 2 * half
    n_local = float(2 * cols * (CHANS // GROUPS))
    n_total = n_local * rows_n
    last = rows_n - 1
    slots = rows_n // 2

    def remote(src, dst, send, recv, **where):
        return pltpu.make_async_remote_copy(
            src_ref=src,
            dst_ref=dst,
            send_sem=send,
            recv_sem=recv,
            device_id=where,
            device_id_type=MESH,
        )

    loads = [
        pltpu.make_async_copy(src, dst, load_sem.at[k])
        for k, (src, dst) in enumerate(
            (
                (img_hbm.at[0], img),
                (cw_hbm, cw),
                (cot_hbm.at[0], cot),
                (dw_hbm, dw),
                (cb_hbm, cb),
                (gain_hbm, gain_ref),
                (shift_hbm, shift_ref),
                (db_hbm, db),
            )
        )
    ]
    x_at, y_at = lax.div(r, 4), lax.rem(slot, 2)
    hops = sorted(
        ((min(dx, 4 - dx) + dy, dc, dx, dy) for dx in range(4) for dy in range(2) for dc in range(2)),
        reverse=True,
    )
    row_peers = [
        lax.rem(x_at + dx, 4) * 4
        + (y_at if dy == 0 else 1 - y_at) * 2
        + (core if dc == 0 else 1 - core)
        for _, dc, dx, dy in hops[:-1]
    ]
    if dp_n == 32:
        z_at, h_at = lax.div(d, 4), lax.rem(d, 4)
        hops = sorted(
            ((min(dz, 8 - dz) + 2 * min(dh, 4 - dh), dz, dh) for dz in range(8) for dh in range(4)),
            reverse=True,
        )
        dp_peers = [
            lax.rem(z_at + dz, 8) * 4 + lax.rem(h_at + dh, 4) for _, dz, dh in hops[:-1]
        ]
    else:
        dp_peers = [lax.rem(d + i, dp_n) for i in range(1, dp_n)]

    barrier = pltpu.get_barrier_semaphore()
    slot_peers = [
        lax.rem(x_at + dx, 4) * 2 + (y_at if dy == 0 else 1 - y_at)
        for dx, dy in ((2, 1), (2, 0), (1, 1), (3, 1), (1, 0), (3, 0), (0, 1))
    ]
    if dp_n == 32:
        z_peers = [lax.rem(z_at + dz, 8) * 4 + h_at for dz in (4, 3, 5, 2, 6, 1, 7)]
        h_peers = [z_at * 4 + lax.rem(h_at + dh, 4) for dh in (2, 1, 3)]
    else:
        z_peers, h_peers = dp_peers, []
    up = lax.max(r - 1, 0)
    down = lax.min(r + 1, last)

    def greet(sem, **where):
        pl.semaphore_signal(sem, inc=1, device_id=where, device_id_type=MESH)

    for to in z_peers + h_peers:
        greet(barrier, dp=to)
    for to in slot_peers:
        greet(barrier, rows=2 * to + core)
    greet(barrier, rows=mate)
    far = r - 1 + 2 * core
    far_is = (far >= 0) & (far <= last)

    @pl.when(far_is)
    def _():
        greet(barrier, rows=lax.min(lax.max(far, 0), last))

    for load in loads:
        load.start()

    pl.semaphore_wait(barrier, slots + len(z_peers) + len(h_peers) + jnp.where(far_is, 1, 0))
    mid = pl.ds(CHANS, 2 * CHANS)
    img_down = remote(img_hbm.at[0, 1], edge_img.at[0], img_s.at[0], img_r.at[0], rows=down)
    img_up = remote(img_hbm.at[0, 0], edge_img.at[1], img_s.at[1], img_r.at[1], rows=up)
    cot_up = remote(cot_hbm.at[0], edge_cot, cot_s, cot_r, rows=up)
    mix_down = remote(m4.at[2, :, mid], m4.at[0, :, mid], mix_s, mix_r, rows=down)
    g_down = remote(g4.at[2, :, mid], g4.at[0, :, mid], g_s.at[0], g_r.at[0], rows=down)
    g_up = remote(g4.at[1, :, mid], g4.at[3, :, mid], g_s.at[1], g_r.at[1], rows=up)

    @pl.when(r < last)
    def _():
        img_down.start()

    @pl.when(r > 0)
    def _():
        img_up.start()
        cot_up.start()

    for to in slot_peers:
        greet(mates_in, rows=2 * to + core)
    if h_peers:
        for to in z_peers:
            greet(dp_in, dp=to)

    loads[1].wait()
    zero_block = jnp.zeros((CHANS, CHANS), BF)
    for kh in range(3):
        for kw in range(3):
            tap = cw[kh, kw]
            wf[kh, kw * CHANS : (kw + 1) * CHANS, :CHANS] = tap
            wf[kh, (kw + 1) * CHANS : (kw + 2) * CHANS, CHANS:] = tap
            wb[kh, :CHANS, (2 - kw) * CHANS : (3 - kw) * CHANS] = tap
            wb[kh, CHANS:, (3 - kw) * CHANS : (4 - kw) * CHANS] = tap
        wf[kh, 3 * CHANS :, :CHANS] = zero_block
        wf[kh, :CHANS, CHANS:] = zero_block
        wb[kh, :CHANS, 3 * CHANS :] = zero_block
        wb[kh, CHANS:, :CHANS] = zero_block

    tall[:8, :] = jnp.zeros((8, CHANS), F32)
    tall[cols + 8 :, :] = jnp.zeros((8, CHANS), F32)
    wide[:8, :] = jnp.zeros((8, OUTS), F32)
    wide[half + 8 :, :] = jnp.zeros((8, OUTS), F32)

    def split_columns(row, f):
        tall[8 : cols + 8, :] = row.astype(F32)
        for k, start in enumerate((7, 8, 9, 10)):
            x4[f, :, k * CHANS : (k + 1) * CHANS] = tall[pl.ds(start, half, stride=2), :].astype(BF)

    def shifted(x, by):
        width = x.shape[1]
        wide[8 : half + 8, :width] = x
        return wide[8 + by : half + 8 + by, :width]

    @pl.when(r == 0)
    def _():
        edge_img[0] = jnp.zeros(edge_img.shape[1:], BF)
        m4[0] = jnp.zeros(m4.shape[1:], BF)
        g4[0] = jnp.zeros(g4.shape[1:], BF)

    @pl.when(r == last)
    def _():
        edge_img[1] = jnp.zeros(edge_img.shape[1:], BF)
        edge_cot[...] = jnp.zeros(edge_cot.shape, BF)
        g4[3] = jnp.zeros(g4.shape[1:], BF)

    for k in (0, 2, 3, 4, 5, 6, 7):
        loads[k].wait()
    for a in range(2):
        split_columns(img[a], a + 1)

    bias = twice(cb[...])
    hid[0] = nn(x4[1], wf[1]) + nn(x4[2], wf[2]) + bias
    hid[1] = nn(x4[1], wf[0]) + nn(x4[2], wf[1]) + bias

    @pl.when(r > 0)
    def _():
        img_down.wait_recv()

    split_columns(edge_img[0], 0)
    hid[0] += nn(x4[0], wf[0])

    @pl.when(r < last)
    def _():
        img_up.wait_recv()

    split_columns(edge_img[1], 3)
    hid[1] += nn(x4[3], wf[2])

    def spread(table, send, recv):
        for to in row_peers:
            remote(table.at[r], table.at[r], send, recv, rows=to).start()

    def whole(table, send, recv):
        part = table.at[pl.ds(0, rows_n - 1)]
        return remote(part, part, send, recv, rows=mate)

    def colsum(x):
        return jnp.sum(x, axis=0, keepdims=True)

    own_sum = fold(colsum(hid[0]) + colsum(hid[1]))
    own_mean = twice(group_sum(jnp.broadcast_to(own_sum, (8, CHANS)))[:1] / n_local)
    off0 = hid[0] - own_mean
    off1 = hid[1] - own_mean
    own_sq = fold(colsum(off0 * off0) + colsum(off1 * off1))
    stat_a[r, 0:1, :] = own_sum
    stat_a[r, 1:2, :] = own_sq
    stat_a[r, 2:8, :] = jnp.zeros((6, CHANS), F32)
    pl.semaphore_wait(mates_in, slots - 1)
    spread(stat_a, sa_s, sa_r)

    @pl.when(r < last)
    def _():
        cot_up.wait_recv()

    def pull(grad, lead, kh):
        both = dw[kh, 1:3].reshape(2 * CHANS, OUTS)
        return nt(grad, both), nt(lead, dw[kh, 0])

    own_cot = cot[...]
    own_cot32 = own_cot.astype(F32)
    cot_sum = colsum(own_cot32)
    lead_cot = shifted(own_cot32, 1).astype(BF)
    full, odd = pull(own_cot, lead_cot, 1)
    gmix[0] = full
    gmix[0, :, CHANS:] += odd
    full, odd = pull(own_cot, lead_cot, 2)
    gmix[1] = full
    gmix[1, :, CHANS:] += odd
    below = edge_cot[...]
    full, odd = pull(below, shifted(below.astype(F32), 1).astype(BF), 0)
    gmix[1] += full
    gmix[1, :, CHANS:] += odd

    whole(stat_a, sa_s, sa_r).wait_recv()
    table = stat_a[...]
    groups = group_sum(table.reshape(rows_n * 8, CHANS)).reshape(rows_n, 8, CHANS)
    group_tot = jnp.sum(groups, axis=0)
    mean = group_tot[0:1] / n_total
    dev = groups / n_local - mean.reshape(1, 1, CHANS)
    spread_sq = jnp.sum(dev * dev, axis=0)[0:1] * n_local
    rstd = lax.rsqrt((group_tot[1:2] + spread_sq) / n_total + EPS)
    channel_sum = jnp.sum(table, axis=0)[0:1]
    mean2, rstd2 = twice(mean), twice(rstd)
    gain2, shift2 = twice(gain_ref[...]), twice(shift_ref[...])

    sum_gp = jnp.zeros((1, 2 * CHANS), F32)
    sum_gpn = jnp.zeros((1, 2 * CHANS), F32)
    for a in (1, 0):
        normed = (hid[a] - mean2) * rstd2
        pre = normed * gain2 + shift2
        sig = jax.nn.sigmoid(pre)
        mixed = (x4[a + 1, :, CHANS : 3 * CHANS].astype(F32) + pre * sig).astype(BF)
        m4[a + 1, :, CHANS:] = mixed
        gp = gmix[a] * sig * (1.0 + pre * (1.0 - sig))
        hid[a] = normed
        gpre[a] = gp
        sum_gp += colsum(gp)
        sum_gpn += colsum(gp * normed)

    stat_b[r, 0:1, :] = fold(sum_gp)
    stat_b[r, 1:2, :] = fold(sum_gpn)
    stat_b[r, 2:3, :] = cot_sum[:, :CHANS]
    stat_b[r, 3:4, :] = cot_sum[:, CHANS:]
    stat_b[r, 4:8, :] = jnp.zeros((4, CHANS), F32)
    spread(stat_b, sb_s, sb_r)

    @pl.when(r < last)
    def _():
        mix_down.start()

    sub = lax.broadcasted_iota(jnp.int32, (CHANS, CHANS), 0) % 8

    def down_grad(kh):
        part = tn(own_cot, m4[kh])
        for kw in range(3):
            tap = 3 * kh + kw
            tiles = part[:, kw * CHANS : (kw + 1) * CHANS].reshape(16, 2, 8, CHANS)
            one = tiles[:, 0].reshape(CHANS, CHANS)
            two = tiles[:, 1].reshape(CHANS, CHANS)
            low = jnp.where(sub < 4, one, pltpu.roll(two, 4, 0))
            high = jnp.where(sub < 4, pltpu.roll(one, CHANS - 4, 0), two)
            if tap >= 3:
                early[0, tap - 3] = low
                early[1, tap - 3] = high
            else:
                late[0, 4 + tap] = low
                late[1, 5 + tap] = high

    def taps(kh):
        return dw[kh].reshape(3 * CHANS, OUTS)

    for a in range(2):
        m4[a + 1, :, :CHANS] = shifted(m4[a + 1, :, 2 * CHANS :].astype(F32), -1).astype(BF)

    down_grad(1)
    down_grad(2)
    cs[...] = early[1 - core].astype(BF)
    pair_one = remote(cs, cr, c_s.at[0], c_r.at[0], rows=mate)
    pair_two = remote(cs2.at[0:FIRST], cr2.at[0:FIRST], c_s.at[1], c_r.at[1], rows=mate)
    pair_rest = remote(cs2.at[FIRST:], cr2.at[FIRST:], c_s.at[2], c_r.at[2], rows=mate)
    pair_one.start()
    out = nn(m4[1], taps(1)) + nn(m4[2], taps(2)) + db[...]
    hold[...] = out

    def early_send(to):
        return remote(rs.at[lax.min(to, EARLY - 1)], rr.at[slot], r_s.at[to], r_r, rows=2 * to + core)

    def late_send(to):
        return remote(rs2.at[number(to)], rr2.at[slot], q_s.at[to], q_r, rows=2 * to + core)

    def number(at):
        return lax.div(at, 2) + 4 * lax.rem(at + core, 2)

    def late_sum(low, high):
        both = late[core, low:high] + cr2[low:high].astype(F32)
        late[core, low:high] = both
        rs2[low:high] = both.astype(BF)
        for to in slot_peers:

            @pl.when((number(to) >= low) & (number(to) < high))
            def _():
                late_send(to).start()

    pair_one.wait()
    both = early[core] + cr[...].astype(F32)
    early[core] = both
    rs[...] = both.astype(BF)
    for to in slot_peers:

        @pl.when(to < EARLY)
        def _():
            early_send(to).start()

    @pl.when(r > 0)
    def _():
        mix_down.wait_recv()
        m4[0, :, :CHANS] = shifted(m4[0, :, 2 * CHANS :].astype(F32), -1).astype(BF)

    down_grad(0)
    late[0, 7] = jnp.zeros((CHANS, CHANS), F32)
    cs2[FIRST:] = late[1 - core, FIRST:].astype(BF)
    pair_rest.start()
    block_out[0, 0] = (hold[...] + nn(m4[0], taps(0))).astype(BF)

    pair_rest.wait()
    late_sum(FIRST, slots)

    whole(stat_b, sb_s, sb_r).wait_recv()
    totals = jnp.sum(stat_b[...], axis=0)
    tot_gp = totals[0:1]
    tot_gpn = totals[1:2]
    means = group_sum(
        jnp.broadcast_to(gain_ref[...], (8, CHANS)) * totals
    ) / n_total
    m1, m2 = means[0:1], means[1:2]
    m1w, m2w = twice(m1), twice(m2)
    for a in range(2):
        grad = (rstd2 * (gpre[a] * gain2 - m1w - hid[a] * m2w)).astype(BF)
        g4[a + 1, :, CHANS : 3 * CHANS] = grad

    n_channel = float(2 * cols * rows_n)
    tot_normed = (channel_sum - n_channel * mean) * rstd
    tot_bias = rstd * (gain_ref[...] * tot_gp - n_channel * m1 - m2 * tot_normed)
    mine[...] = jnp.zeros(mine.shape, F32)
    for k in (0, 4):
        mine[0, k : k + 1, :] = tot_bias
        mine[0, k + 1 : k + 2, :] = tot_gpn
        mine[0, k + 2 : k + 3, :] = tot_gp
        mine[1, k : k + 1, :] = totals[2:3]
        mine[1, k + 1 : k + 2, :] = totals[3:4]

    for kh in range(3):
        part = tn(g4[1, :, CHANS : 3 * CHANS], x4[kh]) + tn(
            g4[2, :, CHANS : 3 * CHANS], x4[kh + 1]
        )
        for kw in range(3):
            tap = 3 * kh + kw
            late[tap % 2 if tap < 8 else 1, tap // 2] = (
                part[:CHANS, kw * CHANS : (kw + 1) * CHANS]
                + part[CHANS:, (kw + 1) * CHANS : (kw + 2) * CHANS]
            )
    cs2[:FIRST] = late[1 - core, :FIRST].astype(BF)
    pair_two.start()

    def sides(f):
        grad = g4[f, :, CHANS : 3 * CHANS].astype(F32)
        g4[f, :, :CHANS] = shifted(grad[:, CHANS:], -1).astype(BF)
        g4[f, :, 3 * CHANS :] = shifted(grad[:, :CHANS], 1).astype(BF)

    pair_two.wait()
    late_sum(0, FIRST)

    @pl.when(r < last)
    def _():
        g_down.start()

    @pl.when(r > 0)
    def _():
        g_up.start()

    sides(1)
    sides(2)
    gmix[0] += nt(g4[1], wb[1]) + nt(g4[2], wb[0])
    gmix[1] += nt(g4[1], wb[2]) + nt(g4[2], wb[1])

    others = pl.ds(0, slots - 1)

    @pl.when(slot < EARLY)
    def _():
        remote(rr.at[others], rr.at[others], r_s.at[slot], r_r, rows=mate).wait_recv()
        total = early[core, lax.min(slot, EARLY - 1)]
        for other in slot_peers:
            total = total + rr[other].astype(F32)
        red1[...] = total

    @pl.when(slot >= EARLY)
    def _():
        red1[...] = jnp.broadcast_to(mine[core][None], (16, 8, CHANS)).reshape(CHANS, CHANS)

    remote(rr2.at[others], rr2.at[others], q_s.at[slot], q_r, rows=mate).wait_recv()
    total = late[core, number(slot)]
    for other in slot_peers:
        total = total + rr2[other].astype(F32)
    red2[...] = total

    one, two = red1[...], red2[...]
    red[:CHANS] = jnp.where(sub < 4, one, pltpu.roll(two, 4, 0))
    red[CHANS:] = jnp.where(sub < 4, pltpu.roll(one, CHANS - 4, 0), two)

    def place(e):
        row = lax.rem(e, 2) * 16 + lax.div(e, 2)
        return pl.ds(pl.multiple_of(row * 8, 8), 8)

    if h_peers:
        pl.semaphore_wait(dp_in, len(z_peers))
    for to in dp_peers:
        remote(red.at[place(to)], dr.at[d], d_s, d_r, dp=to).start()
    dr[d] = red[place(d), :]

    def put_row(a):
        tall[pl.ds(8, half, stride=2), :] = gmix[a, :, :CHANS]
        tall[pl.ds(9, half, stride=2), :] = gmix[a, :, CHANS:]
        gimg_out[0, a] = tall[8 : cols + 8, :].astype(BF)

    @pl.when(r > 0)
    def _():
        g_down.wait_recv()
        sides(0)

    gmix[0] += nt(g4[0], wb[2])
    put_row(0)

    @pl.when(r < last)
    def _():
        g_up.wait_recv()
        sides(3)

    gmix[1] += nt(g4[3], wb[0])
    put_row(1)

    if dp_n > 1:
        part = dr.at[pl.ds(0, dp_n - 1)]
        dp_round = remote(part, part, d_s, d_r, rows=mate)
        dp_round.wait_recv()
    gout[r] = jnp.sum(dr[...], axis=0)
    spread(gout, o_s, o_r)
    whole(gout, o_s, o_r).wait()

    @pl.when(r < last)
    def _():
        img_down.wait_send()
        mix_down.wait_send()
        g_down.wait_send()

    @pl.when(r > 0)
    def _():
        img_up.wait_send()
        cot_up.wait_send()
        g_up.wait_send()

    whole(stat_a, sa_s, sa_r).wait_send()
    whole(stat_b, sb_s, sb_r).wait_send()
    if dp_n > 1:
        dp_round.wait_send()
    for to in slot_peers:
        late_send(to).wait_send()

        @pl.when(to < EARLY)
        def _():
            early_send(to).wait_send()


def finish(
    block, gimg, table, block_out, gimg_out, conv_out, bias_out, gain_out, shift_out, down_out, db_out,
    conv_v, down_v, bias_v, gain_v, shift_v, db_v, sems,
):
    copies = [
        pltpu.make_async_copy(src, dst, sems.at[k])
        for k, (src, dst) in enumerate(
            (
                (block, block_out),
                (gimg, gimg_out),
                (conv_v, conv_out),
                (down_v, down_out),
                (bias_v, bias_out),
                (gain_v, gain_out),
                (shift_v, shift_out),
                (db_v, db_out),
            )
        )
    ]
    copies[0].start()
    copies[1].start()
    for tap in range(TAPS):
        conv_v[tap] = table[2 * tap + tap % 2 if tap < 8 else 1, 4:8]
        if tap < 3:
            down_v[tap, 0:4] = table[2 + 4 * tap, 4:8]
            down_v[tap, 4:8] = table[5 + 4 * tap, 4:8]
        else:
            down_v[tap, 0:4] = table[2 * tap - 6, 0:4]
            down_v[tap, 4:8] = table[2 * tap - 5, 0:4]
    d = lax.axis_index("dp")
    narrow = pltpu.roll(table[12], lax.rem(CHANS - 4 * d, CHANS), 1)
    bias_v[...] = narrow[0:1, :4]
    gain_v[...] = narrow[1:2, :4]
    shift_v[...] = narrow[2:3, :4]
    wide = pltpu.roll(table[13], lax.rem(2 * CHANS - 8 * d, CHANS), 1)
    db_v[...] = jnp.where(d < 16, wide[0:1, :8], wide[1:2, :8])
    for copy in copies[2:]:
        copy.start()
    for copy in copies:
        copy.wait()


def shards(
    images, conv_weight, conv_bias, norm_gain, norm_shift, down_weight, down_bias, cotangent
):
    rows_n = lax.axis_size("rows")
    dp_n = lax.axis_size("dp")
    _, local_rows, cols, chans = images.shape
    half = cols // 2
    vmem = pl.BlockSpec(memory_space=pltpu.VMEM)
    dma = pltpu.SemaphoreType.DMA
    anywhere = pl.BlockSpec(memory_space=pltpu.HBM)
    unit = (CHANS, CHANS)
    slots = rows_n // 2
    scratch = [
        pltpu.VMEM((local_rows, cols, chans), BF),
        pltpu.VMEM(conv_weight.shape, BF),
        pltpu.VMEM((1, CHANS), F32),
        pltpu.VMEM((1, CHANS), F32),
        pltpu.VMEM((1, CHANS), F32),
        pltpu.VMEM(down_weight.shape, BF),
        pltpu.VMEM((1, OUTS), F32),
        pltpu.VMEM((half, OUTS), BF),
        pltpu.VMEM((half + 16, OUTS), F32),
        pltpu.VMEM((cols + 16, CHANS), F32),
        pltpu.VMEM((2, cols, CHANS), BF),
        pltpu.VMEM((half, OUTS), BF),
        pltpu.VMEM((4, half, 4 * CHANS), BF),
        pltpu.VMEM((3, half, 3 * CHANS), BF),
        pltpu.VMEM((4, half, 4 * CHANS), BF),
        pltpu.VMEM((3, 4 * CHANS, 2 * CHANS), BF),
        pltpu.VMEM((3, 2 * CHANS, 4 * CHANS), BF),
        pltpu.VMEM((2, half, 2 * CHANS), F32),
        pltpu.VMEM((2, half, 2 * CHANS), F32),
        pltpu.VMEM((2, half, 2 * CHANS), F32),
        pltpu.VMEM((half, OUTS), F32),
        pltpu.VMEM((rows_n, 8, CHANS), F32),
        pltpu.VMEM((rows_n, 8, CHANS), F32),
        pltpu.VMEM((2, 8, CHANS), F32),
        pltpu.VMEM((2, EARLY) + unit, F32),
        pltpu.VMEM((2, slots) + unit, F32),
        pltpu.VMEM((EARLY,) + unit, BF),
        pltpu.VMEM((EARLY,) + unit, BF),
        pltpu.VMEM((slots,) + unit, BF),
        pltpu.VMEM((slots,) + unit, BF),
        pltpu.VMEM((EARLY,) + unit, BF),
        pltpu.VMEM((slots,) + unit, BF),
        pltpu.VMEM((slots,) + unit, BF),
        pltpu.VMEM((slots,) + unit, BF),
        pltpu.VMEM(unit, F32),
        pltpu.VMEM(unit, F32),
        pltpu.VMEM((OUTS, CHANS), F32),
        pltpu.VMEM((dp_n, 8, CHANS), F32),
        dma((8,)),
        dma((2,)),
        dma((2,)),
        dma,
        dma,
        dma,
        dma,
        dma((2,)),
        dma((2,)),
        dma,
        dma,
        dma,
        dma,
        dma((3,)),
        dma((3,)),
        dma((slots,)),
        dma,
        dma((slots,)),
        dma,
        dma,
        dma,
        dma,
        dma,
        pltpu.SemaphoreType.REGULAR,
        pltpu.SemaphoreType.REGULAR,
    ]

    def body(*refs):
        kernel(rows_n, dp_n, *refs)

    block, grad_image, table = pl.pallas_call(
        body,
        out_shape=(
            jax.ShapeDtypeStruct((1, 1, half, OUTS), BF),
            jax.ShapeDtypeStruct((1, local_rows, cols, chans), BF),
            jax.ShapeDtypeStruct((rows_n, 8, CHANS), F32),
        ),
        in_specs=[anywhere] * 8,
        out_specs=(vmem, vmem, vmem),
        scratch_shapes=scratch,
        compiler_params=pltpu.CompilerParams(
            collective_id=0, has_side_effects=True, vmem_limit_bytes=40 * 1024 * 1024
        ),
        name="step",
    )(*(pltpu.with_memory_space_constraint(x, pltpu.HBM) for x in (
        images,
        conv_weight,
        conv_bias.reshape(1, CHANS),
        norm_gain.reshape(1, CHANS),
        norm_shift.reshape(1, CHANS),
        down_weight,
        down_bias.reshape(1, OUTS),
        cotangent.reshape(1, half, OUTS),
    )))
    shape = jax.ShapeDtypeStruct
    outs = pl.pallas_call(
        finish,
        out_shape=(
            shape(block.shape, BF),
            shape(grad_image.shape, BF),
            shape((TAPS, 4, CHANS), F32),
            shape((1, 4), F32),
            shape((1, 4), F32),
            shape((1, 4), F32),
            shape((TAPS, 8, CHANS), F32),
            shape((1, 8), F32),
        ),
        in_specs=[vmem, vmem, vmem],
        out_specs=[anywhere] * 8,
        scratch_shapes=[
            pltpu.VMEM((TAPS, 4, CHANS), F32),
            pltpu.VMEM((TAPS, 8, CHANS), F32),
            pltpu.VMEM((1, 4), F32),
            pltpu.VMEM((1, 4), F32),
            pltpu.VMEM((1, 4), F32),
            pltpu.VMEM((1, 8), F32),
            dma((8,)),
        ],
        compiler_params=pltpu.CompilerParams(vmem_limit_bytes=4 * 1024 * 1024),
        name="finish",
    )(block, grad_image, table)
    block, grad_image, conv_t, bias, gain, shift, down_t, down_bias_grad = outs
    return (
        block,
        grad_image,
        jnp.swapaxes(conv_t, 1, 2).reshape(3, 3, CHANS, 4),
        bias.reshape(4),
        gain.reshape(4),
        shift.reshape(4),
        jnp.swapaxes(down_t, 1, 2).reshape(3, 3, CHANS, 8),
        down_bias_grad.reshape(8),
    )


def solution(mesh):
    spread = P("dp", "rows", None, None)
    in_specs = (spread, P(), P(), P(), P(), P(), P(), spread)
    out_specs = (
        spread,
        spread,
        P(None, None, None, "dp"),
        P("dp"),
        P("dp"),
        P("dp"),
        P(None, None, None, "dp"),
        P("dp"),
    )
    return jax.shard_map(shards, mesh=mesh, in_specs=in_specs, out_specs=out_specs, check_vma=False)
```

```python
import jax
import jax.numpy as jnp
from jax import lax
from jax.experimental import pallas as pl
from jax.experimental.pallas import tpu as pltpu
from jax.sharding import PartitionSpec as P

GROUPS = 32
CHANS = 128
OUTS = 256
BF = jnp.bfloat16
F32 = jnp.float32
MESH = pl.DeviceIdType.MESH
EPS = 1e-05
TAPS = 9
EARLY = 6
FIRST = 5


def nn(a, b):
    return lax.dot_general(a, b, (((1,), (0,)), ((), ())), preferred_element_type=F32)


def nt(a, b):
    return lax.dot_general(a, b, (((1,), (1,)), ((), ())), preferred_element_type=F32)


def tn(a, b):
    return lax.dot_general(a, b, (((0,), (0,)), ((), ())), preferred_element_type=F32)


def group_sum(x):
    lane = lax.broadcasted_iota(jnp.int32, x.shape, 1)
    x = x + jnp.where(lane % 2 == 0, pltpu.roll(x, CHANS - 1, 1), pltpu.roll(x, 1, 1))
    return x + jnp.where(lane % 4 < 2, pltpu.roll(x, CHANS - 2, 1), pltpu.roll(x, 2, 1))


def twice(x):
    return jnp.concatenate([x, x], axis=1)


def fold(x):
    return x[:, :CHANS] + x[:, CHANS:]


def kernel(
    rows_n,
    dp_n,
    img_hbm,
    cw_hbm,
    cb_hbm,
    gain_hbm,
    shift_hbm,
    dw_hbm,
    db_hbm,
    cot_hbm,
    block_out,
    gimg_out,
    gout,
    img,
    cw,
    cb,
    gain_ref,
    shift_ref,
    dw,
    db,
    cot,
    wide,
    tall,
    edge_img,
    edge_cot,
    x4,
    m4,
    g4,
    wf,
    wb,
    hid,
    gpre,
    gmix,
    hold,
    stat_a,
    stat_b,
    mine,
    early,
    late,
    cs,
    cr,
    cs2,
    cr2,
    rs,
    rr,
    rs2,
    rr2,
    red1,
    red2,
    red,
    dr,
    load_sem,
    img_s,
    img_r,
    cot_s,
    cot_r,
    mix_s,
    mix_r,
    g_s,
    g_r,
    sa_s,
    sa_r,
    sb_s,
    sb_r,
    c_s,
    c_r,
    r_s,
    r_r,
    q_s,
    q_r,
    d_s,
    d_r,
    o_s,
    o_r,
    met,
):
    r = lax.axis_index("rows")
    d = lax.axis_index("dp")
    core = lax.rem(r, 2)
    slot = lax.div(r, 2)
    mate = r + 1 - 2 * core
    half = cot.shape[0]
    cols = 2 * half
    n_local = float(2 * cols * (CHANS // GROUPS))
    n_total = n_local * rows_n
    last = rows_n - 1
    slots = rows_n // 2

    def remote(src, dst, send, recv, **where):
        return pltpu.make_async_remote_copy(
            src_ref=src,
            dst_ref=dst,
            send_sem=send,
            recv_sem=recv,
            device_id=where,
            device_id_type=MESH,
        )

    loads = [
        pltpu.make_async_copy(src, dst, load_sem.at[k])
        for k, (src, dst) in enumerate(
            (
                (img_hbm.at[0], img),
                (cw_hbm, cw),
                (cot_hbm.at[0], cot),
                (dw_hbm, dw),
                (cb_hbm, cb),
                (gain_hbm, gain_ref),
                (shift_hbm, shift_ref),
                (db_hbm, db),
            )
        )
    ]
    x_at, y_at = lax.div(r, 4), lax.rem(slot, 2)
    hops = sorted(
        ((min(dx, 4 - dx) + dy, dc, dx, dy) for dx in range(4) for dy in range(2) for dc in range(2)),
        reverse=True,
    )
    row_peers = [
        lax.rem(x_at + dx, 4) * 4
        + (y_at if dy == 0 else 1 - y_at) * 2
        + (core if dc == 0 else 1 - core)
        for _, dc, dx, dy in hops[:-1]
    ]
    if dp_n == 32:
        z_at, h_at = lax.div(d, 4), lax.rem(d, 4)
        hops = sorted(
            ((min(dz, 8 - dz) + 2 * min(dh, 4 - dh), dz, dh) for dz in range(8) for dh in range(4)),
            reverse=True,
        )
        dp_peers = [
            lax.rem(z_at + dz, 8) * 4 + lax.rem(h_at + dh, 4) for _, dz, dh in hops[:-1]
        ]
    else:
        dp_peers = [lax.rem(d + i, dp_n) for i in range(1, dp_n)]

    barrier = pltpu.get_barrier_semaphore()
    slot_peers = [
        lax.rem(x_at + dx, 4) * 2 + (y_at if dy == 0 else 1 - y_at)
        for dx, dy in ((2, 1), (2, 0), (1, 1), (3, 1), (1, 0), (3, 0), (0, 1))
    ]
    if dp_n == 32:
        z_peers = [lax.rem(z_at + dz, 8) * 4 + h_at for dz in (4, 3, 5, 2, 6, 1, 7)]
        dp_near = z_peers[-2:] + [z_at * 4 + lax.rem(h_at + dh, 4) for dh in (1, 3)]
    else:
        z_peers, dp_near = [], dp_peers
    x_peers = [lax.rem(r + 4 * dx, rows_n) for dx in (2, 1, 3)]
    y_peer = r + 2 - 4 * y_at
    up = lax.max(r - 1, 0)
    down = lax.min(r + 1, last)

    def greet(sem, **where):
        pl.semaphore_signal(sem, inc=1, device_id=where, device_id_type=MESH)

    for to in dp_near:
        greet(barrier, dp=to)
    for to in x_peers[1:] + [y_peer]:
        greet(barrier, rows=to)
    greet(barrier, rows=mate)
    far = r - 1 + 2 * core
    far_is = (far >= 0) & (far <= last)

    @pl.when(far_is)
    def _():
        greet(barrier, rows=lax.min(lax.max(far, 0), last))

    for load in loads:
        load.start()

    pl.semaphore_wait(barrier, 4 + len(dp_near) + jnp.where(far_is, 1, 0))
    mid = pl.ds(CHANS, 2 * CHANS)
    img_down = remote(img_hbm.at[0, 1], edge_img.at[0], img_s.at[0], img_r.at[0], rows=down)
    img_up = remote(img_hbm.at[0, 0], edge_img.at[1], img_s.at[1], img_r.at[1], rows=up)
    cot_up = remote(cot_hbm.at[0], edge_cot, cot_s, cot_r, rows=up)
    mix_down = remote(m4.at[2, :, mid], m4.at[0, :, mid], mix_s, mix_r, rows=down)
    g_down = remote(g4.at[2, :, mid], g4.at[0, :, mid], g_s.at[0], g_r.at[0], rows=down)
    g_up = remote(g4.at[1, :, mid], g4.at[3, :, mid], g_s.at[1], g_r.at[1], rows=up)

    @pl.when(r < last)
    def _():
        img_down.start()

    @pl.when(r > 0)
    def _():
        img_up.start()
        cot_up.start()

    for to in x_peers[1:] + [y_peer]:
        greet(met.at[0], rows=to)
    if z_peers:
        for to in dp_near:
            greet(met.at[1], dp=to)

    loads[1].wait()
    zero_block = jnp.zeros((CHANS, CHANS), BF)
    for kh in range(3):
        for kw in range(3):
            tap = cw[kh, kw]
            wf[kh, kw * CHANS : (kw + 1) * CHANS, :CHANS] = tap
            wf[kh, (kw + 1) * CHANS : (kw + 2) * CHANS, CHANS:] = tap
            wb[kh, :CHANS, (2 - kw) * CHANS : (3 - kw) * CHANS] = tap
            wb[kh, CHANS:, (3 - kw) * CHANS : (4 - kw) * CHANS] = tap
        wf[kh, 3 * CHANS :, :CHANS] = zero_block
        wf[kh, :CHANS, CHANS:] = zero_block
        wb[kh, :CHANS, 3 * CHANS :] = zero_block
        wb[kh, CHANS:, :CHANS] = zero_block

    tall[:8, :] = jnp.zeros((8, CHANS), F32)
    tall[cols + 8 :, :] = jnp.zeros((8, CHANS), F32)
    wide[:8, :] = jnp.zeros((8, OUTS), F32)
    wide[half + 8 :, :] = jnp.zeros((8, OUTS), F32)

    def split_columns(row, f):
        tall[8 : cols + 8, :] = row.astype(F32)
        for k, start in enumerate((7, 8, 9, 10)):
            x4[f, :, k * CHANS : (k + 1) * CHANS] = tall[pl.ds(start, half, stride=2), :].astype(BF)

    def shifted(x, by):
        width = x.shape[1]
        wide[8 : half + 8, :width] = x
        return wide[8 + by : half + 8 + by, :width]

    @pl.when(r == 0)
    def _():
        edge_img[0] = jnp.zeros(edge_img.shape[1:], BF)
        m4[0] = jnp.zeros(m4.shape[1:], BF)
        g4[0] = jnp.zeros(g4.shape[1:], BF)

    @pl.when(r == last)
    def _():
        edge_img[1] = jnp.zeros(edge_img.shape[1:], BF)
        edge_cot[...] = jnp.zeros(edge_cot.shape, BF)
        g4[3] = jnp.zeros(g4.shape[1:], BF)

    for k in (0, 2, 3, 4, 5, 6, 7):
        loads[k].wait()
    for a in range(2):
        split_columns(img[a], a + 1)

    bias = twice(cb[...])
    hid[0] = nn(x4[1], wf[1]) + nn(x4[2], wf[2]) + bias
    hid[1] = nn(x4[1], wf[0]) + nn(x4[2], wf[1]) + bias

    pl.semaphore_wait(met.at[0], 3)
    for to in x_peers:
        greet(met.at[2], rows=to)
    if z_peers:
        pl.semaphore_wait(met.at[1], len(dp_near))
        for to in z_peers[3:5]:
            greet(met.at[3], dp=to)

    @pl.when(r > 0)
    def _():
        img_down.wait_recv()

    split_columns(edge_img[0], 0)
    hid[0] += nn(x4[0], wf[0])

    @pl.when(r < last)
    def _():
        img_up.wait_recv()

    split_columns(edge_img[1], 3)
    hid[1] += nn(x4[3], wf[2])

    def spread(table, send, recv):
        for to in row_peers:
            remote(table.at[r], table.at[r], send, recv, rows=to).start()

    def whole(table, send, recv):
        part = table.at[pl.ds(0, rows_n - 1)]
        return remote(part, part, send, recv, rows=mate)

    def colsum(x):
        return jnp.sum(x, axis=0, keepdims=True)

    own_sum = fold(colsum(hid[0]) + colsum(hid[1]))
    own_mean = twice(group_sum(jnp.broadcast_to(own_sum, (8, CHANS)))[:1] / n_local)
    off0 = hid[0] - own_mean
    off1 = hid[1] - own_mean
    own_sq = fold(colsum(off0 * off0) + colsum(off1 * off1))
    stat_a[r, 0:1, :] = own_sum
    stat_a[r, 1:2, :] = own_sq
    stat_a[r, 2:8, :] = jnp.zeros((6, CHANS), F32)
    pl.semaphore_wait(met.at[2], 3)
    spread(stat_a, sa_s, sa_r)
    if z_peers:
        pl.semaphore_wait(met.at[3], 2)
        for to in z_peers:
            greet(met.at[4], dp=to)

    @pl.when(r < last)
    def _():
        cot_up.wait_recv()

    def pull(grad, lead, kh):
        both = dw[kh, 1:3].reshape(2 * CHANS, OUTS)
        return nt(grad, both), nt(lead, dw[kh, 0])

    own_cot = cot[...]
    own_cot32 = own_cot.astype(F32)
    cot_sum = colsum(own_cot32)
    lead_cot = shifted(own_cot32, 1).astype(BF)
    full, odd = pull(own_cot, lead_cot, 1)
    gmix[0] = full
    gmix[0, :, CHANS:] += odd
    full, odd = pull(own_cot, lead_cot, 2)
    gmix[1] = full
    gmix[1, :, CHANS:] += odd
    below = edge_cot[...]
    full, odd = pull(below, shifted(below.astype(F32), 1).astype(BF), 0)
    gmix[1] += full
    gmix[1, :, CHANS:] += odd

    whole(stat_a, sa_s, sa_r).wait_recv()
    table = stat_a[...]
    groups = group_sum(table.reshape(rows_n * 8, CHANS)).reshape(rows_n, 8, CHANS)
    group_tot = jnp.sum(groups, axis=0)
    mean = group_tot[0:1] / n_total
    dev = groups / n_local - mean.reshape(1, 1, CHANS)
    spread_sq = jnp.sum(dev * dev, axis=0)[0:1] * n_local
    rstd = lax.rsqrt((group_tot[1:2] + spread_sq) / n_total + EPS)
    channel_sum = jnp.sum(table, axis=0)[0:1]
    mean2, rstd2 = twice(mean), twice(rstd)
    gain2, shift2 = twice(gain_ref[...]), twice(shift_ref[...])

    sum_gp = jnp.zeros((1, 2 * CHANS), F32)
    sum_gpn = jnp.zeros((1, 2 * CHANS), F32)
    for a in (1, 0):
        normed = (hid[a] - mean2) * rstd2
        pre = normed * gain2 + shift2
        sig = jax.nn.sigmoid(pre)
        mixed = (x4[a + 1, :, CHANS : 3 * CHANS].astype(F32) + pre * sig).astype(BF)
        m4[a + 1, :, CHANS:] = mixed
        gp = gmix[a] * sig * (1.0 + pre * (1.0 - sig))
        hid[a] = normed
        gpre[a] = gp
        sum_gp += colsum(gp)
        sum_gpn += colsum(gp * normed)

    stat_b[r, 0:1, :] = fold(sum_gp)
    stat_b[r, 1:2, :] = fold(sum_gpn)
    stat_b[r, 2:3, :] = cot_sum[:, :CHANS]
    stat_b[r, 3:4, :] = cot_sum[:, CHANS:]
    stat_b[r, 4:8, :] = jnp.zeros((4, CHANS), F32)
    spread(stat_b, sb_s, sb_r)

    @pl.when(r < last)
    def _():
        mix_down.start()

    sub = lax.broadcasted_iota(jnp.int32, (CHANS, CHANS), 0) % 8

    def down_grad(kh):
        part = tn(own_cot, m4[kh])
        for kw in range(3):
            tap = 3 * kh + kw
            tiles = part[:, kw * CHANS : (kw + 1) * CHANS].reshape(16, 2, 8, CHANS)
            one = tiles[:, 0].reshape(CHANS, CHANS)
            two = tiles[:, 1].reshape(CHANS, CHANS)
            low = jnp.where(sub < 4, one, pltpu.roll(two, 4, 0))
            high = jnp.where(sub < 4, pltpu.roll(one, CHANS - 4, 0), two)
            if tap >= 3:
                early[0, tap - 3] = low
                early[1, tap - 3] = high
            else:
                late[0, 4 + tap] = low
                late[1, 5 + tap] = high

    def taps(kh):
        return dw[kh].reshape(3 * CHANS, OUTS)

    for a in range(2):
        m4[a + 1, :, :CHANS] = shifted(m4[a + 1, :, 2 * CHANS :].astype(F32), -1).astype(BF)

    down_grad(1)
    down_grad(2)
    cs[...] = early[1 - core].astype(BF)
    pair_one = remote(cs, cr, c_s.at[0], c_r.at[0], rows=mate)
    pair_two = remote(cs2.at[0:FIRST], cr2.at[0:FIRST], c_s.at[1], c_r.at[1], rows=mate)
    pair_rest = remote(cs2.at[FIRST:], cr2.at[FIRST:], c_s.at[2], c_r.at[2], rows=mate)
    pair_one.start()
    out = nn(m4[1], taps(1)) + nn(m4[2], taps(2)) + db[...]
    hold[...] = out

    def early_send(to):
        return remote(rs.at[lax.min(to, EARLY - 1)], rr.at[slot], r_s.at[to], r_r, rows=2 * to + core)

    def late_send(to):
        return remote(rs2.at[number(to)], rr2.at[slot], q_s.at[to], q_r, rows=2 * to + core)

    def number(at):
        return lax.div(at, 2) + 4 * lax.rem(at + core, 2)

    def late_sum(low, high):
        both = late[core, low:high] + cr2[low:high].astype(F32)
        late[core, low:high] = both
        rs2[low:high] = both.astype(BF)
        for to in slot_peers:

            @pl.when((number(to) >= low) & (number(to) < high))
            def _():
                late_send(to).start()

    pair_one.wait()
    both = early[core] + cr[...].astype(F32)
    early[core] = both
    rs[...] = both.astype(BF)
    for to in slot_peers:

        @pl.when(to < EARLY)
        def _():
            early_send(to).start()

    @pl.when(r > 0)
    def _():
        mix_down.wait_recv()
        m4[0, :, :CHANS] = shifted(m4[0, :, 2 * CHANS :].astype(F32), -1).astype(BF)

    down_grad(0)
    late[0, 7] = jnp.zeros((CHANS, CHANS), F32)
    cs2[FIRST:] = late[1 - core, FIRST:].astype(BF)
    pair_rest.start()
    block_out[0, 0] = (hold[...] + nn(m4[0], taps(0))).astype(BF)

    pair_rest.wait()
    late_sum(FIRST, slots)

    whole(stat_b, sb_s, sb_r).wait_recv()
    totals = jnp.sum(stat_b[...], axis=0)
    tot_gp = totals[0:1]
    tot_gpn = totals[1:2]
    means = group_sum(
        jnp.broadcast_to(gain_ref[...], (8, CHANS)) * totals
    ) / n_total
    m1, m2 = means[0:1], means[1:2]
    m1w, m2w = twice(m1), twice(m2)
    for a in range(2):
        grad = (rstd2 * (gpre[a] * gain2 - m1w - hid[a] * m2w)).astype(BF)
        g4[a + 1, :, CHANS : 3 * CHANS] = grad

    n_channel = float(2 * cols * rows_n)
    tot_normed = (channel_sum - n_channel * mean) * rstd
    tot_bias = rstd * (gain_ref[...] * tot_gp - n_channel * m1 - m2 * tot_normed)
    mine[...] = jnp.zeros(mine.shape, F32)
    for k in (0, 4):
        mine[0, k : k + 1, :] = tot_bias
        mine[0, k + 1 : k + 2, :] = tot_gpn
        mine[0, k + 2 : k + 3, :] = tot_gp
        mine[1, k : k + 1, :] = totals[2:3]
        mine[1, k + 1 : k + 2, :] = totals[3:4]

    for kh in range(3):
        part = tn(g4[1, :, CHANS : 3 * CHANS], x4[kh]) + tn(
            g4[2, :, CHANS : 3 * CHANS], x4[kh + 1]
        )
        for kw in range(3):
            tap = 3 * kh + kw
            late[tap % 2 if tap < 8 else 1, tap // 2] = (
                part[:CHANS, kw * CHANS : (kw + 1) * CHANS]
                + part[CHANS:, (kw + 1) * CHANS : (kw + 2) * CHANS]
            )
    cs2[:FIRST] = late[1 - core, :FIRST].astype(BF)
    pair_two.start()

    def sides(f):
        grad = g4[f, :, CHANS : 3 * CHANS].astype(F32)
        g4[f, :, :CHANS] = shifted(grad[:, CHANS:], -1).astype(BF)
        g4[f, :, 3 * CHANS :] = shifted(grad[:, :CHANS], 1).astype(BF)

    pair_two.wait()
    late_sum(0, FIRST)

    @pl.when(r < last)
    def _():
        g_down.start()

    @pl.when(r > 0)
    def _():
        g_up.start()

    sides(1)
    sides(2)
    gmix[0] += nt(g4[1], wb[1]) + nt(g4[2], wb[0])
    gmix[1] += nt(g4[1], wb[2]) + nt(g4[2], wb[1])

    others = pl.ds(0, slots - 1)

    @pl.when(slot < EARLY)
    def _():
        remote(rr.at[others], rr.at[others], r_s.at[slot], r_r, rows=mate).wait_recv()
        total = early[core, lax.min(slot, EARLY - 1)]
        for other in slot_peers:
            total = total + rr[other].astype(F32)
        red1[...] = total

    @pl.when(slot >= EARLY)
    def _():
        red1[...] = jnp.broadcast_to(mine[core][None], (16, 8, CHANS)).reshape(CHANS, CHANS)

    remote(rr2.at[others], rr2.at[others], q_s.at[slot], q_r, rows=mate).wait_recv()
    total = late[core, number(slot)]
    for other in slot_peers:
        total = total + rr2[other].astype(F32)
    red2[...] = total

    one, two = red1[...], red2[...]
    red[:CHANS] = jnp.where(sub < 4, one, pltpu.roll(two, 4, 0))
    red[CHANS:] = jnp.where(sub < 4, pltpu.roll(one, CHANS - 4, 0), two)

    def place(e):
        row = lax.rem(e, 2) * 16 + lax.div(e, 2)
        return pl.ds(pl.multiple_of(row * 8, 8), 8)

    if z_peers:
        pl.semaphore_wait(met.at[4], len(z_peers))
    for to in dp_peers:
        remote(red.at[place(to)], dr.at[d], d_s, d_r, dp=to).start()
    dr[d] = red[place(d), :]

    def put_row(a):
        tall[pl.ds(8, half, stride=2), :] = gmix[a, :, :CHANS]
        tall[pl.ds(9, half, stride=2), :] = gmix[a, :, CHANS:]
        gimg_out[0, a] = tall[8 : cols + 8, :].astype(BF)

    @pl.when(r > 0)
    def _():
        g_down.wait_recv()
        sides(0)

    gmix[0] += nt(g4[0], wb[2])
    put_row(0)

    @pl.when(r < last)
    def _():
        g_up.wait_recv()
        sides(3)

    gmix[1] += nt(g4[3], wb[0])
    put_row(1)

    if dp_n > 1:
        part = dr.at[pl.ds(0, dp_n - 1)]
        dp_round = remote(part, part, d_s, d_r, rows=mate)
        dp_round.wait_recv()
    gout[r] = jnp.sum(dr[...], axis=0)
    spread(gout, o_s, o_r)
    whole(gout, o_s, o_r).wait()

    @pl.when(r < last)
    def _():
        img_down.wait_send()
        mix_down.wait_send()
        g_down.wait_send()

    @pl.when(r > 0)
    def _():
        img_up.wait_send()
        cot_up.wait_send()
        g_up.wait_send()

    whole(stat_a, sa_s, sa_r).wait_send()
    whole(stat_b, sb_s, sb_r).wait_send()
    if dp_n > 1:
        dp_round.wait_send()
    for to in slot_peers:
        late_send(to).wait_send()

        @pl.when(to < EARLY)
        def _():
            early_send(to).wait_send()


def finish(
    block, gimg, table, block_out, gimg_out, conv_out, bias_out, gain_out, shift_out, down_out, db_out,
    conv_v, down_v, bias_v, gain_v, shift_v, db_v, sems,
):
    copies = [
        pltpu.make_async_copy(src, dst, sems.at[k])
        for k, (src, dst) in enumerate(
            (
                (block, block_out),
                (gimg, gimg_out),
                (conv_v, conv_out),
                (down_v, down_out),
                (bias_v, bias_out),
                (gain_v, gain_out),
                (shift_v, shift_out),
                (db_v, db_out),
            )
        )
    ]
    copies[0].start()
    copies[1].start()
    for tap in range(TAPS):
        conv_v[tap] = table[2 * tap + tap % 2 if tap < 8 else 1, 4:8]
        if tap < 3:
            down_v[tap, 0:4] = table[2 + 4 * tap, 4:8]
            down_v[tap, 4:8] = table[5 + 4 * tap, 4:8]
        else:
            down_v[tap, 0:4] = table[2 * tap - 6, 0:4]
            down_v[tap, 4:8] = table[2 * tap - 5, 0:4]
    d = lax.axis_index("dp")
    narrow = pltpu.roll(table[12], lax.rem(CHANS - 4 * d, CHANS), 1)
    bias_v[...] = narrow[0:1, :4]
    gain_v[...] = narrow[1:2, :4]
    shift_v[...] = narrow[2:3, :4]
    wide = pltpu.roll(table[13], lax.rem(2 * CHANS - 8 * d, CHANS), 1)
    db_v[...] = jnp.where(d < 16, wide[0:1, :8], wide[1:2, :8])
    for copy in copies[2:]:
        copy.start()
    for copy in copies:
        copy.wait()


def shards(
    images, conv_weight, conv_bias, norm_gain, norm_shift, down_weight, down_bias, cotangent
):
    rows_n = lax.axis_size("rows")
    dp_n = lax.axis_size("dp")
    _, local_rows, cols, chans = images.shape
    half = cols // 2
    vmem = pl.BlockSpec(memory_space=pltpu.VMEM)
    dma = pltpu.SemaphoreType.DMA
    anywhere = pl.BlockSpec(memory_space=pltpu.HBM)
    unit = (CHANS, CHANS)
    slots = rows_n // 2
    scratch = [
        pltpu.VMEM((local_rows, cols, chans), BF),
        pltpu.VMEM(conv_weight.shape, BF),
        pltpu.VMEM((1, CHANS), F32),
        pltpu.VMEM((1, CHANS), F32),
        pltpu.VMEM((1, CHANS), F32),
        pltpu.VMEM(down_weight.shape, BF),
        pltpu.VMEM((1, OUTS), F32),
        pltpu.VMEM((half, OUTS), BF),
        pltpu.VMEM((half + 16, OUTS), F32),
        pltpu.VMEM((cols + 16, CHANS), F32),
        pltpu.VMEM((2, cols, CHANS), BF),
        pltpu.VMEM((half, OUTS), BF),
        pltpu.VMEM((4, half, 4 * CHANS), BF),
        pltpu.VMEM((3, half, 3 * CHANS), BF),
        pltpu.VMEM((4, half, 4 * CHANS), BF),
        pltpu.VMEM((3, 4 * CHANS, 2 * CHANS), BF),
        pltpu.VMEM((3, 2 * CHANS, 4 * CHANS), BF),
        pltpu.VMEM((2, half, 2 * CHANS), F32),
        pltpu.VMEM((2, half, 2 * CHANS), F32),
        pltpu.VMEM((2, half, 2 * CHANS), F32),
        pltpu.VMEM((half, OUTS), F32),
        pltpu.VMEM((rows_n, 8, CHANS), F32),
        pltpu.VMEM((rows_n, 8, CHANS), F32),
        pltpu.VMEM((2, 8, CHANS), F32),
        pltpu.VMEM((2, EARLY) + unit, F32),
        pltpu.VMEM((2, slots) + unit, F32),
        pltpu.VMEM((EARLY,) + unit, BF),
        pltpu.VMEM((EARLY,) + unit, BF),
        pltpu.VMEM((slots,) + unit, BF),
        pltpu.VMEM((slots,) + unit, BF),
        pltpu.VMEM((EARLY,) + unit, BF),
        pltpu.VMEM((slots,) + unit, BF),
        pltpu.VMEM((slots,) + unit, BF),
        pltpu.VMEM((slots,) + unit, BF),
        pltpu.VMEM(unit, F32),
        pltpu.VMEM(unit, F32),
        pltpu.VMEM((OUTS, CHANS), F32),
        pltpu.VMEM((dp_n, 8, CHANS), F32),
        dma((8,)),
        dma((2,)),
        dma((2,)),
        dma,
        dma,
        dma,
        dma,
        dma((2,)),
        dma((2,)),
        dma,
        dma,
        dma,
        dma,
        dma((3,)),
        dma((3,)),
        dma((slots,)),
        dma,
        dma((slots,)),
        dma,
        dma,
        dma,
        dma,
        dma,
        pltpu.SemaphoreType.REGULAR((5,)),
    ]

    def body(*refs):
        kernel(rows_n, dp_n, *refs)

    block, grad_image, table = pl.pallas_call(
        body,
        out_shape=(
            jax.ShapeDtypeStruct((1, 1, half, OUTS), BF),
            jax.ShapeDtypeStruct((1, local_rows, cols, chans), BF),
            jax.ShapeDtypeStruct((rows_n, 8, CHANS), F32),
        ),
        in_specs=[anywhere] * 8,
        out_specs=(vmem, vmem, vmem),
        scratch_shapes=scratch,
        compiler_params=pltpu.CompilerParams(
            collective_id=0, has_side_effects=True, vmem_limit_bytes=40 * 1024 * 1024
        ),
        name="step",
    )(*(pltpu.with_memory_space_constraint(x, pltpu.HBM) for x in (
        images,
        conv_weight,
        conv_bias.reshape(1, CHANS),
        norm_gain.reshape(1, CHANS),
        norm_shift.reshape(1, CHANS),
        down_weight,
        down_bias.reshape(1, OUTS),
        cotangent.reshape(1, half, OUTS),
    )))
    shape = jax.ShapeDtypeStruct
    outs = pl.pallas_call(
        finish,
        out_shape=(
            shape(block.shape, BF),
            shape(grad_image.shape, BF),
            shape((TAPS, 4, CHANS), F32),
            shape((1, 4), F32),
            shape((1, 4), F32),
            shape((1, 4), F32),
            shape((TAPS, 8, CHANS), F32),
            shape((1, 8), F32),
        ),
        in_specs=[vmem, vmem, vmem],
        out_specs=[anywhere] * 8,
        scratch_shapes=[
            pltpu.VMEM((TAPS, 4, CHANS), F32),
            pltpu.VMEM((TAPS, 8, CHANS), F32),
            pltpu.VMEM((1, 4), F32),
            pltpu.VMEM((1, 4), F32),
            pltpu.VMEM((1, 4), F32),
            pltpu.VMEM((1, 8), F32),
            dma((8,)),
        ],
        compiler_params=pltpu.CompilerParams(vmem_limit_bytes=4 * 1024 * 1024),
        name="finish",
    )(block, grad_image, table)
    block, grad_image, conv_t, bias, gain, shift, down_t, down_bias_grad = outs
    return (
        block,
        grad_image,
        jnp.swapaxes(conv_t, 1, 2).reshape(3, 3, CHANS, 4),
        bias.reshape(4),
        gain.reshape(4),
        shift.reshape(4),
        jnp.swapaxes(down_t, 1, 2).reshape(3, 3, CHANS, 8),
        down_bias_grad.reshape(8),
    )


def solution(mesh):
    spread = P("dp", "rows", None, None)
    in_specs = (spread, P(), P(), P(), P(), P(), P(), spread)
    out_specs = (
        spread,
        spread,
        P(None, None, None, "dp"),
        P("dp"),
        P("dp"),
        P("dp"),
        P(None, None, None, "dp"),
        P("dp"),
    )
    return jax.shard_map(shards, mesh=mesh, in_specs=in_specs, out_specs=out_specs, check_vma=False)
```

```python
import jax
import jax.numpy as jnp
from jax import lax
from jax.experimental import pallas as pl
from jax.experimental.pallas import tpu as pltpu
from jax.sharding import PartitionSpec as P

GROUPS = 32
CHANS = 128
OUTS = 256
BF = jnp.bfloat16
F32 = jnp.float32
MESH = pl.DeviceIdType.MESH
EPS = 1e-05
TAPS = 9
EARLY = 6
FIRST = 5


def nn(a, b):
    return lax.dot_general(a, b, (((1,), (0,)), ((), ())), preferred_element_type=F32)


def nt(a, b):
    return lax.dot_general(a, b, (((1,), (1,)), ((), ())), preferred_element_type=F32)


def tn(a, b):
    return lax.dot_general(a, b, (((0,), (0,)), ((), ())), preferred_element_type=F32)


def group_sum(x):
    lane = lax.broadcasted_iota(jnp.int32, x.shape, 1)
    x = x + jnp.where(lane % 2 == 0, pltpu.roll(x, CHANS - 1, 1), pltpu.roll(x, 1, 1))
    return x + jnp.where(lane % 4 < 2, pltpu.roll(x, CHANS - 2, 1), pltpu.roll(x, 2, 1))


def twice(x):
    return jnp.concatenate([x, x], axis=1)


def fold(x):
    return x[:, :CHANS] + x[:, CHANS:]


def kernel(
    rows_n,
    dp_n,
    img_hbm,
    cw_hbm,
    cb_hbm,
    gain_hbm,
    shift_hbm,
    dw_hbm,
    db_hbm,
    cot_hbm,
    block_out,
    gimg_out,
    gout,
    img,
    cw,
    cb,
    gain_ref,
    shift_ref,
    dw,
    db,
    cot,
    wide,
    tall,
    edge_img,
    edge_cot,
    x4,
    m4,
    g4,
    wf,
    wb,
    hid,
    gpre,
    gmix,
    hold,
    stat_a,
    stat_b,
    mine,
    early,
    late,
    cs,
    cr,
    cs2,
    cr2,
    rs,
    rr,
    rs2,
    rr2,
    red1,
    red2,
    red,
    dr,
    load_sem,
    img_s,
    img_r,
    cot_s,
    cot_r,
    mix_s,
    mix_r,
    g_s,
    g_r,
    sa_s,
    sa_r,
    sb_s,
    sb_r,
    c_s,
    c_r,
    r_s,
    r_r,
    q_s,
    q_r,
    d_s,
    d_r,
    o_s,
    o_r,
    met,
):
    r = lax.axis_index("rows")
    d = lax.axis_index("dp")
    core = lax.rem(r, 2)
    slot = lax.div(r, 2)
    mate = r + 1 - 2 * core
    half = cot.shape[0]
    cols = 2 * half
    n_local = float(2 * cols * (CHANS // GROUPS))
    n_total = n_local * rows_n
    last = rows_n - 1
    slots = rows_n // 2

    def remote(src, dst, send, recv, **where):
        return pltpu.make_async_remote_copy(
            src_ref=src,
            dst_ref=dst,
            send_sem=send,
            recv_sem=recv,
            device_id=where,
            device_id_type=MESH,
        )

    loads = [
        pltpu.make_async_copy(src, dst, load_sem.at[k])
        for k, (src, dst) in enumerate(
            (
                (img_hbm.at[0], img),
                (cw_hbm, cw),
                (cot_hbm.at[0], cot),
                (dw_hbm, dw),
                (cb_hbm, cb),
                (gain_hbm, gain_ref),
                (shift_hbm, shift_ref),
                (db_hbm, db),
            )
        )
    ]
    x_at, y_at = lax.div(r, 4), lax.rem(slot, 2)
    hops = sorted(
        ((min(dx, 4 - dx) + dy, dc, dx, dy) for dx in range(4) for dy in range(2) for dc in range(2)),
        reverse=True,
    )
    row_peers = [
        lax.rem(x_at + dx, 4) * 4
        + (y_at if dy == 0 else 1 - y_at) * 2
        + (core if dc == 0 else 1 - core)
        for _, dc, dx, dy in hops[:-1]
    ]
    if dp_n == 32:
        z_at, h_at = lax.div(d, 4), lax.rem(d, 4)
        hops = sorted(
            ((min(dz, 8 - dz) + 2 * min(dh, 4 - dh), dz, dh) for dz in range(8) for dh in range(4)),
            reverse=True,
        )
        dp_peers = [
            lax.rem(z_at + dz, 8) * 4 + lax.rem(h_at + dh, 4) for _, dz, dh in hops[:-1]
        ]
    else:
        dp_peers = [lax.rem(d + i, dp_n) for i in range(1, dp_n)]

    barrier = pltpu.get_barrier_semaphore()
    slot_peers = [
        lax.rem(x_at + dx, 4) * 2 + (y_at if dy == 0 else 1 - y_at)
        for dx, dy in ((2, 1), (2, 0), (1, 1), (3, 1), (1, 0), (3, 0), (0, 1))
    ]
    if dp_n == 32:
        z_peers = [lax.rem(z_at + dz, 8) * 4 + h_at for dz in (4, 3, 5, 2, 6, 1, 7)]
        dp_near = z_peers[-2:] + [z_at * 4 + lax.rem(h_at + dh, 4) for dh in (1, 3)]
    else:
        z_peers, dp_near = [], dp_peers
    x_peers = [lax.rem(r + 4 * dx, rows_n) for dx in (2, 1, 3)]
    y_peer = r + 2 - 4 * y_at
    up = lax.max(r - 1, 0)
    down = lax.min(r + 1, last)

    def greet(sem, **where):
        pl.semaphore_signal(sem, inc=1, device_id=where, device_id_type=MESH)

    for to in dp_near:
        greet(barrier, dp=to)
    for to in x_peers[1:] + [y_peer]:
        greet(barrier, rows=to)
    greet(barrier, rows=mate)
    far = r - 1 + 2 * core
    far_is = (far >= 0) & (far <= last)

    @pl.when(far_is)
    def _():
        greet(barrier, rows=lax.min(lax.max(far, 0), last))

    for load in loads:
        load.start()

    pl.semaphore_wait(barrier, 4 + len(dp_near) + jnp.where(far_is, 1, 0))
    mid = pl.ds(CHANS, 2 * CHANS)
    img_down = remote(img_hbm.at[0, 1], edge_img.at[0], img_s.at[0], img_r.at[0], rows=down)
    img_up = remote(img_hbm.at[0, 0], edge_img.at[1], img_s.at[1], img_r.at[1], rows=up)
    cot_up = remote(cot_hbm.at[0], edge_cot, cot_s, cot_r, rows=up)
    mix_down = remote(m4.at[2, :, mid], m4.at[0, :, mid], mix_s, mix_r, rows=down)
    g_down = remote(g4.at[2, :, mid], g4.at[0, :, mid], g_s.at[0], g_r.at[0], rows=down)
    g_up = remote(g4.at[1, :, mid], g4.at[3, :, mid], g_s.at[1], g_r.at[1], rows=up)

    @pl.when(r < last)
    def _():
        img_down.start()

    @pl.when(r > 0)
    def _():
        img_up.start()
        cot_up.start()

    for to in x_peers[1:] + [y_peer]:
        greet(met.at[0], rows=to)
    if z_peers:
        for to in dp_near:
            greet(met.at[1], dp=to)

    loads[1].wait()
    zero_block = jnp.zeros((CHANS, CHANS), BF)
    for kh in range(3):
        for kw in range(3):
            tap = cw[kh, kw]
            wf[kh, kw * CHANS : (kw + 1) * CHANS, :CHANS] = tap
            wf[kh, (kw + 1) * CHANS : (kw + 2) * CHANS, CHANS:] = tap
            wb[kh, :CHANS, (2 - kw) * CHANS : (3 - kw) * CHANS] = tap
            wb[kh, CHANS:, (3 - kw) * CHANS : (4 - kw) * CHANS] = tap
        wf[kh, 3 * CHANS :, :CHANS] = zero_block
        wf[kh, :CHANS, CHANS:] = zero_block
        wb[kh, :CHANS, 3 * CHANS :] = zero_block
        wb[kh, CHANS:, :CHANS] = zero_block

    tall[:8, :] = jnp.zeros((8, CHANS), F32)
    tall[cols + 8 :, :] = jnp.zeros((8, CHANS), F32)
    wide[:8, :] = jnp.zeros((8, OUTS), F32)
    wide[half + 8 :, :] = jnp.zeros((8, OUTS), F32)

    def split_columns(row, f):
        tall[8 : cols + 8, :] = row.astype(F32)
        for k, start in enumerate((7, 8, 9, 10)):
            x4[f, :, k * CHANS : (k + 1) * CHANS] = tall[pl.ds(start, half, stride=2), :].astype(BF)

    def shifted(x, by):
        width = x.shape[1]
        wide[8 : half + 8, :width] = x
        return wide[8 + by : half + 8 + by, :width]

    @pl.when(r == 0)
    def _():
        edge_img[0] = jnp.zeros(edge_img.shape[1:], BF)
        m4[0] = jnp.zeros(m4.shape[1:], BF)
        g4[0] = jnp.zeros(g4.shape[1:], BF)

    @pl.when(r == last)
    def _():
        edge_img[1] = jnp.zeros(edge_img.shape[1:], BF)
        edge_cot[...] = jnp.zeros(edge_cot.shape, BF)
        g4[3] = jnp.zeros(g4.shape[1:], BF)

    for k in (0, 2, 3, 4, 5, 6, 7):
        loads[k].wait()
    for a in range(2):
        split_columns(img[a], a + 1)

    bias = twice(cb[...])
    hid[0] = nn(x4[1], wf[1]) + nn(x4[2], wf[2]) + bias
    hid[1] = nn(x4[1], wf[0]) + nn(x4[2], wf[1]) + bias

    pl.semaphore_wait(met.at[0], 3)
    for to in x_peers:
        greet(met.at[2], rows=to)
    if z_peers:
        pl.semaphore_wait(met.at[1], len(dp_near))
        for to in z_peers[3:5]:
            greet(met.at[3], dp=to)

    def add_edge(e):
        split_columns(edge_img[e], 3 * e)
        hid[e] += nn(x4[3 * e], wf[2 * e])

    def edge_in(e):
        remote(img_hbm.at[0, 0], edge_img.at[e], img_s.at[0], img_r.at[e], rows=mate).wait_recv()

    edge_in(1 - core)
    add_edge(1 - core)

    @pl.when(far_is)
    def _():
        edge_in(core)

    add_edge(core)

    def spread(table, send, recv):
        for to in row_peers:
            remote(table.at[r], table.at[r], send, recv, rows=to).start()

    def whole(table, send, recv):
        part = table.at[pl.ds(0, rows_n - 1)]
        return remote(part, part, send, recv, rows=mate)

    def colsum(x):
        return jnp.sum(x, axis=0, keepdims=True)

    own_sum = fold(colsum(hid[0]) + colsum(hid[1]))
    own_mean = twice(group_sum(jnp.broadcast_to(own_sum, (8, CHANS)))[:1] / n_local)
    off0 = hid[0] - own_mean
    off1 = hid[1] - own_mean
    own_sq = fold(colsum(off0 * off0) + colsum(off1 * off1))
    stat_a[r, 0:1, :] = own_sum
    stat_a[r, 1:2, :] = own_sq
    stat_a[r, 2:8, :] = jnp.zeros((6, CHANS), F32)
    pl.semaphore_wait(met.at[2], 3)
    spread(stat_a, sa_s, sa_r)
    if z_peers:
        pl.semaphore_wait(met.at[3], 2)
        for to in z_peers:
            greet(met.at[4], dp=to)

    @pl.when(r < last)
    def _():
        cot_up.wait_recv()

    def pull(grad, lead, kh):
        both = dw[kh, 1:3].reshape(2 * CHANS, OUTS)
        return nt(grad, both), nt(lead, dw[kh, 0])

    own_cot = cot[...]
    own_cot32 = own_cot.astype(F32)
    cot_sum = colsum(own_cot32)
    lead_cot = shifted(own_cot32, 1).astype(BF)
    full, odd = pull(own_cot, lead_cot, 1)
    gmix[0] = full
    gmix[0, :, CHANS:] += odd
    full, odd = pull(own_cot, lead_cot, 2)
    gmix[1] = full
    gmix[1, :, CHANS:] += odd
    below = edge_cot[...]
    full, odd = pull(below, shifted(below.astype(F32), 1).astype(BF), 0)
    gmix[1] += full
    gmix[1, :, CHANS:] += odd

    whole(stat_a, sa_s, sa_r).wait_recv()
    table = stat_a[...]
    groups = group_sum(table.reshape(rows_n * 8, CHANS)).reshape(rows_n, 8, CHANS)
    group_tot = jnp.sum(groups, axis=0)
    mean = group_tot[0:1] / n_total
    dev = groups / n_local - mean.reshape(1, 1, CHANS)
    spread_sq = jnp.sum(dev * dev, axis=0)[0:1] * n_local
    rstd = lax.rsqrt((group_tot[1:2] + spread_sq) / n_total + EPS)
    channel_sum = jnp.sum(table, axis=0)[0:1]
    mean2, rstd2 = twice(mean), twice(rstd)
    gain2, shift2 = twice(gain_ref[...]), twice(shift_ref[...])

    sum_gp = jnp.zeros((1, 2 * CHANS), F32)
    sum_gpn = jnp.zeros((1, 2 * CHANS), F32)
    for a in (1, 0):
        normed = (hid[a] - mean2) * rstd2
        pre = normed * gain2 + shift2
        sig = jax.nn.sigmoid(pre)
        mixed = (x4[a + 1, :, CHANS : 3 * CHANS].astype(F32) + pre * sig).astype(BF)
        m4[a + 1, :, CHANS:] = mixed
        gp = gmix[a] * sig * (1.0 + pre * (1.0 - sig))
        hid[a] = normed
        gpre[a] = gp
        sum_gp += colsum(gp)
        sum_gpn += colsum(gp * normed)

    stat_b[r, 0:1, :] = fold(sum_gp)
    stat_b[r, 1:2, :] = fold(sum_gpn)
    stat_b[r, 2:3, :] = cot_sum[:, :CHANS]
    stat_b[r, 3:4, :] = cot_sum[:, CHANS:]
    stat_b[r, 4:8, :] = jnp.zeros((4, CHANS), F32)
    spread(stat_b, sb_s, sb_r)

    @pl.when(r < last)
    def _():
        mix_down.start()

    sub = lax.broadcasted_iota(jnp.int32, (CHANS, CHANS), 0) % 8

    def down_grad(kh):
        part = tn(own_cot, m4[kh])
        for kw in range(3):
            tap = 3 * kh + kw
            tiles = part[:, kw * CHANS : (kw + 1) * CHANS].reshape(16, 2, 8, CHANS)
            one = tiles[:, 0].reshape(CHANS, CHANS)
            two = tiles[:, 1].reshape(CHANS, CHANS)
            low = jnp.where(sub < 4, one, pltpu.roll(two, 4, 0))
            high = jnp.where(sub < 4, pltpu.roll(one, CHANS - 4, 0), two)
            if tap >= 3:
                early[0, tap - 3] = low
                early[1, tap - 3] = high
            else:
                late[0, 4 + tap] = low
                late[1, 5 + tap] = high

    def taps(kh):
        return dw[kh].reshape(3 * CHANS, OUTS)

    for a in range(2):
        m4[a + 1, :, :CHANS] = shifted(m4[a + 1, :, 2 * CHANS :].astype(F32), -1).astype(BF)

    down_grad(1)
    down_grad(2)
    cs[...] = early[1 - core].astype(BF)
    pair_one = remote(cs, cr, c_s.at[0], c_r.at[0], rows=mate)
    pair_two = remote(cs2.at[0:FIRST], cr2.at[0:FIRST], c_s.at[1], c_r.at[1], rows=mate)
    pair_rest = remote(cs2.at[FIRST:], cr2.at[FIRST:], c_s.at[2], c_r.at[2], rows=mate)
    pair_one.start()
    out = nn(m4[1], taps(1)) + nn(m4[2], taps(2)) + db[...]
    hold[...] = out

    def early_send(to):
        return remote(rs.at[lax.min(to, EARLY - 1)], rr.at[slot], r_s.at[to], r_r, rows=2 * to + core)

    def late_send(to):
        return remote(rs2.at[number(to)], rr2.at[slot], q_s.at[to], q_r, rows=2 * to + core)

    def number(at):
        return lax.div(at, 2) + 4 * lax.rem(at + core, 2)

    def late_sum(low, high):
        both = late[core, low:high] + cr2[low:high].astype(F32)
        late[core, low:high] = both
        rs2[low:high] = both.astype(BF)
        for to in slot_peers:

            @pl.when((number(to) >= low) & (number(to) < high))
            def _():
                late_send(to).start()

    pair_one.wait()
    both = early[core] + cr[...].astype(F32)
    early[core] = both
    rs[...] = both.astype(BF)
    for to in slot_peers:

        @pl.when(to < EARLY)
        def _():
            early_send(to).start()

    @pl.when(r > 0)
    def _():
        mix_down.wait_recv()
        m4[0, :, :CHANS] = shifted(m4[0, :, 2 * CHANS :].astype(F32), -1).astype(BF)

    down_grad(0)
    late[0, 7] = jnp.zeros((CHANS, CHANS), F32)
    cs2[FIRST:] = late[1 - core, FIRST:].astype(BF)
    pair_rest.start()
    block_out[0, 0] = (hold[...] + nn(m4[0], taps(0))).astype(BF)

    pair_rest.wait()
    late_sum(FIRST, slots)

    whole(stat_b, sb_s, sb_r).wait_recv()
    totals = jnp.sum(stat_b[...], axis=0)
    tot_gp = totals[0:1]
    tot_gpn = totals[1:2]
    means = group_sum(
        jnp.broadcast_to(gain_ref[...], (8, CHANS)) * totals
    ) / n_total
    m1, m2 = means[0:1], means[1:2]
    m1w, m2w = twice(m1), twice(m2)
    for a in range(2):
        grad = (rstd2 * (gpre[a] * gain2 - m1w - hid[a] * m2w)).astype(BF)
        g4[a + 1, :, CHANS : 3 * CHANS] = grad

    n_channel = float(2 * cols * rows_n)
    tot_normed = (channel_sum - n_channel * mean) * rstd
    tot_bias = rstd * (gain_ref[...] * tot_gp - n_channel * m1 - m2 * tot_normed)
    mine[...] = jnp.zeros(mine.shape, F32)
    for k in (0, 4):
        mine[0, k : k + 1, :] = tot_bias
        mine[0, k + 1 : k + 2, :] = tot_gpn
        mine[0, k + 2 : k + 3, :] = tot_gp
        mine[1, k : k + 1, :] = totals[2:3]
        mine[1, k + 1 : k + 2, :] = totals[3:4]

    for kh in range(3):
        part = tn(g4[1, :, CHANS : 3 * CHANS], x4[kh]) + tn(
            g4[2, :, CHANS : 3 * CHANS], x4[kh + 1]
        )
        for kw in range(3):
            tap = 3 * kh + kw
            late[tap % 2 if tap < 8 else 1, tap // 2] = (
                part[:CHANS, kw * CHANS : (kw + 1) * CHANS]
                + part[CHANS:, (kw + 1) * CHANS : (kw + 2) * CHANS]
            )
    cs2[:FIRST] = late[1 - core, :FIRST].astype(BF)
    pair_two.start()

    def sides(f):
        grad = g4[f, :, CHANS : 3 * CHANS].astype(F32)
        g4[f, :, :CHANS] = shifted(grad[:, CHANS:], -1).astype(BF)
        g4[f, :, 3 * CHANS :] = shifted(grad[:, :CHANS], 1).astype(BF)

    pair_two.wait()
    late_sum(0, FIRST)

    @pl.when(r < last)
    def _():
        g_down.start()

    @pl.when(r > 0)
    def _():
        g_up.start()

    sides(1)
    sides(2)
    gmix[0] += nt(g4[1], wb[1]) + nt(g4[2], wb[0])
    gmix[1] += nt(g4[1], wb[2]) + nt(g4[2], wb[1])

    others = pl.ds(0, slots - 1)

    @pl.when(slot < EARLY)
    def _():
        remote(rr.at[others], rr.at[others], r_s.at[slot], r_r, rows=mate).wait_recv()
        total = early[core, lax.min(slot, EARLY - 1)]
        for other in slot_peers:
            total = total + rr[other].astype(F32)
        red1[...] = total

    @pl.when(slot >= EARLY)
    def _():
        red1[...] = jnp.broadcast_to(mine[core][None], (16, 8, CHANS)).reshape(CHANS, CHANS)

    remote(rr2.at[others], rr2.at[others], q_s.at[slot], q_r, rows=mate).wait_recv()
    total = late[core, number(slot)]
    for other in slot_peers:
        total = total + rr2[other].astype(F32)
    red2[...] = total

    one, two = red1[...], red2[...]
    red[:CHANS] = jnp.where(sub < 4, one, pltpu.roll(two, 4, 0))
    red[CHANS:] = jnp.where(sub < 4, pltpu.roll(one, CHANS - 4, 0), two)

    def place(e):
        row = lax.rem(e, 2) * 16 + lax.div(e, 2)
        return pl.ds(pl.multiple_of(row * 8, 8), 8)

    if z_peers:
        pl.semaphore_wait(met.at[4], len(z_peers))
    for to in dp_peers:
        remote(red.at[place(to)], dr.at[d], d_s, d_r, dp=to).start()
    dr[d] = red[place(d), :]

    def put_row(a):
        tall[pl.ds(8, half, stride=2), :] = gmix[a, :, :CHANS]
        tall[pl.ds(9, half, stride=2), :] = gmix[a, :, CHANS:]
        gimg_out[0, a] = tall[8 : cols + 8, :].astype(BF)

    @pl.when(r > 0)
    def _():
        g_down.wait_recv()
        sides(0)

    gmix[0] += nt(g4[0], wb[2])
    put_row(0)

    @pl.when(r < last)
    def _():
        g_up.wait_recv()
        sides(3)

    gmix[1] += nt(g4[3], wb[0])
    put_row(1)

    if dp_n > 1:
        part = dr.at[pl.ds(0, dp_n - 1)]
        dp_round = remote(part, part, d_s, d_r, rows=mate)
        dp_round.wait_recv()
    gout[r] = jnp.sum(dr[...], axis=0)
    spread(gout, o_s, o_r)
    whole(gout, o_s, o_r).wait()

    @pl.when(r < last)
    def _():
        img_down.wait_send()
        mix_down.wait_send()
        g_down.wait_send()

    @pl.when(r > 0)
    def _():
        img_up.wait_send()
        cot_up.wait_send()
        g_up.wait_send()

    whole(stat_a, sa_s, sa_r).wait_send()
    whole(stat_b, sb_s, sb_r).wait_send()
    if dp_n > 1:
        dp_round.wait_send()
    for to in slot_peers:
        late_send(to).wait_send()

        @pl.when(to < EARLY)
        def _():
            early_send(to).wait_send()


def finish(
    block, gimg, table, block_out, gimg_out, conv_out, bias_out, gain_out, shift_out, down_out, db_out,
    conv_v, down_v, bias_v, gain_v, shift_v, db_v, sems,
):
    copies = [
        pltpu.make_async_copy(src, dst, sems.at[k])
        for k, (src, dst) in enumerate(
            (
                (block, block_out),
                (gimg, gimg_out),
                (conv_v, conv_out),
                (down_v, down_out),
                (bias_v, bias_out),
                (gain_v, gain_out),
                (shift_v, shift_out),
                (db_v, db_out),
            )
        )
    ]
    copies[0].start()
    copies[1].start()
    for tap in range(TAPS):
        conv_v[tap] = table[2 * tap + tap % 2 if tap < 8 else 1, 4:8]
        if tap < 3:
            down_v[tap, 0:4] = table[2 + 4 * tap, 4:8]
            down_v[tap, 4:8] = table[5 + 4 * tap, 4:8]
        else:
            down_v[tap, 0:4] = table[2 * tap - 6, 0:4]
            down_v[tap, 4:8] = table[2 * tap - 5, 0:4]
    d = lax.axis_index("dp")
    narrow = pltpu.roll(table[12], lax.rem(CHANS - 4 * d, CHANS), 1)
    bias_v[...] = narrow[0:1, :4]
    gain_v[...] = narrow[1:2, :4]
    shift_v[...] = narrow[2:3, :4]
    wide = pltpu.roll(table[13], lax.rem(2 * CHANS - 8 * d, CHANS), 1)
    db_v[...] = jnp.where(d < 16, wide[0:1, :8], wide[1:2, :8])
    for copy in copies[2:]:
        copy.start()
    for copy in copies:
        copy.wait()


def shards(
    images, conv_weight, conv_bias, norm_gain, norm_shift, down_weight, down_bias, cotangent
):
    rows_n = lax.axis_size("rows")
    dp_n = lax.axis_size("dp")
    _, local_rows, cols, chans = images.shape
    half = cols // 2
    vmem = pl.BlockSpec(memory_space=pltpu.VMEM)
    dma = pltpu.SemaphoreType.DMA
    anywhere = pl.BlockSpec(memory_space=pltpu.HBM)
    unit = (CHANS, CHANS)
    slots = rows_n // 2
    scratch = [
        pltpu.VMEM((local_rows, cols, chans), BF),
        pltpu.VMEM(conv_weight.shape, BF),
        pltpu.VMEM((1, CHANS), F32),
        pltpu.VMEM((1, CHANS), F32),
        pltpu.VMEM((1, CHANS), F32),
        pltpu.VMEM(down_weight.shape, BF),
        pltpu.VMEM((1, OUTS), F32),
        pltpu.VMEM((half, OUTS), BF),
        pltpu.VMEM((half + 16, OUTS), F32),
        pltpu.VMEM((cols + 16, CHANS), F32),
        pltpu.VMEM((2, cols, CHANS), BF),
        pltpu.VMEM((half, OUTS), BF),
        pltpu.VMEM((4, half, 4 * CHANS), BF),
        pltpu.VMEM((3, half, 3 * CHANS), BF),
        pltpu.VMEM((4, half, 4 * CHANS), BF),
        pltpu.VMEM((3, 4 * CHANS, 2 * CHANS), BF),
        pltpu.VMEM((3, 2 * CHANS, 4 * CHANS), BF),
        pltpu.VMEM((2, half, 2 * CHANS), F32),
        pltpu.VMEM((2, half, 2 * CHANS), F32),
        pltpu.VMEM((2, half, 2 * CHANS), F32),
        pltpu.VMEM((half, OUTS), F32),
        pltpu.VMEM((rows_n, 8, CHANS), F32),
        pltpu.VMEM((rows_n, 8, CHANS), F32),
        pltpu.VMEM((2, 8, CHANS), F32),
        pltpu.VMEM((2, EARLY) + unit, F32),
        pltpu.VMEM((2, slots) + unit, F32),
        pltpu.VMEM((EARLY,) + unit, BF),
        pltpu.VMEM((EARLY,) + unit, BF),
        pltpu.VMEM((slots,) + unit, BF),
        pltpu.VMEM((slots,) + unit, BF),
        pltpu.VMEM((EARLY,) + unit, BF),
        pltpu.VMEM((slots,) + unit, BF),
        pltpu.VMEM((slots,) + unit, BF),
        pltpu.VMEM((slots,) + unit, BF),
        pltpu.VMEM(unit, F32),
        pltpu.VMEM(unit, F32),
        pltpu.VMEM((OUTS, CHANS), F32),
        pltpu.VMEM((dp_n, 8, CHANS), F32),
        dma((8,)),
        dma((2,)),
        dma((2,)),
        dma,
        dma,
        dma,
        dma,
        dma((2,)),
        dma((2,)),
        dma,
        dma,
        dma,
        dma,
        dma((3,)),
        dma((3,)),
        dma((slots,)),
        dma,
        dma((slots,)),
        dma,
        dma,
        dma,
        dma,
        dma,
        pltpu.SemaphoreType.REGULAR((5,)),
    ]

    def body(*refs):
        kernel(rows_n, dp_n, *refs)

    block, grad_image, table = pl.pallas_call(
        body,
        out_shape=(
            jax.ShapeDtypeStruct((1, 1, half, OUTS), BF),
            jax.ShapeDtypeStruct((1, local_rows, cols, chans), BF),
            jax.ShapeDtypeStruct((rows_n, 8, CHANS), F32),
        ),
        in_specs=[anywhere] * 8,
        out_specs=(vmem, vmem, vmem),
        scratch_shapes=scratch,
        compiler_params=pltpu.CompilerParams(
            collective_id=0, has_side_effects=True, vmem_limit_bytes=40 * 1024 * 1024
        ),
        name="step",
    )(*(pltpu.with_memory_space_constraint(x, pltpu.HBM) for x in (
        images,
        conv_weight,
        conv_bias.reshape(1, CHANS),
        norm_gain.reshape(1, CHANS),
        norm_shift.reshape(1, CHANS),
        down_weight,
        down_bias.reshape(1, OUTS),
        cotangent.reshape(1, half, OUTS),
    )))
    shape = jax.ShapeDtypeStruct
    outs = pl.pallas_call(
        finish,
        out_shape=(
            shape(block.shape, BF),
            shape(grad_image.shape, BF),
            shape((TAPS, 4, CHANS), F32),
            shape((1, 4), F32),
            shape((1, 4), F32),
            shape((1, 4), F32),
            shape((TAPS, 8, CHANS), F32),
            shape((1, 8), F32),
        ),
        in_specs=[vmem, vmem, vmem],
        out_specs=[anywhere] * 8,
        scratch_shapes=[
            pltpu.VMEM((TAPS, 4, CHANS), F32),
            pltpu.VMEM((TAPS, 8, CHANS), F32),
            pltpu.VMEM((1, 4), F32),
            pltpu.VMEM((1, 4), F32),
            pltpu.VMEM((1, 4), F32),
            pltpu.VMEM((1, 8), F32),
            dma((8,)),
        ],
        compiler_params=pltpu.CompilerParams(vmem_limit_bytes=4 * 1024 * 1024),
        name="finish",
    )(block, grad_image, table)
    block, grad_image, conv_t, bias, gain, shift, down_t, down_bias_grad = outs
    return (
        block,
        grad_image,
        jnp.swapaxes(conv_t, 1, 2).reshape(3, 3, CHANS, 4),
        bias.reshape(4),
        gain.reshape(4),
        shift.reshape(4),
        jnp.swapaxes(down_t, 1, 2).reshape(3, 3, CHANS, 8),
        down_bias_grad.reshape(8),
    )


def solution(mesh):
    spread = P("dp", "rows", None, None)
    in_specs = (spread, P(), P(), P(), P(), P(), P(), spread)
    out_specs = (
        spread,
        spread,
        P(None, None, None, "dp"),
        P("dp"),
        P("dp"),
        P("dp"),
        P(None, None, None, "dp"),
        P("dp"),
    )
    return jax.shard_map(shards, mesh=mesh, in_specs=in_specs, out_specs=out_specs, check_vma=False)
```

```python
import jax
import jax.numpy as jnp
from jax import lax
from jax.experimental import pallas as pl
from jax.experimental.pallas import tpu as pltpu
from jax.sharding import PartitionSpec as P

GROUPS = 32
CHANS = 128
OUTS = 256
BF = jnp.bfloat16
F32 = jnp.float32
MESH = pl.DeviceIdType.MESH
EPS = 1e-05
TAPS = 9
EARLY = 6
FIRST = 5


def nn(a, b):
    return lax.dot_general(a, b, (((1,), (0,)), ((), ())), preferred_element_type=F32)


def nt(a, b):
    return lax.dot_general(a, b, (((1,), (1,)), ((), ())), preferred_element_type=F32)


def tn(a, b):
    return lax.dot_general(a, b, (((0,), (0,)), ((), ())), preferred_element_type=F32)


def group_sum(x):
    lane = lax.broadcasted_iota(jnp.int32, x.shape, 1)
    x = x + jnp.where(lane % 2 == 0, pltpu.roll(x, CHANS - 1, 1), pltpu.roll(x, 1, 1))
    return x + jnp.where(lane % 4 < 2, pltpu.roll(x, CHANS - 2, 1), pltpu.roll(x, 2, 1))


def twice(x):
    return jnp.concatenate([x, x], axis=1)


def fold(x):
    return x[:, :CHANS] + x[:, CHANS:]


def kernel(
    rows_n,
    dp_n,
    img_hbm,
    cw_hbm,
    cb_hbm,
    gain_hbm,
    shift_hbm,
    dw_hbm,
    db_hbm,
    cot_hbm,
    block_out,
    gimg_out,
    gout,
    img,
    cw,
    cb,
    gain_ref,
    shift_ref,
    dw,
    db,
    cot,
    wide,
    tall,
    edge_img,
    edge_cot,
    x4,
    m4,
    g4,
    wf,
    wb,
    hid,
    gpre,
    gmix,
    hold,
    stat_a,
    stat_b,
    mine,
    early,
    late,
    cs,
    cr,
    cs2,
    cr2,
    rs,
    rr,
    rs2,
    rr2,
    red1,
    red2,
    red,
    dr,
    load_sem,
    img_s,
    img_r,
    cot_s,
    cot_r,
    mix_s,
    mix_r,
    g_s,
    g_r,
    sa_s,
    sa_r,
    sb_s,
    sb_r,
    c_s,
    c_r,
    r_s,
    r_r,
    q_s,
    q_r,
    d_s,
    d_r,
    o_s,
    o_r,
    met,
):
    r = lax.axis_index("rows")
    d = lax.axis_index("dp")
    core = lax.rem(r, 2)
    slot = lax.div(r, 2)
    mate = r + 1 - 2 * core
    half = cot.shape[0]
    cols = 2 * half
    n_local = float(2 * cols * (CHANS // GROUPS))
    n_total = n_local * rows_n
    last = rows_n - 1
    slots = rows_n // 2

    def remote(src, dst, send, recv, **where):
        return pltpu.make_async_remote_copy(
            src_ref=src,
            dst_ref=dst,
            send_sem=send,
            recv_sem=recv,
            device_id=where,
            device_id_type=MESH,
        )

    loads = [
        pltpu.make_async_copy(src, dst, load_sem.at[k])
        for k, (src, dst) in enumerate(
            (
                (img_hbm.at[0], img),
                (cw_hbm, cw),
                (cot_hbm.at[0], cot),
                (dw_hbm, dw),
                (cb_hbm, cb),
                (gain_hbm, gain_ref),
                (shift_hbm, shift_ref),
                (db_hbm, db),
            )
        )
    ]
    x_at, y_at = lax.div(r, 4), lax.rem(slot, 2)
    hops = sorted(
        ((min(dx, 4 - dx) + dy, dc, dx, dy) for dx in range(4) for dy in range(2) for dc in range(2)),
        reverse=True,
    )
    row_peers = [
        lax.rem(x_at + dx, 4) * 4
        + (y_at if dy == 0 else 1 - y_at) * 2
        + (core if dc == 0 else 1 - core)
        for _, dc, dx, dy in hops[:-1]
    ]
    if dp_n == 32:
        z_at, h_at = lax.div(d, 4), lax.rem(d, 4)
        hops = sorted(
            ((min(dz, 8 - dz) + 2 * min(dh, 4 - dh), dz, dh) for dz in range(8) for dh in range(4)),
            reverse=True,
        )
        dp_peers = [
            lax.rem(z_at + dz, 8) * 4 + lax.rem(h_at + dh, 4) for _, dz, dh in hops[:-1]
        ]
    else:
        dp_peers = [lax.rem(d + i, dp_n) for i in range(1, dp_n)]

    barrier = pltpu.get_barrier_semaphore()
    slot_peers = [
        lax.rem(x_at + dx, 4) * 2 + (y_at if dy == 0 else 1 - y_at)
        for dx, dy in ((2, 1), (2, 0), (1, 1), (3, 1), (1, 0), (3, 0), (0, 1))
    ]
    if dp_n == 32:
        z_peers = [lax.rem(z_at + dz, 8) * 4 + h_at for dz in (4, 3, 5, 2, 6, 1, 7)]
        dp_near = z_peers[-2:] + [z_at * 4 + lax.rem(h_at + dh, 4) for dh in (1, 3)]
    else:
        z_peers, dp_near = [], dp_peers
    x_peers = [lax.rem(r + 4 * dx, rows_n) for dx in (2, 1, 3)]
    y_peer = r + 2 - 4 * y_at
    up = lax.max(r - 1, 0)
    down = lax.min(r + 1, last)

    def greet(sem, **where):
        pl.semaphore_signal(sem, inc=1, device_id=where, device_id_type=MESH)

    for to in dp_near:
        greet(barrier, dp=to)
    for to in x_peers[1:] + [y_peer]:
        greet(barrier, rows=to)
    greet(barrier, rows=mate)
    far = r - 1 + 2 * core
    far_is = (far >= 0) & (far <= last)

    @pl.when(far_is)
    def _():
        greet(barrier, rows=lax.min(lax.max(far, 0), last))

    for load in loads:
        load.start()

    pl.semaphore_wait(barrier, 4 + len(dp_near) + jnp.where(far_is, 1, 0))
    mid = pl.ds(CHANS, 2 * CHANS)
    img_down = remote(img_hbm.at[0, 1], edge_img.at[0], img_s.at[0], img_r.at[0], rows=down)
    img_up = remote(img_hbm.at[0, 0], edge_img.at[1], img_s.at[1], img_r.at[1], rows=up)
    cot_up = remote(cot_hbm.at[0], edge_cot, cot_s, cot_r, rows=up)
    mix_down = remote(m4.at[2, :, mid], m4.at[0, :, mid], mix_s, mix_r, rows=down)
    g_down = remote(g4.at[2, :, mid], g4.at[0, :, mid], g_s.at[0], g_r.at[0], rows=down)
    g_up = remote(g4.at[1, :, mid], g4.at[3, :, mid], g_s.at[1], g_r.at[1], rows=up)

    @pl.when(r < last)
    def _():
        img_down.start()

    @pl.when(r > 0)
    def _():
        img_up.start()
        cot_up.start()

    for to in x_peers[1:] + [y_peer]:
        greet(met.at[0], rows=to)
    if z_peers:
        for to in dp_near:
            greet(met.at[1], dp=to)

    loads[1].wait()
    zero_block = jnp.zeros((CHANS, CHANS), BF)
    for kh in range(3):
        for kw in range(3):
            tap = cw[kh, kw]
            wf[kh, kw * CHANS : (kw + 1) * CHANS, :CHANS] = tap
            wf[kh, (kw + 1) * CHANS : (kw + 2) * CHANS, CHANS:] = tap
            wb[kh, :CHANS, (2 - kw) * CHANS : (3 - kw) * CHANS] = tap
            wb[kh, CHANS:, (3 - kw) * CHANS : (4 - kw) * CHANS] = tap
        wf[kh, 3 * CHANS :, :CHANS] = zero_block
        wf[kh, :CHANS, CHANS:] = zero_block
        wb[kh, :CHANS, 3 * CHANS :] = zero_block
        wb[kh, CHANS:, :CHANS] = zero_block

    tall[:8, :] = jnp.zeros((8, CHANS), F32)
    tall[cols + 8 :, :] = jnp.zeros((8, CHANS), F32)
    wide[:8, :] = jnp.zeros((8, OUTS), F32)
    wide[half + 8 :, :] = jnp.zeros((8, OUTS), F32)

    def split_columns(row, f):
        tall[8 : cols + 8, :] = row.astype(F32)
        for k, start in enumerate((7, 8, 9, 10)):
            x4[f, :, k * CHANS : (k + 1) * CHANS] = tall[pl.ds(start, half, stride=2), :].astype(BF)

    def shifted(x, by):
        width = x.shape[1]
        wide[8 : half + 8, :width] = x
        return wide[8 + by : half + 8 + by, :width]

    @pl.when(r == 0)
    def _():
        edge_img[0] = jnp.zeros(edge_img.shape[1:], BF)
        m4[0] = jnp.zeros(m4.shape[1:], BF)
        g4[0] = jnp.zeros(g4.shape[1:], BF)

    @pl.when(r == last)
    def _():
        edge_img[1] = jnp.zeros(edge_img.shape[1:], BF)
        edge_cot[...] = jnp.zeros(edge_cot.shape, BF)
        g4[3] = jnp.zeros(g4.shape[1:], BF)

    for k in (0, 2, 3, 4, 5, 6, 7):
        loads[k].wait()
    for a in range(2):
        split_columns(img[a], a + 1)

    bias = twice(cb[...])
    hid[0] = nn(x4[1], wf[1]) + nn(x4[2], wf[2]) + bias
    hid[1] = nn(x4[1], wf[0]) + nn(x4[2], wf[1]) + bias

    pl.semaphore_wait(met.at[0], 3)
    for to in x_peers:
        greet(met.at[2], rows=to)
    if z_peers:
        pl.semaphore_wait(met.at[1], len(dp_near))
        for to in z_peers[3:5]:
            greet(met.at[3], dp=to)

    def add_edge(e):
        split_columns(edge_img[e], 3 * e)
        hid[e] += nn(x4[3 * e], wf[2 * e])

    def edge_in(e):
        remote(img_hbm.at[0, 0], edge_img.at[e], img_s.at[0], img_r.at[e], rows=mate).wait_recv()

    edge_in(1 - core)
    add_edge(1 - core)

    @pl.when(far_is)
    def _():
        edge_in(core)

    add_edge(core)

    def spread(table, send, recv):
        for to in row_peers:
            remote(table.at[r], table.at[r], send, recv, rows=to).start()

    def whole(table, send, recv):
        part = table.at[pl.ds(0, rows_n - 1)]
        return remote(part, part, send, recv, rows=mate)

    def colsum(x):
        return jnp.sum(x, axis=0, keepdims=True)

    own_sum = fold(colsum(hid[0]) + colsum(hid[1]))
    own_mean = twice(group_sum(jnp.broadcast_to(own_sum, (8, CHANS)))[:1] / n_local)
    off0 = hid[0] - own_mean
    off1 = hid[1] - own_mean
    own_sq = fold(colsum(off0 * off0) + colsum(off1 * off1))
    stat_a[r, 0:1, :] = own_sum
    stat_a[r, 1:2, :] = own_sq
    stat_a[r, 2:8, :] = jnp.zeros((6, CHANS), F32)
    pl.semaphore_wait(met.at[2], 3)
    spread(stat_a, sa_s, sa_r)
    if z_peers:
        pl.semaphore_wait(met.at[3], 2)
        for to in z_peers:
            greet(met.at[4], dp=to)

    @pl.when(r < last)
    def _():
        cot_up.wait_recv()

    def pull(grad, lead, kh):
        both = dw[kh, 1:3].reshape(2 * CHANS, OUTS)
        return nt(grad, both), nt(lead, dw[kh, 0])

    own_cot = cot[...]
    own_cot32 = own_cot.astype(F32)
    cot_sum = colsum(own_cot32)
    lead_cot = shifted(own_cot32, 1).astype(BF)
    full, odd = pull(own_cot, lead_cot, 1)
    gmix[0] = full
    gmix[0, :, CHANS:] += odd
    full, odd = pull(own_cot, lead_cot, 2)
    gmix[1] = full
    gmix[1, :, CHANS:] += odd
    below = edge_cot[...]
    full, odd = pull(below, shifted(below.astype(F32), 1).astype(BF), 0)
    gmix[1] += full
    gmix[1, :, CHANS:] += odd

    whole(stat_a, sa_s, sa_r).wait_recv()
    table = stat_a[...]
    groups = group_sum(table.reshape(rows_n * 8, CHANS)).reshape(rows_n, 8, CHANS)
    group_tot = jnp.sum(groups, axis=0)
    mean = group_tot[0:1] / n_total
    dev = groups / n_local - mean.reshape(1, 1, CHANS)
    spread_sq = jnp.sum(dev * dev, axis=0)[0:1] * n_local
    rstd = lax.rsqrt((group_tot[1:2] + spread_sq) / n_total + EPS)
    channel_sum = jnp.sum(table, axis=0)[0:1]
    mean2, rstd2 = twice(mean), twice(rstd)
    gain2, shift2 = twice(gain_ref[...]), twice(shift_ref[...])

    sum_gp = jnp.zeros((1, 2 * CHANS), F32)
    sum_gpn = jnp.zeros((1, 2 * CHANS), F32)
    for a in (1, 0):
        normed = (hid[a] - mean2) * rstd2
        pre = normed * gain2 + shift2
        sig = jax.nn.sigmoid(pre)
        mixed = (x4[a + 1, :, CHANS : 3 * CHANS].astype(F32) + pre * sig).astype(BF)
        m4[a + 1, :, CHANS:] = mixed
        gp = gmix[a] * sig * (1.0 + pre * (1.0 - sig))
        hid[a] = normed
        gpre[a] = gp
        sum_gp += colsum(gp)
        sum_gpn += colsum(gp * normed)

    stat_b[r, 0:1, :] = fold(sum_gp)
    stat_b[r, 1:2, :] = fold(sum_gpn)
    stat_b[r, 2:3, :] = cot_sum[:, :CHANS]
    stat_b[r, 3:4, :] = cot_sum[:, CHANS:]
    stat_b[r, 4:8, :] = jnp.zeros((4, CHANS), F32)
    spread(stat_b, sb_s, sb_r)

    @pl.when(r < last)
    def _():
        mix_down.start()

    sub = lax.broadcasted_iota(jnp.int32, (CHANS, CHANS), 0) % 8

    def down_grad(kh):
        part = tn(own_cot, m4[kh])
        for kw in range(3):
            tap = 3 * kh + kw
            tiles = part[:, kw * CHANS : (kw + 1) * CHANS].reshape(16, 2, 8, CHANS)
            one = tiles[:, 0].reshape(CHANS, CHANS)
            two = tiles[:, 1].reshape(CHANS, CHANS)
            low = jnp.where(sub < 4, one, pltpu.roll(two, 4, 0))
            high = jnp.where(sub < 4, pltpu.roll(one, CHANS - 4, 0), two)
            if tap >= 3:
                early[0, tap - 3] = low
                early[1, tap - 3] = high
            else:
                late[0, 4 + tap] = low
                late[1, 5 + tap] = high

    def taps(kh):
        return dw[kh].reshape(3 * CHANS, OUTS)

    for a in range(2):
        m4[a + 1, :, :CHANS] = shifted(m4[a + 1, :, 2 * CHANS :].astype(F32), -1).astype(BF)

    down_grad(1)
    down_grad(2)
    cs[...] = early[1 - core].astype(BF)
    pair_one = remote(cs, cr, c_s.at[0], c_r.at[0], rows=mate)
    pair_two = remote(cs2.at[0:FIRST], cr2.at[0:FIRST], c_s.at[1], c_r.at[1], rows=mate)
    pair_rest = remote(cs2.at[FIRST:], cr2.at[FIRST:], c_s.at[2], c_r.at[2], rows=mate)
    pair_one.start()
    out = nn(m4[1], taps(1)) + nn(m4[2], taps(2)) + db[...]
    hold[...] = out

    def early_send(to):
        return remote(rs.at[lax.min(to, EARLY - 1)], rr.at[slot], r_s.at[to], r_r, rows=2 * to + core)

    def late_send(to):
        return remote(rs2.at[number(to)], rr2.at[slot], q_s.at[to], q_r, rows=2 * to + core)

    def number(at):
        return lax.div(at, 2) + 4 * lax.rem(at + core, 2)

    def late_sum(low, high):
        both = late[core, low:high] + cr2[low:high].astype(F32)
        late[core, low:high] = both
        rs2[low:high] = both.astype(BF)
        for to in slot_peers:

            @pl.when((number(to) >= low) & (number(to) < high))
            def _():
                late_send(to).start()

    pair_one.wait()
    both = early[core] + cr[...].astype(F32)
    early[core] = both
    rs[...] = both.astype(BF)
    for to in slot_peers:

        @pl.when(to < EARLY)
        def _():
            early_send(to).start()

    @pl.when(r > 0)
    def _():
        mix_down.wait_recv()
        m4[0, :, :CHANS] = shifted(m4[0, :, 2 * CHANS :].astype(F32), -1).astype(BF)

    down_grad(0)
    late[0, 7] = jnp.zeros((CHANS, CHANS), F32)
    cs2[FIRST:] = late[1 - core, FIRST:].astype(BF)
    pair_rest.start()

    whole(stat_b, sb_s, sb_r).wait_recv()
    totals = jnp.sum(stat_b[...], axis=0)
    tot_gp = totals[0:1]
    tot_gpn = totals[1:2]
    means = group_sum(
        jnp.broadcast_to(gain_ref[...], (8, CHANS)) * totals
    ) / n_total
    m1, m2 = means[0:1], means[1:2]
    m1w, m2w = twice(m1), twice(m2)
    for a in range(2):
        grad = (rstd2 * (gpre[a] * gain2 - m1w - hid[a] * m2w)).astype(BF)
        g4[a + 1, :, CHANS : 3 * CHANS] = grad

    n_channel = float(2 * cols * rows_n)
    tot_normed = (channel_sum - n_channel * mean) * rstd
    tot_bias = rstd * (gain_ref[...] * tot_gp - n_channel * m1 - m2 * tot_normed)
    mine[...] = jnp.zeros(mine.shape, F32)
    for k in (0, 4):
        mine[0, k : k + 1, :] = tot_bias
        mine[0, k + 1 : k + 2, :] = tot_gpn
        mine[0, k + 2 : k + 3, :] = tot_gp
        mine[1, k : k + 1, :] = totals[2:3]
        mine[1, k + 1 : k + 2, :] = totals[3:4]

    for kh in range(3):
        part = tn(g4[1, :, CHANS : 3 * CHANS], x4[kh]) + tn(
            g4[2, :, CHANS : 3 * CHANS], x4[kh + 1]
        )
        for kw in range(3):
            tap = 3 * kh + kw
            late[tap % 2 if tap < 8 else 1, tap // 2] = (
                part[:CHANS, kw * CHANS : (kw + 1) * CHANS]
                + part[CHANS:, (kw + 1) * CHANS : (kw + 2) * CHANS]
            )
    cs2[:FIRST] = late[1 - core, :FIRST].astype(BF)
    pair_two.start()

    def sides(f):
        grad = g4[f, :, CHANS : 3 * CHANS].astype(F32)
        g4[f, :, :CHANS] = shifted(grad[:, CHANS:], -1).astype(BF)
        g4[f, :, 3 * CHANS :] = shifted(grad[:, :CHANS], 1).astype(BF)

    pair_rest.wait()
    late_sum(FIRST, slots)

    pair_two.wait()
    late_sum(0, FIRST)

    @pl.when(r < last)
    def _():
        g_down.start()

    @pl.when(r > 0)
    def _():
        g_up.start()

    block_out[0, 0] = (hold[...] + nn(m4[0], taps(0))).astype(BF)
    sides(1)
    sides(2)
    gmix[0] += nt(g4[1], wb[1]) + nt(g4[2], wb[0])
    gmix[1] += nt(g4[1], wb[2]) + nt(g4[2], wb[1])

    others = pl.ds(0, slots - 1)

    @pl.when(slot < EARLY)
    def _():
        remote(rr.at[others], rr.at[others], r_s.at[slot], r_r, rows=mate).wait_recv()
        total = early[core, lax.min(slot, EARLY - 1)]
        for other in slot_peers:
            total = total + rr[other].astype(F32)
        red1[...] = total

    @pl.when(slot >= EARLY)
    def _():
        red1[...] = jnp.broadcast_to(mine[core][None], (16, 8, CHANS)).reshape(CHANS, CHANS)

    remote(rr2.at[others], rr2.at[others], q_s.at[slot], q_r, rows=mate).wait_recv()
    total = late[core, number(slot)]
    for other in slot_peers:
        total = total + rr2[other].astype(F32)
    red2[...] = total

    one, two = red1[...], red2[...]
    red[:CHANS] = jnp.where(sub < 4, one, pltpu.roll(two, 4, 0))
    red[CHANS:] = jnp.where(sub < 4, pltpu.roll(one, CHANS - 4, 0), two)

    def place(e):
        row = lax.rem(e, 2) * 16 + lax.div(e, 2)
        return pl.ds(pl.multiple_of(row * 8, 8), 8)

    if z_peers:
        pl.semaphore_wait(met.at[4], len(z_peers))
    for to in dp_peers:
        remote(red.at[place(to)], dr.at[d], d_s, d_r, dp=to).start()
    dr[d] = red[place(d), :]

    def put_row(a):
        tall[pl.ds(8, half, stride=2), :] = gmix[a, :, :CHANS]
        tall[pl.ds(9, half, stride=2), :] = gmix[a, :, CHANS:]
        gimg_out[0, a] = tall[8 : cols + 8, :].astype(BF)

    @pl.when(r > 0)
    def _():
        g_down.wait_recv()
        sides(0)

    gmix[0] += nt(g4[0], wb[2])
    put_row(0)

    @pl.when(r < last)
    def _():
        g_up.wait_recv()
        sides(3)

    gmix[1] += nt(g4[3], wb[0])
    put_row(1)

    if dp_n > 1:
        part = dr.at[pl.ds(0, dp_n - 1)]
        dp_round = remote(part, part, d_s, d_r, rows=mate)
        dp_round.wait_recv()
    gout[r] = jnp.sum(dr[...], axis=0)
    spread(gout, o_s, o_r)
    whole(gout, o_s, o_r).wait()

    @pl.when(r < last)
    def _():
        img_down.wait_send()
        mix_down.wait_send()
        g_down.wait_send()

    @pl.when(r > 0)
    def _():
        img_up.wait_send()
        cot_up.wait_send()
        g_up.wait_send()

    whole(stat_a, sa_s, sa_r).wait_send()
    whole(stat_b, sb_s, sb_r).wait_send()
    if dp_n > 1:
        dp_round.wait_send()
    for to in slot_peers:
        late_send(to).wait_send()

        @pl.when(to < EARLY)
        def _():
            early_send(to).wait_send()


def finish(
    block, gimg, table, block_out, gimg_out, conv_out, bias_out, gain_out, shift_out, down_out, db_out,
    conv_v, down_v, bias_v, gain_v, shift_v, db_v, sems,
):
    copies = [
        pltpu.make_async_copy(src, dst, sems.at[k])
        for k, (src, dst) in enumerate(
            (
                (block, block_out),
                (gimg, gimg_out),
                (conv_v, conv_out),
                (down_v, down_out),
                (bias_v, bias_out),
                (gain_v, gain_out),
                (shift_v, shift_out),
                (db_v, db_out),
            )
        )
    ]
    copies[0].start()
    copies[1].start()
    for tap in range(TAPS):
        conv_v[tap] = table[2 * tap + tap % 2 if tap < 8 else 1, 4:8]
        if tap < 3:
            down_v[tap, 0:4] = table[2 + 4 * tap, 4:8]
            down_v[tap, 4:8] = table[5 + 4 * tap, 4:8]
        else:
            down_v[tap, 0:4] = table[2 * tap - 6, 0:4]
            down_v[tap, 4:8] = table[2 * tap - 5, 0:4]
    d = lax.axis_index("dp")
    narrow = pltpu.roll(table[12], lax.rem(CHANS - 4 * d, CHANS), 1)
    bias_v[...] = narrow[0:1, :4]
    gain_v[...] = narrow[1:2, :4]
    shift_v[...] = narrow[2:3, :4]
    wide = pltpu.roll(table[13], lax.rem(2 * CHANS - 8 * d, CHANS), 1)
    db_v[...] = jnp.where(d < 16, wide[0:1, :8], wide[1:2, :8])
    for copy in copies[2:]:
        copy.start()
    for copy in copies:
        copy.wait()


def shards(
    images, conv_weight, conv_bias, norm_gain, norm_shift, down_weight, down_bias, cotangent
):
    rows_n = lax.axis_size("rows")
    dp_n = lax.axis_size("dp")
    _, local_rows, cols, chans = images.shape
    half = cols // 2
    vmem = pl.BlockSpec(memory_space=pltpu.VMEM)
    dma = pltpu.SemaphoreType.DMA
    anywhere = pl.BlockSpec(memory_space=pltpu.HBM)
    unit = (CHANS, CHANS)
    slots = rows_n // 2
    scratch = [
        pltpu.VMEM((local_rows, cols, chans), BF),
        pltpu.VMEM(conv_weight.shape, BF),
        pltpu.VMEM((1, CHANS), F32),
        pltpu.VMEM((1, CHANS), F32),
        pltpu.VMEM((1, CHANS), F32),
        pltpu.VMEM(down_weight.shape, BF),
        pltpu.VMEM((1, OUTS), F32),
        pltpu.VMEM((half, OUTS), BF),
        pltpu.VMEM((half + 16, OUTS), F32),
        pltpu.VMEM((cols + 16, CHANS), F32),
        pltpu.VMEM((2, cols, CHANS), BF),
        pltpu.VMEM((half, OUTS), BF),
        pltpu.VMEM((4, half, 4 * CHANS), BF),
        pltpu.VMEM((3, half, 3 * CHANS), BF),
        pltpu.VMEM((4, half, 4 * CHANS), BF),
        pltpu.VMEM((3, 4 * CHANS, 2 * CHANS), BF),
        pltpu.VMEM((3, 2 * CHANS, 4 * CHANS), BF),
        pltpu.VMEM((2, half, 2 * CHANS), F32),
        pltpu.VMEM((2, half, 2 * CHANS), F32),
        pltpu.VMEM((2, half, 2 * CHANS), F32),
        pltpu.VMEM((half, OUTS), F32),
        pltpu.VMEM((rows_n, 8, CHANS), F32),
        pltpu.VMEM((rows_n, 8, CHANS), F32),
        pltpu.VMEM((2, 8, CHANS), F32),
        pltpu.VMEM((2, EARLY) + unit, F32),
        pltpu.VMEM((2, slots) + unit, F32),
        pltpu.VMEM((EARLY,) + unit, BF),
        pltpu.VMEM((EARLY,) + unit, BF),
        pltpu.VMEM((slots,) + unit, BF),
        pltpu.VMEM((slots,) + unit, BF),
        pltpu.VMEM((EARLY,) + unit, BF),
        pltpu.VMEM((slots,) + unit, BF),
        pltpu.VMEM((slots,) + unit, BF),
        pltpu.VMEM((slots,) + unit, BF),
        pltpu.VMEM(unit, F32),
        pltpu.VMEM(unit, F32),
        pltpu.VMEM((OUTS, CHANS), F32),
        pltpu.VMEM((dp_n, 8, CHANS), F32),
        dma((8,)),
        dma((2,)),
        dma((2,)),
        dma,
        dma,
        dma,
        dma,
        dma((2,)),
        dma((2,)),
        dma,
        dma,
        dma,
        dma,
        dma((3,)),
        dma((3,)),
        dma((slots,)),
        dma,
        dma((slots,)),
        dma,
        dma,
        dma,
        dma,
        dma,
        pltpu.SemaphoreType.REGULAR((5,)),
    ]

    def body(*refs):
        kernel(rows_n, dp_n, *refs)

    block, grad_image, table = pl.pallas_call(
        body,
        out_shape=(
            jax.ShapeDtypeStruct((1, 1, half, OUTS), BF),
            jax.ShapeDtypeStruct((1, local_rows, cols, chans), BF),
            jax.ShapeDtypeStruct((rows_n, 8, CHANS), F32),
        ),
        in_specs=[anywhere] * 8,
        out_specs=(vmem, vmem, vmem),
        scratch_shapes=scratch,
        compiler_params=pltpu.CompilerParams(
            collective_id=0, has_side_effects=True, vmem_limit_bytes=40 * 1024 * 1024
        ),
        name="step",
    )(*(pltpu.with_memory_space_constraint(x, pltpu.HBM) for x in (
        images,
        conv_weight,
        conv_bias.reshape(1, CHANS),
        norm_gain.reshape(1, CHANS),
        norm_shift.reshape(1, CHANS),
        down_weight,
        down_bias.reshape(1, OUTS),
        cotangent.reshape(1, half, OUTS),
    )))
    shape = jax.ShapeDtypeStruct
    outs = pl.pallas_call(
        finish,
        out_shape=(
            shape(block.shape, BF),
            shape(grad_image.shape, BF),
            shape((TAPS, 4, CHANS), F32),
            shape((1, 4), F32),
            shape((1, 4), F32),
            shape((1, 4), F32),
            shape((TAPS, 8, CHANS), F32),
            shape((1, 8), F32),
        ),
        in_specs=[vmem, vmem, vmem],
        out_specs=[anywhere] * 8,
        scratch_shapes=[
            pltpu.VMEM((TAPS, 4, CHANS), F32),
            pltpu.VMEM((TAPS, 8, CHANS), F32),
            pltpu.VMEM((1, 4), F32),
            pltpu.VMEM((1, 4), F32),
            pltpu.VMEM((1, 4), F32),
            pltpu.VMEM((1, 8), F32),
            dma((8,)),
        ],
        compiler_params=pltpu.CompilerParams(vmem_limit_bytes=4 * 1024 * 1024),
        name="finish",
    )(block, grad_image, table)
    block, grad_image, conv_t, bias, gain, shift, down_t, down_bias_grad = outs
    return (
        block,
        grad_image,
        jnp.swapaxes(conv_t, 1, 2).reshape(3, 3, CHANS, 4),
        bias.reshape(4),
        gain.reshape(4),
        shift.reshape(4),
        jnp.swapaxes(down_t, 1, 2).reshape(3, 3, CHANS, 8),
        down_bias_grad.reshape(8),
    )


def solution(mesh):
    spread = P("dp", "rows", None, None)
    in_specs = (spread, P(), P(), P(), P(), P(), P(), spread)
    out_specs = (
        spread,
        spread,
        P(None, None, None, "dp"),
        P("dp"),
        P("dp"),
        P("dp"),
        P(None, None, None, "dp"),
        P("dp"),
    )
    return jax.shard_map(shards, mesh=mesh, in_specs=in_specs, out_specs=out_specs, check_vma=False)
```
